256 devices in a mesh: seq: 64 (over x, z, core), tp: 4 (over y).
Axes of the slice: x: 4, y: 4, z: 8, core: 2. Of those that a mesh axis runs over, the one named last changes fastest.
Arguments:
- tokens: bfloat16 [8192, 1536], P('seq'), may hold values from -6 to 6
- attn_gain: float32 [1536], replicated, may hold values from 0.1 to 1.9
- w_query: bfloat16 [1536, 1536], P(None, 'tp')
- w_keyval: bfloat16 [1536, 8, 128], P(None, 'tp'), may hold values from -0.15625 to 0.15625
- w_out: bfloat16 [1536, 1536], P('tp'), may hold values from -0.15625 to 0.15625
- ffn_gain: float32 [1536], replicated, may hold values from 0.1 to 1.9
- lengths: int32 [4], replicated, may hold values from 1 to 6144, 8192 in all
- routes: int32 [8192, 8], P(('seq', 'tp')), may hold values from 0 to 31, all different within a row; in each aligned block of 32 rows (0 to 31, 32 to 63, ...) at most 16 rows name the same one
- route_gates: float32 [8192, 8], P(('seq', 'tp')), may hold values from 0.05 to 0.3
- w_gate: bfloat16 [64, 1536, 256], P('seq'), may hold values from -0.15625 to 0.15625
- w_up: bfloat16 [64, 1536, 256], P('seq'), may hold values from -0.15625 to 0.15625
- w_down: bfloat16 [64, 256, 1536], P('seq'), may hold values from -0.25 to 0.25
- page_slot_index: int32 [64], replicated, may hold values from 0 to 127, as said below
Outputs:
- layer_out: bfloat16 [8192, 1536], P(('seq', 'tp'))
- key_value_pages: bfloat16 [128, 128, 8, 128], P('seq', None, 'tp')
The draws below stay inside these ranges and needn't reach their ends.
Inputs may be any that keep to these rules, and one draw needn't show every extreme that they name: The 4 lengths sum to 8192 and the largest is exactly 6144. `routes`: each row names 8 different experts; among the 32 rows of one device (aligned blocks) no expert is named more than 16 times. `page_slot_index`: distinct slots; slot s lies on index s // 2 of seq, at place s % 2.
All inputs are finite; a program needn't handle non-finite values.
Results may differ from the reference program's by a relative error of at most 0.013.
The reference program's roundings to bfloat16 on the way count: a program that leaves them out, or rounds other values in their place, can miss the bound.
Values may be sent and summed in bfloat16 or wider, within the bound.
A program may use at most 128 MiB of HBM per device.

```python
import math
import jax
import jax.numpy as jnp
import numpy as np
from jax import lax

D = 1536
QH = 24
KEY_VALUE_HEADS = 8
HEAD_SIZE = 64
FF = 512
TOP = 8
EXPERTS = 32
PAGE_TOKENS = 128
TOKENS = 8192
TPB = 32
MOST = 16
HALF = 256
PIECES = 64
MAXLEN = 6144
NDOCS = 4
SLOT_TOTAL = 128
PAGE_TOTAL = 64


def draw_w_query(key, part):
    matrix = jax.random.normal(key, (D, QH * HEAD_SIZE), jnp.float32) * D ** (-0.5)
    return matrix.astype(jnp.bfloat16)


def draw_page_slot_index(key, part):
    hidden_middle = jax.random.permutation(key, SLOT_TOTAL - 2).astype(jnp.int32) + 1
    selected_experts = jnp.concatenate([jnp.array([0, SLOT_TOTAL - 1], jnp.int32), hidden_middle[:PAGE_TOTAL - 2]])
    return jax.random.permutation(jax.random.fold_in(key, 3), selected_experts).astype(jnp.int32)


def block_scale(rng, dims, pieces, least, high):
    level, own = 1.0, jax.random.fold_in(rng, 6)
    for dim, shards_of in pieces:
        draws = jnp.exp(jax.random.uniform(jax.random.fold_in(own, dim), (shards_of,), jnp.float32, least / len(pieces), high / len(pieces)))
        level = level * jnp.repeat(draws, dims[dim] // shards_of).reshape([-1 if axis == dim else 1 for axis in range(len(dims))])
    return level


def profile(amount, total, limit, lean):
    weights = [(1 << 20) // math.isqrt(rank ** lean) + 1 for rank in range(2, amount + 1)]
    spare, given = total - limit - (amount - 1), [1] * (amount - 1)
    while spare > 0:
        movable = [i for i in range(amount - 1) if given[i] < limit]
        whole, left = sum([weights[i] for i in movable]), spare
        for i in movable:
            more = min(limit - given[i], max(1, left * weights[i] // whole), spare)
            given[i] = given[i] + more
            spare = spare - more
    return np.array([limit] + given)


def ragged(own_key, count, total, limit, skew):
    if count == 2:
        one = jax.random.randint(own_key, (), max(1, total - limit), min(limit, total - 1) + 1)
        return jnp.stack([one, total - one])
    sizes = jnp.asarray(profile(count, total, limit, skew), jnp.int32)
    twos = (count - 1) // 2
    donor, receiver = sizes[1:1 + 2 * twos:2], sizes[2:2 + 2 * twos:2]
    margin = jnp.minimum(donor - 1, limit - receiver)
    passed = jax.random.randint(jax.random.fold_in(own_key, 1), (twos,), 0, 1 << 20) % (margin + 1)
    sizes = sizes.at[1:1 + 2 * twos:2].set(donor - passed).at[2:2 + 2 * twos:2].set(receiver + passed)
    return sizes[jax.random.permutation(jax.random.fold_in(own_key, 2), count)]


def deal_out(key, own, number, rows, number_of, top, bound, skew):
    sequence = jax.random.permutation(key, number_of)
    crowded, ordinary = load_shares(number_of, rows * top, bound, skew, True), load_shares(number_of, rows * top, bound, skew, False)
    places = jnp.arange(number_of)

    def named(tallies, rotation):
        used = int((tallies > 0).sum())
        fixed = max(1, used // 4)
        moved = fixed + (places - fixed + rotation * (used - fixed)) % max(1, number_of - fixed)
        return jnp.zeros((number_of,), jnp.int32).at[sequence[jnp.where(places < fixed, places, moved)]].set(jnp.asarray(tallies, jnp.int32))

    tallies = jnp.where(number % 4 == 0, named(crowded, number // 4), named(ordinary, number - number // 4 - 1))
    mixed = jax.random.permutation(jax.random.fold_in(own, 3), number_of)
    donor, taker = mixed[0:number_of // 2 * 2:2], mixed[1:number_of // 2 * 2:2]
    slack = jnp.minimum(tallies[donor] - 1, bound - tallies[taker]) // 2
    slack = jnp.where((donor == sequence[0]) | (taker == sequence[0]) | (tallies[taker] == 0), 0, jnp.maximum(slack, 0))
    moved = jax.random.randint(jax.random.fold_in(own, 4), (number_of // 2,), 0, 1 << 20) % (slack + 1)
    tallies = tallies.at[donor].add(-moved).at[taker].add(moved)
    members = jnp.searchsorted(jnp.cumsum(tallies), jnp.arange(rows * top), side="right").astype(jnp.int32)
    table = members.reshape(top, rows).T
    table = table[jax.random.permutation(jax.random.fold_in(own, 1), rows)]
    rotation = jax.random.randint(jax.random.fold_in(own, 2), (rows, 1), 0, top)
    return jnp.take_along_axis(table, (jnp.arange(top)[None, :] + rotation) % top, axis=1)


def load_shares(amount, total, most, skew, full):
    weights = [(1 << 20) // math.isqrt(standing ** skew) + 1 for standing in range(1, amount + 1)]
    largest = most if full else min(most, max(-(-total // amount), total * weights[0] // sum(weights)))
    least = 1 if total - largest >= amount - 1 else 0
    counts, spare = [largest] + [least] * (amount - 1), total - largest - least * (amount - 1)
    while spare > 0:
        candidates = [i for i in range(1, amount) if counts[i] < largest] or [i for i in range(1, amount) if counts[i] < most]
        mass, remaining = sum([weights[i] for i in candidates]), spare
        for i in candidates:
            more = min(most - counts[i], max(1, remaining * weights[i] // mass), spare)
            counts[i] = counts[i] + more
            spare = spare - more
    return np.array(counts)


def scatter_about(rng, extent, width, limit, shards=(), held_as=jnp.bfloat16):
    drawn = jax.random.normal(rng, extent, jnp.float32) * width
    if len(shards) > 0:
        drawn = block_scale(rng, extent, shards, -0.22, 0.18) * drawn
    return jnp.clip(drawn, min=-limit, max=limit).astype(held_as)


def setup_inputs(seed: int = 0) -> dict:
    key_list = jax.random.split(jax.random.key(seed), 14)
    tokens = scatter_about(key_list[0], (TOKENS, D), 1.0, 6.0, ((0, 64),))
    attn_gain = jnp.clip(1.0 + 0.18 * jax.random.normal(key_list[1], (D,), jnp.float32), 0.1, 1.9)
    w_query = draw_w_query(jax.random.fold_in(key_list[13], 71), 0)
    w_keyval = scatter_about(key_list[3], (D, KEY_VALUE_HEADS, 2 * HEAD_SIZE), D ** -0.5, 0.15625, ((1, 4),))
    w_out = scatter_about(key_list[4], (QH * HEAD_SIZE, D), (QH * HEAD_SIZE) ** -0.5, 0.15625, ((0, 4),))
    ffn_gain = jnp.clip(1.0 + 0.18 * jax.random.normal(key_list[5], (D,), jnp.float32), 0.1, 1.9)
    lengths = ragged(key_list[6], NDOCS, TOKENS, MAXLEN, 2).astype(jnp.int32)
    routes_keys = jax.random.split(jax.random.fold_in(key_list[7], 1), TOKENS // TPB)
    routes_turns = jax.random.permutation(jax.random.fold_in(key_list[7], 3), TOKENS // TPB)
    routes = jax.vmap(lambda own, number: deal_out(jax.random.fold_in(key_list[7], 2), own, number, TPB, EXPERTS, TOP, MOST, 2))(routes_keys, routes_turns).reshape((TOKENS, TOP))
    route_gates = jnp.clip(0.05 + 0.25 * jax.random.uniform(key_list[8], (TOKENS, TOP), jnp.float32) ** block_scale(key_list[8], (TOKENS, TOP), ((0, 256),), -0.2, 0.2), 0.05, 0.3)
    w_gate = scatter_about(key_list[9], (PIECES, D, HALF), D ** -0.5, 0.15625, ((0, 64),))
    w_up = scatter_about(key_list[10], (PIECES, D, HALF), D ** -0.5, 0.15625, ((0, 64),))
    w_down = scatter_about(key_list[11], (PIECES, HALF, D), FF ** -0.5, 0.25, ((0, 64),))
    page_slot_index = draw_page_slot_index(jax.random.fold_in(key_list[13], 71), 0)
    return {"tokens": tokens, "attn_gain": attn_gain, "w_query": w_query, "w_keyval": w_keyval, "w_out": w_out, "ffn_gain": ffn_gain, "lengths": lengths, "routes": routes, "route_gates": route_gates, "w_gate": w_gate, "w_up": w_up, "w_down": w_down, "page_slot_index": page_slot_index}


epsilon = 1e-05
rope_base = 10000.0

def rms_scale(inputs, gain_vec):
    inputs = inputs.astype(jnp.float32)
    mean_sq = lax.optimization_barrier(jnp.mean(inputs * inputs, axis=-1, keepdims=True))
    return inputs * lax.rsqrt(mean_sq + epsilon) * gain_vec

def doc_info(lengths, first_row, count_rows):
    doc_ends = jnp.cumsum(lengths).astype(jnp.int32)
    starts = doc_ends - lengths
    tok_index = first_row + jnp.arange(count_rows, dtype=jnp.int32)
    inside = (tok_index[:, None] >= starts[None, :]) & (tok_index[:, None] < doc_ends[None, :])
    doc_ids = jnp.arange(lengths.shape[0], dtype=jnp.int32)
    segment = lax.optimization_barrier(jnp.sum(jnp.where(inside, doc_ids[None, :], 0), axis=1)).astype(jnp.int32)
    doc_begin = lax.optimization_barrier(jnp.sum(jnp.where(inside, starts[None, :], 0), axis=1)).astype(jnp.int32)
    return (tok_index, segment, tok_index - doc_begin)

def rotate(inputs, position):
    half_dim = inputs.shape[-1] // 2
    inv_freq = rope_base ** (-jnp.arange(half_dim, dtype=jnp.float32) / half_dim)
    angle = position.astype(jnp.float32)[:, None] * inv_freq[None, :]
    cosine = jnp.cos(angle)[:, None, :]
    sine_val = jnp.sin(angle)[:, None, :]
    first_part = inputs[..., :half_dim]
    second_part = inputs[..., half_dim:]
    return jnp.concatenate([first_part * cosine - second_part * sine_val, second_part * cosine + first_part * sine_val], axis=-1)

def reference(tokens, attn_gain, w_query, w_keyval, w_out, ffn_gain, lengths, routes, route_gates, w_gate, w_up, w_down, page_slot_index):
    group_size = QH // KEY_VALUE_HEADS
    normed = rms_scale(tokens, attn_gain).astype(jnp.bfloat16)
    tok_index, segment, position = doc_info(lengths, 0, TOKENS)
    queries = jnp.dot(normed, w_query, preferred_element_type=jnp.float32).reshape(TOKENS, QH, HEAD_SIZE)
    queries = rotate(queries, position).astype(jnp.bfloat16)
    key_value_rows = jnp.dot(normed, w_keyval.reshape(D, KEY_VALUE_HEADS * 2 * HEAD_SIZE), preferred_element_type=jnp.float32).reshape(TOKENS, KEY_VALUE_HEADS, 2 * HEAD_SIZE)
    key_rot = rotate(key_value_rows[..., :HEAD_SIZE], position)
    key_value_rows = jnp.concatenate([key_rot, key_value_rows[..., HEAD_SIZE:]], axis=-1).astype(jnp.bfloat16)
    key_value_pages = jnp.zeros((SLOT_TOTAL, PAGE_TOKENS, KEY_VALUE_HEADS, 2 * HEAD_SIZE), jnp.bfloat16).at[page_slot_index].set(key_value_rows.reshape(PAGE_TOTAL, PAGE_TOKENS, KEY_VALUE_HEADS, 2 * HEAD_SIZE))
    block_len = min(256, TOKENS)
    window = min(TOKENS, MAXLEN - 1 + block_len)
    scale = HEAD_SIZE ** (-0.5)

    def attend(block_id):
        query_start = block_id * block_len
        key_start = jnp.clip(query_start + block_len - window, 0, TOKENS - window).astype(jnp.int32)
        query_block = lax.dynamic_slice_in_dim(queries, query_start, block_len, 0).astype(jnp.float32)
        query_block = query_block.reshape(block_len, KEY_VALUE_HEADS, group_size, HEAD_SIZE)
        key_block = lax.dynamic_slice_in_dim(key_value_rows, key_start, window, 0).astype(jnp.float32)
        query_seg = lax.dynamic_slice_in_dim(segment, query_start, block_len, 0)
        key_seg = lax.dynamic_slice_in_dim(segment, key_start, window, 0)
        query_pos = query_start + jnp.arange(block_len, dtype=jnp.int32)
        key_pos = key_start + jnp.arange(window, dtype=jnp.int32)
        scores = jnp.einsum('qhgd,khd->hgqk', query_block, key_block[..., :HEAD_SIZE]) * scale
        allowed = (query_seg[:, None] == key_seg[None, :]) & (key_pos[None, :] <= query_pos[:, None])
        scores = jnp.where(allowed[None, None], scores, -jnp.inf)
        row_best = lax.optimization_barrier(jnp.max(scores, axis=-1, keepdims=True))
        expd = jnp.exp(scores - row_best)
        weight_sum = lax.optimization_barrier(jnp.sum(expd, axis=-1))
        rounded = lax.optimization_barrier(expd.astype(jnp.bfloat16)).astype(jnp.float32)
        weighted = jnp.einsum('hgqk,khd->hgqd', rounded, key_block[..., HEAD_SIZE:]) / weight_sum[..., None]
        return jnp.transpose(weighted, (2, 0, 1, 3)).reshape(block_len, QH * HEAD_SIZE).astype(jnp.bfloat16)
    block_ids = jnp.arange(TOKENS // block_len, dtype=jnp.int32)
    attended = lax.map(attend, block_ids).reshape(TOKENS, QH * HEAD_SIZE)
    resid = tokens.astype(jnp.float32) + jnp.dot(attended, w_out, preferred_element_type=jnp.float32)
    ffn_in = rms_scale(resid, ffn_gain).astype(jnp.bfloat16)
    flat_routes = routes.reshape(-1)
    flat_gates = route_gates.reshape(-1)
    capacity = TOKENS // TPB * MOST

    def expert_pass(moe_sum, expert_id):
        picked_order = jnp.argsort((flat_routes != expert_id).astype(jnp.int32), stable=True)[:capacity]
        is_valid = flat_routes[picked_order] == expert_id
        tok_rows = picked_order // TOP
        gathered = ffn_in[tok_rows]
        result = jnp.zeros((capacity, D), jnp.float32)
        for which_half in range(2):
            piece_id = 2 * expert_id + which_half
            gate_part = jnp.dot(gathered, w_gate[piece_id], preferred_element_type=jnp.float32)
            up_part = jnp.dot(gathered, w_up[piece_id], preferred_element_type=jnp.float32)
            hidden = (jax.nn.silu(gate_part) * up_part).astype(jnp.bfloat16)
            piece_out = jnp.dot(hidden, w_down[piece_id], preferred_element_type=jnp.float32).astype(jnp.bfloat16)
            result = result + lax.optimization_barrier(piece_out).astype(jnp.float32)
        factor = jnp.where(is_valid, flat_gates[picked_order], 0.0).astype(jnp.float32)
        return (moe_sum.at[tok_rows].add(result * factor[:, None]), None)
    moe_sum, unused = lax.scan(expert_pass, jnp.zeros((TOKENS, D), jnp.float32), jnp.arange(EXPERTS, dtype=jnp.int32))
    layer_out = (resid + moe_sum).astype(jnp.bfloat16)
    return (layer_out, key_value_pages)
```

```python
import jax
import jax.numpy as jnp
from jax import lax
from jax.experimental import pallas as pl
from jax.experimental.pallas import tpu as pltpu
from jax.sharding import PartitionSpec as P

PAGE_TOKENS = 128


epsilon = 1e-05
rope_base = 10000.0


def rms_scale(inputs, gain_vec):
    inputs = inputs.astype(jnp.float32)
    mean_sq = jnp.mean(inputs * inputs, axis=-1, keepdims=True)
    return inputs * lax.rsqrt(mean_sq + epsilon) * gain_vec


def doc_info(lengths, first_row, count_rows):
    doc_ends = jnp.cumsum(lengths)
    starts = doc_ends - lengths
    tok_index = first_row + jnp.arange(count_rows, dtype=jnp.int32)
    inside = (tok_index[:, None] >= starts[None, :]) & (tok_index[:, None] < doc_ends[None, :])
    doc_ids = jnp.arange(lengths.shape[0], dtype=jnp.int32)
    segment = jnp.sum(jnp.where(inside, doc_ids[None, :], 0), axis=1)
    doc_begin = jnp.sum(jnp.where(inside, starts[None, :], 0), axis=1)
    return (tok_index, segment, tok_index - doc_begin)


def rotate(inputs, position):
    half_dim = inputs.shape[-1] // 2
    inv_freq = rope_base ** (-jnp.arange(half_dim, dtype=jnp.float32) / half_dim)
    angle = position.astype(jnp.float32)[:, None] * inv_freq[None, :]
    cosine = jnp.cos(angle)[:, None, :]
    sine_val = jnp.sin(angle)[:, None, :]
    first_part = inputs[..., :half_dim]
    second_part = inputs[..., half_dim:]
    return jnp.concatenate(
        [
            first_part * cosine - second_part * sine_val,
            second_part * cosine + first_part * sine_val,
        ],
        axis=-1,
    )


MESH = pl.DeviceIdType.MESH
CHIPS_X = 4
CHIPS_Z = 8


def signed_z(dz):
    return dz - CHIPS_Z if dz > CHIPS_Z // 2 else dz


def route_in(stream, dx, dz):
    dz_signed = signed_z(dz)
    if stream == 0:
        if dz == 0:
            return None if dx == 0 else ("x", dx)
        if abs(dz_signed) == 4:
            return ("z", -1) if dx < 2 else ("z", 1)
        return ("z", 1) if dz_signed > 0 else ("z", -1)
    if dx == 0:
        if dz == 0:
            return None
        return ("z", 1) if 0 < dz_signed < 4 else ("z", -1)
    if dx == 2:
        return ("x", -1) if dz % 2 == 0 else ("x", 1)
    return ("x", 1) if dx == 1 else ("x", -1)


def round_in(stream, dx, dz):
    far = abs(signed_z(dz))
    if stream == 0:
        return far + (1 if dx else 0)
    return far + min(dx, CHIPS_X - dx)


PIECES = [(s, dx, dz) for s in range(2) for dx in range(CHIPS_X) for dz in range(CHIPS_Z)]
PARENT = {p: route_in(*p) for p in PIECES}
CHILDREN = {p: [] for p in PIECES}
for piece, came in PARENT.items():
    if came is not None:
        axis, step = came
        moved_x = (piece[1] - step) % CHIPS_X if axis == "x" else piece[1]
        moved_z = (piece[2] - step) % CHIPS_Z if axis == "z" else piece[2]
        CHILDREN[(piece[0], moved_x, moved_z)].append((piece, (axis, -step)))
ROUNDS = max(round_in(*p) for p in PIECES)
ORDER = [[p for p in PIECES if round_in(*p) == r] for r in range(ROUNDS + 1)]


def flat_piece(piece):
    return (piece[0] * CHIPS_X + piece[1]) * CHIPS_Z + piece[2]


class Place:
    def __init__(self):
        self.seq = lax.axis_index("seq")
        self.tp = lax.axis_index("tp")
        self.x = self.seq // (2 * CHIPS_Z)
        self.z = (self.seq // 2) % CHIPS_Z
        self.core = self.seq % 2

    def xs(self, dx):
        return lax.rem(self.x + dx + CHIPS_X, CHIPS_X)

    def zs(self, dz):
        return lax.rem(self.z + dz + CHIPS_Z, CHIPS_Z)

    def chip(self, axis, step):
        if axis == "x":
            return ((self.xs(step) * CHIPS_Z + self.z) * 2 + self.core, self.tp)
        return ((self.x * CHIPS_Z + self.zs(step)) * 2 + self.core, self.tp)

    def twin(self):
        return (self.x * CHIPS_Z * 2 + self.z * 2 + 1 - self.core, self.tp)

    def row(self, step):
        return (self.seq, lax.rem(self.tp + step + 4, 4))


def remote(src, dst, send_sem, recv_sem, device):
    return pltpu.make_async_remote_copy(
        src_ref=src,
        dst_ref=dst,
        send_sem=send_sem,
        recv_sem=recv_sem,
        device_id=device,
        device_id_type=MESH,
    )


def greet(partners):
    barrier = pltpu.get_barrier_semaphore()
    for partner in partners:
        pl.semaphore_signal(barrier, inc=1, device_id=partner, device_id_type=MESH)
    pl.semaphore_wait(barrier, len(partners))


PLANE = (("x", 1), ("x", -1), ("x", 2), ("z", 1), ("z", -1))


def moe_kernel(
    attended,
    w_out,
    tokens,
    gain,
    gates,
    w_gate,
    w_up,
    w_down,
    out,
    gate_w,
    up_w,
    down_w,
    projected,
    proj_send,
    proj_recv,
    rows,
    parts,
    sums,
    resid,
    w_local,
    w_send,
    w_recv,
    y_send,
    y_recv,
    ag_send,
    ag_recv,
    rs_send,
    rs_recv,
):
    at = Place()
    share = tokens.shape[0]
    half = share // 2
    greet([at.chip(*d) for d in PLANE] + [at.twin()] + [at.row(d) for d in (1, 2, 3)])
    weights = ((w_gate, gate_w), (w_up, up_w), (w_down, down_w))
    local_copies, twin_copies = [], []
    for i, (source, held) in enumerate(weights):
        local_copies.append(pltpu.make_async_copy(source.at[0], held.at[at.core], w_local.at[i]))
        twin_copies.append(
            remote(source.at[0], held.at[at.core], w_send.at[i], w_recv.at[i], at.twin())
        )
    projected[...] = jnp.dot(attended[...], w_out[...], preferred_element_type=jnp.float32)
    proj_send[...] = projected[...].astype(jnp.bfloat16)
    y_copies = []
    for step in (2, 1, 3):
        theirs = at.row(step)[1]
        y_copies.append(
            remote(
                proj_send.at[pl.ds(pl.multiple_of(theirs * share, share), share)],
                proj_recv.at[step - 1],
                y_send.at[step - 1],
                y_recv.at[step - 1],
                at.row(step),
            )
        )
        y_copies[-1].start()
    for copy in local_copies + twin_copies:
        copy.start()
    own = projected[pl.ds(pl.multiple_of(at.tp * share, share), share), :]
    own = own + tokens[...].astype(jnp.float32)
    for copy in y_copies:
        copy.wait_recv()
    for step in range(3):
        own = own + proj_recv[step].astype(jnp.float32)
    resid[...] = own
    mean_sq = jnp.mean(own * own, axis=-1, keepdims=True)
    normed = (own * lax.rsqrt(mean_sq + epsilon) * gain[...]).astype(jnp.bfloat16)

    def spot(ref, piece):
        stream, dx, dz = piece
        first = pl.multiple_of((stream * CHIPS_X + at.xs(dx)) * half, half)
        return ref.at[at.zs(dz), pl.ds(first, half)]

    for stream in range(2):
        spot(rows, (stream, 0, 0))[...] = normed[stream * half : (stream + 1) * half]

    sent = []

    def forward(piece):
        for child, (axis, step) in CHILDREN[piece]:
            copy = remote(
                spot(rows, piece),
                spot(rows, piece),
                ag_send.at[flat_piece(child)],
                ag_recv.at[flat_piece(child)],
                at.chip(axis, step),
            )
            copy.start()
            sent.append(copy)

    def arrive(piece):
        remote(
            spot(rows, piece),
            spot(rows, piece),
            ag_send.at[flat_piece(piece)],
            ag_recv.at[flat_piece(piece)],
            at.chip(*PARENT[piece]),
        ).wait_recv()

    def experts(places):
        block = jnp.concatenate([rows[p] for p in places], axis=0)
        gate_col = jnp.concatenate([gates[p] for p in places], axis=0)
        total = None
        for part in range(2):
            gate_part = jnp.dot(block, gate_w[part], preferred_element_type=jnp.float32)
            up_part = jnp.dot(block, up_w[part], preferred_element_type=jnp.float32)
            hidden = gate_part / (1.0 + jnp.exp(-gate_part)) * up_part * gate_col
            term = jnp.dot(
                hidden.astype(jnp.bfloat16), down_w[part], preferred_element_type=jnp.float32
            )
            total = term if total is None else total + term
        total = total.astype(jnp.bfloat16)
        for i, p in enumerate(places):
            parts[p] = total[i * 4 * share : (i + 1) * 4 * share]

    for piece in ORDER[0]:
        forward(piece)
    for r in range(1, ROUNDS + 1):
        for piece in ORDER[r]:
            arrive(piece)
            forward(piece)
        if r == 1:
            for copy in local_copies:
                copy.wait()
            for copy in twin_copies:
                copy.wait_recv()
        done = r - 2
        if done == 0:
            experts([at.zs(0)])
        elif 0 < done < 4:
            experts([at.zs(done), at.zs(-done)])
        elif done == 4:
            experts([at.zs(4)])

    def slot(piece):
        return sums.at[flat_piece(piece)]

    def child_wait(child):
        remote(
            slot(child), slot(child), rs_send.at[flat_piece(child)], rs_recv.at[flat_piece(child)], at.twin()
        ).wait_recv()

    totals = []
    for r in range(ROUNDS, -1, -1):
        for piece in ORDER[r]:
            total = None
            for child, _ in CHILDREN[piece]:
                child_wait(child)
                if total is None:
                    total = spot(parts, piece)[...].astype(jnp.float32)
                total = total + slot(child)[...].astype(jnp.float32)
            if PARENT[piece] is None:
                totals.append(total)
                continue
            if total is not None:
                spot(parts, piece)[...] = total.astype(jnp.bfloat16)
            copy = remote(
                spot(parts, piece),
                slot(piece),
                rs_send.at[flat_piece(piece)],
                rs_recv.at[flat_piece(piece)],
                at.chip(*PARENT[piece]),
            )
            copy.start()
            sent.append(copy)
    for stream in range(2):
        lines = slice(stream * half, (stream + 1) * half)
        out[lines, :] = (resid[lines, :] + totals[stream]).astype(jnp.bfloat16)
    for copy in y_copies + twin_copies + sent:
        copy.wait_send()


def moe_call(attended, w_out, tokens, gain, gates, w_gate, w_up, w_down):
    share, width = tokens.shape
    piece = w_gate.shape[2]
    half = share // 2
    vmem = pl.BlockSpec(memory_space=pltpu.VMEM)
    hbm = pl.BlockSpec(memory_space=pl.ANY)
    bundle = (CHIPS_Z, 2 * CHIPS_X * half, width)
    count = len(PIECES)
    dma = pltpu.SemaphoreType.DMA
    return pl.pallas_call(
        moe_kernel,
        out_shape=jax.ShapeDtypeStruct((share, width), jnp.bfloat16),
        in_specs=[vmem] * 5 + [hbm] * 3,
        out_specs=vmem,
        scratch_shapes=[
            pltpu.VMEM((2, width, piece), jnp.bfloat16),
            pltpu.VMEM((2, width, piece), jnp.bfloat16),
            pltpu.VMEM((2, piece, width), jnp.bfloat16),
            pltpu.VMEM((4 * share, width), jnp.float32),
            pltpu.VMEM((4 * share, width), jnp.bfloat16),
            pltpu.VMEM((3, share, width), jnp.bfloat16),
            pltpu.VMEM(bundle, jnp.bfloat16),
            pltpu.VMEM(bundle, jnp.bfloat16),
            pltpu.VMEM((count, half, width), jnp.bfloat16),
            pltpu.VMEM((share, width), jnp.float32),
            dma((3,)),
            dma((3,)),
            dma((3,)),
            dma((3,)),
            dma((3,)),
            dma((count,)),
            dma((count,)),
            dma((count,)),
            dma((count,)),
        ],
        compiler_params=pltpu.CompilerParams(
            collective_id=1, has_side_effects=True, vmem_limit_bytes=48 << 20
        ),
        cost_estimate=pl.CostEstimate(flops=5 << 30, bytes_accessed=16 << 20, transcendentals=1 << 20),
        name="moe",
    )(attended, w_out, tokens, gain, gates, w_gate, w_up, w_down)


def gate_columns(routes, route_gates, seq_index, experts):
    chosen = routes[:, :, None] == jnp.arange(experts, dtype=jnp.int32)[None, None, :]
    table = jnp.sum(jnp.where(chosen, route_gates[:, :, None], 0.0), axis=1)
    table = lax.all_gather(table, "seq", axis=0)
    table = table.reshape(CHIPS_X, CHIPS_Z, 2, 2, -1, experts)
    mine = lax.dynamic_index_in_dim(table, seq_index % 2, 2, keepdims=False)
    column = lax.dynamic_index_in_dim(mine, seq_index // 2, 4, keepdims=False)
    return jnp.transpose(column, (1, 2, 0, 3)).reshape(CHIPS_Z, -1, 1)


def body(
    tokens,
    attn_gain,
    w_query,
    w_keyval,
    w_out,
    ffn_gain,
    lengths,
    routes,
    route_gates,
    w_gate,
    w_up,
    w_down,
    page_slot_index,
):
    row_count = tokens.shape[0]
    seq_count = lax.axis_size("seq")
    seq_index = lax.axis_index("seq")
    kv_heads = w_keyval.shape[1]
    head_dim = w_keyval.shape[2] // 2
    q_heads = w_query.shape[1] // head_dim
    group_size = q_heads // kv_heads
    width = tokens.shape[1]
    scale = head_dim ** (-0.5)
    gate_cols = gate_columns(routes, route_gates, seq_index, w_gate.shape[0] * seq_count // 2)
    tok_index, segment, position = doc_info(lengths, seq_index * row_count, row_count)
    normed = rms_scale(tokens, attn_gain).astype(jnp.bfloat16)
    queries = jnp.dot(normed, w_query, preferred_element_type=jnp.float32).reshape(
        row_count, q_heads, head_dim
    )
    queries = (
        rotate(queries, position)
        .astype(jnp.bfloat16)
        .reshape(row_count, kv_heads, group_size, head_dim)
    )
    key_value_rows = jnp.einsum("td,dhe->the", normed, w_keyval, preferred_element_type=jnp.float32)
    key_rot = rotate(key_value_rows[..., :head_dim], position)
    key_value_rows = jnp.concatenate([key_rot, key_value_rows[..., head_dim:]], axis=-1).astype(
        jnp.bfloat16
    )
    pages_dev = row_count // PAGE_TOKENS
    slots_dev = 2 * pages_dev
    page_width = PAGE_TOKENS * kv_heads * 2 * head_dim
    local_slot = page_slot_index - seq_index * slots_dev
    slot_range = jnp.arange(slots_dev, dtype=jnp.int32)
    kv_piece = lax.all_gather(key_value_rows, "seq", axis=0, tiled=True)
    row_best = jnp.full((kv_heads, group_size, row_count), -1e30, jnp.float32)
    piece_len = kv_piece.shape[0]
    key_index, key_segment, unused = doc_info(lengths, jnp.int32(0), piece_len)
    scores = (
        jnp.einsum(
            "qhgd,khd->hgqk", queries, kv_piece[..., :head_dim], preferred_element_type=jnp.float32
        )
        * scale
    )
    allowed = (segment[:, None] == key_segment[None, :]) & (
        key_index[None, :] <= tok_index[:, None]
    )
    scores = jnp.where(allowed[None, None], scores, -jnp.inf)
    new_best = jnp.maximum(row_best, jnp.max(scores, axis=-1))
    expd = jnp.exp(scores - new_best[..., None])
    weight_sum = jnp.sum(expd, axis=-1)
    weighted = jnp.einsum(
        "hgqk,khd->hgqd",
        expd.astype(jnp.bfloat16),
        kv_piece[..., head_dim:],
        preferred_element_type=jnp.float32,
    )
    by_slot = slot_range[:, None] == local_slot[None, :]
    page_of = jnp.sum(jnp.where(by_slot, jnp.arange(local_slot.shape[0])[None, :], 0), axis=1)
    filled = jnp.any(by_slot, axis=1)
    all_pages = kv_piece.reshape(-1, PAGE_TOKENS, kv_heads, 2 * head_dim)
    key_value_pages = jnp.stack(
        [
            jnp.where(
                filled[i], lax.dynamic_index_in_dim(all_pages, page_of[i], 0, keepdims=False), 0
            ).astype(jnp.bfloat16)
            for i in range(slots_dev)
        ]
    )
    weighted = weighted / weight_sum[..., None]
    attended = (
        jnp.transpose(weighted, (2, 0, 1, 3))
        .reshape(row_count, q_heads * head_dim)
        .astype(jnp.bfloat16)
    )
    tp_index = lax.axis_index("tp")
    tok_share = routes.shape[0]
    own_tokens = lax.dynamic_slice_in_dim(tokens, tp_index * tok_share, tok_share, 0)
    layer_out = moe_call(
        attended, w_out, own_tokens, ffn_gain[None, :], gate_cols, w_gate, w_up, w_down
    )
    return (layer_out, key_value_pages)


def solution(mesh):
    placed = (
        P("seq", None),
        P(),
        P(None, "tp"),
        P(None, "tp", None),
        P("tp", None),
        P(),
        P(),
        P(("seq", "tp"), None),
        P(("seq", "tp"), None),
        P("seq", None, None),
        P("seq", None, None),
        P("seq", None, None),
        P(),
    )
    return jax.shard_map(
        body,
        mesh=mesh,
        in_specs=placed,
        out_specs=(P(("seq", "tp"), None), P("seq", None, "tp", None)),
        check_vma=False,
    )
```

```python
import jax
import jax.numpy as jnp
from jax import lax
from jax.experimental import pallas as pl
from jax.experimental.pallas import tpu as pltpu
from jax.sharding import PartitionSpec as P

PAGE_TOKENS = 128


epsilon = 1e-05
rope_base = 10000.0

MESH = pl.DeviceIdType.MESH
CHIPS_X = 4
CHIPS_Z = 8


def signed_z(dz):
    return dz - CHIPS_Z if dz > CHIPS_Z // 2 else dz


def route_in(stream, dx, dz):
    dz_signed = signed_z(dz)
    if stream == 0:
        if dz == 0:
            return None if dx == 0 else ("x", dx)
        if abs(dz_signed) == 4:
            return ("z", -1) if dx < 2 else ("z", 1)
        return ("z", 1) if dz_signed > 0 else ("z", -1)
    if dx == 0:
        if dz == 0:
            return None
        return ("z", 1) if 0 < dz_signed < 4 else ("z", -1)
    if dx == 2:
        return ("x", -1) if dz % 2 == 0 else ("x", 1)
    return ("x", 1) if dx == 1 else ("x", -1)


def round_in(stream, dx, dz):
    far = abs(signed_z(dz))
    if stream == 0:
        return far + (1 if dx else 0)
    return far + min(dx, CHIPS_X - dx)


PIECES = [(s, dx, dz) for s in range(2) for dx in range(CHIPS_X) for dz in range(CHIPS_Z)]
PARENT = {p: route_in(*p) for p in PIECES}
CHILDREN = {p: [] for p in PIECES}
for piece, came in PARENT.items():
    if came is not None:
        axis, step = came
        moved_x = (piece[1] - step) % CHIPS_X if axis == "x" else piece[1]
        moved_z = (piece[2] - step) % CHIPS_Z if axis == "z" else piece[2]
        CHILDREN[(piece[0], moved_x, moved_z)].append((piece, (axis, -step)))
ROUNDS = max(round_in(*p) for p in PIECES)
ORDER = [[p for p in PIECES if round_in(*p) == r] for r in range(ROUNDS + 1)]


def flat_piece(piece):
    return (piece[0] * CHIPS_X + piece[1]) * CHIPS_Z + piece[2]


class Place:
    def __init__(self):
        self.seq = lax.axis_index("seq")
        self.tp = lax.axis_index("tp")
        self.x = self.seq // (2 * CHIPS_Z)
        self.z = (self.seq // 2) % CHIPS_Z
        self.core = self.seq % 2

    def xs(self, dx):
        return lax.rem(self.x + dx + CHIPS_X, CHIPS_X)

    def zs(self, dz):
        return lax.rem(self.z + dz + CHIPS_Z, CHIPS_Z)

    def chip(self, axis, step):
        if axis == "x":
            return ((self.xs(step) * CHIPS_Z + self.z) * 2 + self.core, self.tp)
        return ((self.x * CHIPS_Z + self.zs(step)) * 2 + self.core, self.tp)

    def twin(self):
        return (self.x * CHIPS_Z * 2 + self.z * 2 + 1 - self.core, self.tp)

    def row(self, step):
        return (self.seq, lax.rem(self.tp + step + 4, 4))


def remote(src, dst, send_sem, recv_sem, device):
    return pltpu.make_async_remote_copy(
        src_ref=src,
        dst_ref=dst,
        send_sem=send_sem,
        recv_sem=recv_sem,
        device_id=device,
        device_id_type=MESH,
    )


def greet(partners):
    barrier = pltpu.get_barrier_semaphore()
    for partner in partners:
        pl.semaphore_signal(barrier, inc=1, device_id=partner, device_id_type=MESH)
    pl.semaphore_wait(barrier, len(partners))


PLANE = (("x", 1), ("x", -1), ("x", 2), ("z", 1), ("z", -1))


def layer_kernel(
    lengths,
    page_slots,
    tokens,
    attn_gain,
    cosine,
    sine,
    ffn_gain,
    routes,
    route_gates,
    w_query,
    w_keyval,
    w_out,
    w_gate,
    w_up,
    w_down,
    out,
    pages,
    query_w,
    keyval_w,
    out_w,
    gate_w,
    up_w,
    down_w,
    queries,
    keyval,
    best,
    weight_sum,
    weighted,
    projected,
    proj_send,
    proj_recv,
    rows,
    parts,
    sums,
    resid,
    w_local,
    w_send,
    w_recv,
    kv_send,
    kv_recv,
    tw_send,
    tw_recv,
    y_send,
    y_recv,
    ag_send,
    ag_recv,
    rs_send,
    rs_recv,
):
    at = Place()
    width = tokens.shape[1]
    block = tokens.shape[0]
    share = block // 4
    half = share // 2
    lines = block // 2
    early = [
        pltpu.make_async_copy(w_query, query_w, w_local.at[3]),
        pltpu.make_async_copy(w_keyval, keyval_w, w_local.at[4]),
    ]
    out_copy = pltpu.make_async_copy(w_out, out_w, w_local.at[5])
    for copy in early:
        copy.start()
    out_copy.start()
    greet([at.chip(*d) for d in PLANE] + [at.twin()] + [at.row(d) for d in (1, 2, 3)])

    inputs = tokens[...].astype(jnp.float32)
    mean_sq = jnp.mean(inputs * inputs, axis=-1, keepdims=True)
    normed = (inputs * lax.rsqrt(mean_sq + epsilon) * attn_gain[...]).astype(jnp.bfloat16)
    lane = lax.broadcasted_iota(jnp.int32, (block, 128), 1)
    low = lane % 64 < 32
    cos_all, sin_all = cosine[...], sine[...]

    def turn(values, cos_part, sin_part):
        swapped = jnp.where(low, pltpu.roll(values, 96, 1), pltpu.roll(values, 32, 1))
        return values * cos_part + swapped * sin_part

    early[1].wait()
    key_value_rows = jnp.dot(normed, keyval_w[...], preferred_element_type=jnp.float32)
    kv_heads = key_value_rows.shape[1] // 128
    cos_kv, sin_kv = jnp.where(lane < 64, cos_all, 1.0), jnp.where(lane < 64, sin_all, 0.0)
    for head in range(kv_heads):
        spread = slice(head * 128, (head + 1) * 128)
        turned = turn(key_value_rows[:, spread], cos_kv, sin_kv).astype(jnp.bfloat16)
        for stream in range(2):
            keyval[at.z, at.core, stream, at.x, :, spread] = turned[
                stream * lines : (stream + 1) * lines
            ]

    sent = []

    def forwarder(spot, send_sem, recv_sem):
        def forward(piece):
            for child, (axis, step) in CHILDREN[piece]:
                copy = remote(
                    spot(piece),
                    spot(piece),
                    send_sem.at[flat_piece(child)],
                    recv_sem.at[flat_piece(child)],
                    at.chip(axis, step),
                )
                copy.start()
                sent.append(copy)

        def arrive(piece):
            remote(
                spot(piece),
                spot(piece),
                send_sem.at[flat_piece(piece)],
                recv_sem.at[flat_piece(piece)],
                at.chip(*PARENT[piece]),
            ).wait_recv()

        return forward, arrive

    def kv_spot(piece):
        stream, dx, dz = piece
        return keyval.at[at.zs(dz), at.core, stream, at.xs(dx)]

    forward, arrive = forwarder(kv_spot, kv_send, kv_recv)
    for piece in ORDER[0]:
        forward(piece)
    weights = ((w_gate, gate_w), (w_up, up_w), (w_down, down_w))
    local_copies, twin_copies = [], []
    for i, (source, held) in enumerate(weights):
        local_copies.append(pltpu.make_async_copy(source.at[0], held.at[at.core], w_local.at[i]))
        twin_copies.append(
            remote(source.at[0], held.at[at.core], w_send.at[i], w_recv.at[i], at.twin())
        )
    early[0].wait()
    scale = 64**-0.5 * 1.4426950408889634
    group = query_w.shape[1] // 64 // kv_heads
    query_rows = jnp.dot(normed, query_w[...], preferred_element_type=jnp.float32)
    for pair in range(query_rows.shape[1] // 128):
        turned = turn(query_rows[:, pair * 128 : (pair + 1) * 128], cos_all, sin_all) * scale
        for odd in range(2):
            head = 2 * pair + odd
            placed = pltpu.roll(turned, 64, 1) if odd else turned
            placed = jnp.where(lane < 64, placed, 0.0).astype(jnp.bfloat16)
            queries[head // group, (head % group) * block : (head % group + 1) * block, :] = placed

    best[...] = jnp.full_like(best, -1e30)
    weight_sum[...] = jnp.zeros_like(weight_sum)
    weighted[...] = jnp.zeros_like(weighted)
    token = at.seq * block + lax.broadcasted_iota(jnp.int32, (1, block), 1)
    begin = jnp.zeros((1, block), jnp.int32)
    edge = lengths[0]
    for d in range(1, lengths.shape[0]):
        begin = jnp.where(token >= edge, edge, begin)
        edge = edge + lengths[d]
    count_keys = CHIPS_X * lines
    key_row = lax.broadcasted_iota(jnp.int32, (count_keys, 1), 0)
    key_base = (key_row // lines) * (CHIPS_Z * 2 * block) + key_row % lines

    def attend(zi, ci):
        for stream in range(2):
            bundle = keyval[zi, ci, stream].reshape(count_keys, 128 * kv_heads)
            turned = bundle.T
            key = key_base + ((zi * 2 + ci) * block + stream * lines)
            bias = jnp.where((key <= token) & (key >= begin), 0.0, -1e30)
            bias = jnp.concatenate([bias] * group, axis=1)
            for head in range(kv_heads):
                scores = lax.dot_general(
                    bundle[:, head * 128 : (head + 1) * 128],
                    queries[head],
                    (((1,), (1,)), ((), ())),
                    preferred_element_type=jnp.float32,
                )
                scores = scores + bias
                old = best[head]
                new = jnp.maximum(old, jnp.max(scores, axis=0, keepdims=True))
                expd = jnp.exp2(scores - new)
                fade = jnp.exp2(old - new)
                best[head] = new
                weight_sum[head] = weight_sum[head] * fade + jnp.sum(expd, axis=0, keepdims=True)
                fresh = jnp.dot(
                    turned[head * 128 + 64 : (head + 1) * 128],
                    expd.astype(jnp.bfloat16),
                    preferred_element_type=jnp.float32,
                )
                weighted[head] = weighted[head] * fade + fresh

    shared = []

    def share_bundle(dz):
        place = keyval.at[at.zs(dz), at.core]
        copy = remote(place, place, tw_send.at[dz], tw_recv.at[dz], at.twin())
        copy.start()
        shared.append(copy)

    def twin_bundle(dz):
        place = keyval.at[at.zs(dz), 1 - at.core]
        remote(place, place, tw_send.at[dz], tw_recv.at[dz], at.twin()).wait_recv()

    for r in range(1, ROUNDS + 1):
        for piece in ORDER[r]:
            arrive(piece)
            forward(piece)
        done = r - 2
        if done < 0:
            for copy in local_copies + twin_copies:
                copy.start()
            continue
        steps = [done] if done in (0, 4) else [done, CHIPS_Z - done]
        for dz in steps:
            share_bundle(dz)
        for core in (at.core, 1 - at.core):
            if core is not at.core:
                for dz in steps:
                    twin_bundle(dz)
            for dz in steps:
                attend(at.zs(dz), core)

    for slot in range(pages.shape[0]):
        wanted = at.seq * pages.shape[0] + slot

        def look(n, found):
            return jnp.where(page_slots[n] == wanted, n, found)

        page = lax.fori_loop(0, page_slots.shape[0], look, jnp.int32(-1))
        taken = jnp.maximum(page, 0)
        for stream in range(2):
            held = keyval[(taken // 2) % CHIPS_Z, taken % 2, stream, taken // (2 * CHIPS_Z)]
            shown = jnp.broadcast_to(page, held.shape) >= 0
            pages[slot, stream * lines : (stream + 1) * lines, :] = jnp.where(
                shown, held.astype(jnp.float32), 0.0
            ).astype(jnp.bfloat16)

    columns = []
    for head in range(kv_heads):
        mean = weighted[head] / weight_sum[head]
        for g in range(group):
            columns.append(mean[:, g * block : (g + 1) * block])
    attended = jnp.concatenate(columns, axis=0).T.astype(jnp.bfloat16)

    out_copy.wait()
    projected[...] = jnp.dot(attended, out_w[...], preferred_element_type=jnp.float32)
    proj_send[...] = projected[...].astype(jnp.bfloat16)
    y_copies = []
    for step in (2, 1, 3):
        theirs = at.row(step)[1]
        y_copies.append(
            remote(
                proj_send.at[pl.ds(pl.multiple_of(theirs * share, share), share)],
                proj_recv.at[step - 1],
                y_send.at[step - 1],
                y_recv.at[step - 1],
                at.row(step),
            )
        )
        y_copies[-1].start()
    first = pl.multiple_of(at.tp * share, share)
    own = projected[pl.ds(first, share), :] + tokens[pl.ds(first, share), :].astype(jnp.float32)
    wide = lax.broadcasted_iota(jnp.int32, (share, 128), 1)
    table = jnp.zeros((share, 128), jnp.float32)
    for k in range(routes.shape[1]):
        chosen = wide % 32 == routes[:, k : k + 1]
        table = table + jnp.where(chosen, route_gates[:, k : k + 1], 0.0)
    rounded = table.astype(jnp.bfloat16).astype(jnp.float32)
    table = jnp.where(wide < 32, rounded, table - rounded).astype(jnp.bfloat16)
    for copy in y_copies:
        copy.wait_recv()
    for step in range(3):
        own = own + proj_recv[step].astype(jnp.float32)
    resid[...] = own
    mean_sq = jnp.mean(own * own, axis=-1, keepdims=True)
    ffn_in = (own * lax.rsqrt(mean_sq + epsilon) * ffn_gain[...]).astype(jnp.bfloat16)

    def spot(ref, piece):
        stream, dx, dz = piece
        return ref.at[at.zs(dz), stream, at.xs(dx)]

    for stream in range(2):
        mine = slice(stream * half, (stream + 1) * half)
        rows[at.z, stream, at.x, :, :width] = ffn_in[mine]
        rows[at.z, stream, at.x, :, width:] = table[mine]

    forward, arrive = forwarder(lambda piece: spot(rows, piece), ag_send, ag_recv)
    bundle_rows = 2 * CHIPS_X * half
    expert_lane = lax.broadcasted_iota(jnp.int32, (bundle_rows, 128), 1)
    expert_lane = (expert_lane % 32 == at.seq // 2) & (expert_lane < 64)

    def experts(places):
        blocks, gate_cols = [], []
        for p in places:
            bundle = rows[p].reshape(bundle_rows, rows.shape[-1])
            blocks.append(bundle[:, :width])
            gate = jnp.where(expert_lane, bundle[:, width:].astype(jnp.float32), 0.0)
            gate_cols.append(jnp.sum(gate, axis=1, keepdims=True))
        gathered = jnp.concatenate(blocks, axis=0)
        gate_col = jnp.concatenate(gate_cols, axis=0)
        total = None
        for part in range(2):
            gate_part = jnp.dot(gathered, gate_w[part], preferred_element_type=jnp.float32)
            up_part = jnp.dot(gathered, up_w[part], preferred_element_type=jnp.float32)
            hidden = gate_part / (1.0 + jnp.exp(-gate_part)) * up_part * gate_col
            term = jnp.dot(
                hidden.astype(jnp.bfloat16), down_w[part], preferred_element_type=jnp.float32
            )
            total = term if total is None else total + term
        total = total.astype(jnp.bfloat16)
        for i, p in enumerate(places):
            parts[p] = total[i * bundle_rows : (i + 1) * bundle_rows].reshape(parts.shape[1:])

    for piece in ORDER[0]:
        forward(piece)
    for r in range(1, ROUNDS + 1):
        for piece in ORDER[r]:
            arrive(piece)
            forward(piece)
        if r == 1:
            for copy in local_copies:
                copy.wait()
            for copy in twin_copies:
                copy.wait_recv()
        done = r - 2
        if done == 0:
            experts([at.zs(0)])
        elif 0 < done < 4:
            experts([at.zs(done), at.zs(-done)])
        elif done == 4:
            experts([at.zs(4)])

    def slot_of(piece):
        return sums.at[flat_piece(piece)]

    def child_wait(child):
        remote(
            slot_of(child),
            slot_of(child),
            rs_send.at[flat_piece(child)],
            rs_recv.at[flat_piece(child)],
            at.twin(),
        ).wait_recv()

    totals = []
    for r in range(ROUNDS, -1, -1):
        for piece in ORDER[r]:
            total = None
            for child, _ in CHILDREN[piece]:
                child_wait(child)
                if total is None:
                    total = spot(parts, piece)[...].astype(jnp.float32)
                total = total + slot_of(child)[...].astype(jnp.float32)
            if PARENT[piece] is None:
                totals.append(total)
                continue
            if total is not None:
                spot(parts, piece)[...] = total.astype(jnp.bfloat16)
            copy = remote(
                spot(parts, piece),
                slot_of(piece),
                rs_send.at[flat_piece(piece)],
                rs_recv.at[flat_piece(piece)],
                at.chip(*PARENT[piece]),
            )
            copy.start()
            sent.append(copy)
    for stream in range(2):
        mine = slice(stream * half, (stream + 1) * half)
        out[mine, :] = (resid[mine, :] + totals[stream]).astype(jnp.bfloat16)
    for copy in y_copies + twin_copies + shared + sent:
        copy.wait_send()


def layer_call(lengths, page_slots, tokens, *others):
    block, width = tokens.shape
    w_query, w_keyval, w_out, w_gate, w_up, w_down = others[-6:]
    share, half, lines = block // 4, block // 8, block // 2
    piece = w_gate.shape[2]
    kv_width = w_keyval.shape[1]
    kv_heads = kv_width // 128
    group = w_query.shape[1] // 64 // kv_heads
    smem = pl.BlockSpec(memory_space=pltpu.SMEM)
    vmem = pl.BlockSpec(memory_space=pltpu.VMEM)
    hbm = pl.BlockSpec(memory_space=pl.ANY)
    count = len(PIECES)
    dma = pltpu.SemaphoreType.DMA
    bf16, f32 = jnp.bfloat16, jnp.float32
    scratch = [
        (w_query.shape, bf16),
        (w_keyval.shape, bf16),
        (w_out.shape, bf16),
        ((2, width, piece), bf16),
        ((2, width, piece), bf16),
        ((2, piece, width), bf16),
        ((kv_heads, group * block, 128), bf16),
        ((CHIPS_Z, 2, 2, CHIPS_X, lines, kv_width), bf16),
        ((kv_heads, 1, group * block), f32),
        ((kv_heads, 1, group * block), f32),
        ((kv_heads, 64, group * block), f32),
        ((block, width), f32),
        ((block, width), bf16),
        ((3, share, width), bf16),
        ((CHIPS_Z, 2, CHIPS_X, half, width + 128), bf16),
        ((CHIPS_Z, 2, CHIPS_X, half, width), bf16),
        ((count, half, width), bf16),
        ((share, width), f32),
    ]
    sems = [6, 3, 3, count, count, CHIPS_Z, CHIPS_Z, 3, 3, count, count, count, count]
    return pl.pallas_call(
        layer_kernel,
        out_shape=(
            jax.ShapeDtypeStruct((share, width), bf16),
            jax.ShapeDtypeStruct((2, block, kv_width), bf16),
        ),
        in_specs=[smem] * 2 + [vmem] * 7 + [hbm] * 6,
        out_specs=(vmem, vmem),
        scratch_shapes=[pltpu.VMEM(*s) for s in scratch] + [dma((n,)) for n in sems],
        compiler_params=pltpu.CompilerParams(
            collective_id=1, has_side_effects=True, vmem_limit_bytes=56 << 20
        ),
        name="layer",
    )(lengths, page_slots, tokens, *others)


def body(
    tokens,
    attn_gain,
    w_query,
    w_keyval,
    w_out,
    ffn_gain,
    lengths,
    routes,
    route_gates,
    w_gate,
    w_up,
    w_down,
    page_slot_index,
):
    row_count = tokens.shape[0]
    seq_index = lax.axis_index("seq")
    kv_heads = w_keyval.shape[1]
    token = seq_index * row_count + jnp.arange(row_count, dtype=jnp.int32)
    edges = [jnp.sum(lengths[:d]) for d in range(1, lengths.shape[0])]
    begin = jnp.zeros_like(token)
    for edge in edges:
        begin = jnp.where(token >= edge, edge, begin)
    position = (token - begin).astype(jnp.float32)
    lane = jnp.arange(128, dtype=jnp.int32)
    inv_freq = rope_base ** (-(lane % 32).astype(jnp.float32) / 32)
    angle = position[:, None] * inv_freq[None, :]
    sign = jnp.where(lane % 64 < 32, -1.0, 1.0)
    layer_out, pages = layer_call(
        lengths,
        page_slot_index,
        tokens,
        attn_gain[None, :],
        jnp.cos(angle),
        jnp.sin(angle) * sign[None, :],
        ffn_gain[None, :],
        routes,
        route_gates,
        w_query,
        w_keyval.reshape(w_keyval.shape[0], -1),
        w_out,
        w_gate,
        w_up,
        w_down,
    )
    return (layer_out, pages.reshape(2, PAGE_TOKENS, kv_heads, -1))


def solution(mesh):
    placed = (
        P("seq", None),
        P(),
        P(None, "tp"),
        P(None, "tp", None),
        P("tp", None),
        P(),
        P(),
        P(("seq", "tp"), None),
        P(("seq", "tp"), None),
        P("seq", None, None),
        P("seq", None, None),
        P("seq", None, None),
        P(),
    )
    return jax.shard_map(
        body,
        mesh=mesh,
        in_specs=placed,
        out_specs=(P(("seq", "tp"), None), P("seq", None, "tp", None)),
        check_vma=False,
    )
```

```python
import jax
import jax.numpy as jnp
import numpy as np
from jax import lax
from jax.experimental import pallas as pl
from jax.experimental.pallas import tpu as pltpu
from jax.sharding import PartitionSpec as P

PAGE_TOKENS = 128


epsilon = 1e-05
rope_base = 10000.0

MESH = pl.DeviceIdType.MESH
CHIPS_X = 4
CHIPS_Z = 8

KEYVAL_TREE = (
    (0, 0, 0, 0, 0, -1), (1, 0, 0, 0, 0, -1), (0, 3, 0, 0, -1, 0), (1, 1, 0, 0, 1, 1),
    (1, 0, 2, 1, 2, 1), (0, 1, 0, 0, 1, 0), (1, 3, 0, 0, -1, 1), (1, 0, 5, 1, -3, 1),
    (1, 0, 1, 1, 1, 1), (0, 0, 7, 1, -1, 0), (1, 0, 7, 1, -1, 1), (0, 2, 0, 0, -1, 2),
    (1, 2, 0, 0, 1, 3), (0, 0, 3, 1, 3, 0), (1, 1, 2, 0, 1, 4), (1, 3, 2, 0, -1, 4),
    (1, 1, 1, 0, 1, 8), (1, 3, 5, 0, -1, 7), (0, 0, 5, 1, -3, 0), (0, 3, 2, 1, 2, 2),
    (0, 3, 7, 0, -1, 9), (1, 1, 5, 0, 1, 7), (0, 0, 6, 1, -1, 9), (1, 3, 1, 1, 1, 6),
    (1, 1, 7, 0, 1, 10), (1, 3, 7, 0, -1, 10), (0, 1, 7, 1, -1, 5), (1, 0, 6, 1, 1, 7),
    (0, 1, 3, 0, 1, 13), (0, 3, 3, 0, -1, 13), (1, 1, 3, 1, 1, 14), (1, 2, 2, 0, 1, 14),
    (0, 0, 1, 1, -2, 13), (1, 2, 5, 0, -1, 17), (0, 2, 1, 1, 1, 11), (0, 1, 5, 0, 1, 18),
    (0, 3, 5, 0, -1, 18), (0, 1, 1, 1, 1, 5), (1, 1, 4, 1, -1, 21), (0, 0, 2, 0, 1, 19),
    (0, 3, 6, 0, -1, 22), (1, 2, 1, 1, 1, 12), (1, 1, 6, 0, 1, 27), (1, 3, 3, 1, -2, 17),
    (0, 2, 3, 0, -1, 29), (0, 3, 4, 1, 1, 29), (1, 2, 3, 0, 1, 30), (1, 2, 7, 0, -1, 25),
    (0, 3, 1, 1, -1, 19), (0, 2, 7, 0, 1, 26), (1, 3, 4, 1, 2, 15), (1, 3, 6, 0, -1, 27),
    (0, 1, 4, 1, -1, 35), (0, 2, 5, 0, 1, 35), (1, 0, 4, 0, -1, 38), (0, 1, 2, 1, -1, 28),
    (0, 1, 6, 1, 1, 35), (0, 2, 6, 0, -1, 40), (1, 2, 4, 1, -1, 33), (1, 2, 6, 1, 1, 33),
    (1, 0, 3, 0, 1, 43), (0, 2, 4, 0, -1, 45), (0, 2, 2, 1, 1, 34), (0, 0, 4, 0, 1, 45),
)
KEYVAL_ACTS = (
    -2, -4, -7, -3, -5, -6, -8, -13, -9, -10, -18, 2, 3, -11, -12, 4, -14, -15, -19, 5,
    6, 7, -17, 8, -16, -21, -23, 9, -22, -20, -26, -27, 10, -24, -25, 11, 12, 13, -28, -29,
    -32, 14, 15, -30, -31, -34, 16, 17, -33, 18, -35, 19, -36, -37, -39, 20, 21, -38, -41, -43,
    22, 23, -40, 24, 25, 26, 27, -42, 28, 29, -44, -45, -47, -48, -50, 30, -46, -49, 31, 32,
    -51, 33, 34, 35, -52, -53, 36, -55, -56, 37, 38, -54, 39, 40, -57, -58, -59, 41, 42, 43,
    -60, 44, -62, 45, -61, -63, 46, 47, 48, 49, 50, 51, 52, 53, 54, 55, 56, 57, 58, 59,
    60, 61, 62, 63,
)

ROWS_TREE = (
    (0, 0, 0, 0, 0, -1), (1, 0, 0, 0, 0, -1), (0, 1, 0, 0, 1, 0), (0, 3, 0, 0, -1, 0),
    (1, 0, 1, 1, 1, 1), (1, 0, 6, 1, -2, 1), (1, 1, 0, 0, 1, 1), (1, 3, 0, 0, -1, 1),
    (0, 0, 2, 1, 2, 0), (0, 0, 7, 1, -1, 0), (1, 0, 7, 1, -1, 1), (0, 2, 0, 0, -1, 3),
    (1, 0, 2, 1, 1, 4), (1, 1, 6, 0, 1, 5), (0, 3, 1, 1, 1, 3), (1, 3, 6, 0, -1, 5),
    (0, 1, 6, 1, -2, 2), (1, 2, 0, 0, 1, 6), (0, 1, 1, 1, 1, 2), (0, 3, 7, 0, -1, 9),
    (0, 1, 7, 0, 1, 9), (0, 0, 3, 1, 1, 8), (1, 3, 2, 0, -1, 12), (1, 1, 7, 0, 1, 10),
    (1, 1, 5, 1, -3, 6), (1, 0, 3, 1, 1, 12), (1, 2, 6, 0, -1, 15), (1, 1, 2, 0, 1, 12),
    (0, 3, 2, 1, 1, 14), (0, 0, 1, 0, -1, 18), (0, 2, 1, 0, 1, 18), (0, 1, 5, 1, -1, 16),
    (1, 3, 7, 1, 1, 15), (0, 2, 7, 0, -1, 19), (0, 1, 3, 0, 1, 21), (1, 3, 1, 1, -1, 22),
    (0, 3, 3, 0, -1, 21), (1, 0, 4, 1, 1, 25), (1, 2, 5, 0, 1, 24), (1, 1, 1, 1, -1, 27),
    (1, 1, 3, 1, 1, 27), (1, 3, 3, 0, -1, 25), (0, 2, 5, 0, 1, 31), (0, 0, 5, 0, -1, 31),
    (0, 2, 2, 1, 1, 30), (0, 3, 6, 1, -2, 3), (0, 2, 3, 0, 1, 34), (0, 1, 4, 1, 1, 34),
    (1, 2, 1, 0, -1, 35), (1, 2, 4, 1, -1, 38), (1, 3, 5, 0, 1, 38), (0, 3, 4, 1, 1, 36),
    (1, 0, 5, 0, -1, 24), (1, 2, 3, 0, 1, 40), (0, 2, 4, 1, -1, 42), (1, 1, 4, 1, 1, 40),
    (1, 3, 4, 0, -1, 37), (0, 0, 6, 0, 1, 45), (0, 0, 4, 1, -1, 43), (0, 2, 6, 0, -1, 45),
    (1, 2, 7, 1, 1, 26), (0, 3, 5, 0, 1, 42), (0, 1, 2, 0, -1, 44), (1, 2, 2, 1, 1, 48),
)
ROWS_ACTS = (
    -2, -3, -4, -5, -8, -6, -7, -9, -10, 2, 3, 4, -11, -12, 5, -13, -16, -14, -15, 6,
    7, -17, 8, -18, 9, -19, -20, -24, -21, 10, 11, 12, -22, -23, 13, -25, 14, 15, -26, -27,
    16, 17, -28, 18, 19, -29, -30, -31, 20, -32, -33, 21, -34, 22, -35, 23, -36, 24, 25, -37,
    -38, 26, 27, -39, -40, -41, 28, 29, -45, 30, -44, 31, -43, -42, 32, 33, 34, -46, -47, 35,
    -48, 36, 37, 38, -49, -50, -51, -52, 39, 40, 41, -53, -55, -56, 42, -54, 43, 44, 45, -57,
    -58, -59, -60, 46, 47, 48, -61, -62, -63, 49, 50, 51, 52, 53, 54, 55, 56, 57, 58, 59,
    60, 61, 62, 63,
)

CHILDREN = {
    tree: [[c for c in range(len(tree)) if tree[c][5] == r] for r in range(len(tree))]
    for tree in (KEYVAL_TREE, ROWS_TREE)
}


class Place:
    def __init__(self):
        self.seq = lax.axis_index("seq")
        self.tp = lax.axis_index("tp")
        self.x = self.seq // (2 * CHIPS_Z)
        self.z = (self.seq // 2) % CHIPS_Z
        self.core = self.seq % 2

    def xs(self, dx):
        return lax.rem(self.x + dx + CHIPS_X, CHIPS_X)

    def zs(self, dz):
        return lax.rem(self.z + dz + CHIPS_Z, CHIPS_Z)

    def chip(self, axis, step):
        if axis == 0:
            return ((self.xs(step) * CHIPS_Z + self.z) * 2 + self.core, self.tp)
        return ((self.x * CHIPS_Z + self.zs(step)) * 2 + self.core, self.tp)

    def twin(self):
        return ((self.x * CHIPS_Z + self.z) * 2 + 1 - self.core, self.tp)

    def row(self, step):
        return (self.seq, lax.rem(self.tp + step + 4, 4))


def remote(src, dst, send_sem, recv_sem, device):
    return pltpu.make_async_remote_copy(
        src_ref=src,
        dst_ref=dst,
        send_sem=send_sem,
        recv_sem=recv_sem,
        device_id=device,
        device_id_type=MESH,
    )


def greet(at):
    steps = set()
    for tree in (KEYVAL_TREE, ROWS_TREE):
        for row in tree:
            if row[5] >= 0:
                size = CHIPS_Z if row[3] else CHIPS_X
                steps |= {(row[3], row[4] % size), (row[3], -row[4] % size)}
    partners = [at.chip(*s) for s in sorted(steps)]
    partners += [at.twin()] + [at.row(d) for d in (1, 2, 3)]
    barrier = pltpu.get_barrier_semaphore()
    for partner in partners:
        pl.semaphore_signal(barrier, inc=1, device_id=partner, device_id_type=MESH)
    pl.semaphore_wait(barrier, len(partners))


def spread(at, tree, acts, spot, send_sem, recv_sem, sent, arrived):
    count = 2
    for i, act in enumerate(acts):
        if act < 0:
            axis, step, parent = tree[-act][3:]
            copy = remote(
                spot(parent), spot(-act), send_sem.at[-act], recv_sem.at[-act], at.chip(axis, -step)
            )
            copy.start()
            sent.append(copy)
        else:
            remote(
                spot(act), spot(act), send_sem.at[act], recv_sem.at[act], at.chip(*tree[act][3:5])
            ).wait_recv()
            count = act + 1
        if i + 1 == len(acts) or acts[i + 1] > 0:
            arrived(count)


KV_GROUP = 4
KV_SHARES = (8, 16, 24, 32, 40, 48, 56, 60, 64)
ROW_GROUPS = (8, 16, 24, 32, 40, 48, 56, 64)


def layer_kernel(
    lengths,
    page_slots,
    numbers,
    tokens,
    attn_gain,
    ffn_gain,
    near_turn,
    far_turn,
    routes,
    route_gates,
    w_keyval,
    w_query,
    w_out,
    w_gate,
    w_up,
    w_down,
    out,
    pages,
    query_w,
    out_w,
    gate_w,
    up_w,
    down_w,
    queries,
    keyval,
    best,
    weight_sum,
    weighted,
    projected,
    proj_send,
    proj_recv,
    rows,
    parts,
    sums,
    resid,
    w_local,
    w_send,
    w_recv,
    kv_send,
    kv_recv,
    tw_send,
    tw_recv,
    y_send,
    y_recv,
    ag_send,
    ag_recv,
    rs_send,
    rs_recv,
):
    at = Place()
    width = tokens.shape[1]
    block = tokens.shape[0]
    share = block // 4
    half = share // 2
    lines = block // 2
    kv_heads = w_keyval.shape[1]
    query_copy = pltpu.make_async_copy(w_query, query_w, w_local.at[3])
    out_copy = pltpu.make_async_copy(w_out, out_w, w_local.at[4])
    query_copy.start()
    out_copy.start()

    def row_of(gain):
        return jnp.concatenate([gain[i : i + 1, :] for i in range(gain.shape[0])], axis=1)

    inputs = tokens[...].astype(jnp.float32)
    mean_sq = jnp.mean(inputs * inputs, axis=-1, keepdims=True)
    normed = (inputs * lax.rsqrt(mean_sq + epsilon) * row_of(attn_gain)).astype(jnp.bfloat16)
    keyval_w = w_keyval[...].reshape(width, kv_heads * 128)
    key_value_rows = jnp.dot(normed, keyval_w, preferred_element_type=jnp.float32)

    line = lax.broadcasted_iota(jnp.int32, (block, 128), 0)
    lane = lax.broadcasted_iota(jnp.int32, (block, 128), 1)
    low = lane % 64 < 32
    cos_all = jnp.zeros((block, 128), jnp.float32)
    sin_all = jnp.zeros((block, 128), jnp.float32)
    near_cos, near_sin = near_turn[0], near_turn[1]
    edge = jnp.int32(0)
    for d in range(lengths.shape[0]):
        base = at.seq * block - edge
        away = jnp.maximum(base, -base)
        tens, ones = pl.ds(away // block, 1), pl.ds(away % block, 1)
        cos_far, sin_far = far_turn[0, tens, :], far_turn[1, tens, :]
        cos_one, sin_one = near_turn[0, ones, :], near_turn[1, ones, :]
        cos_base = cos_far * cos_one - sin_far * sin_one
        sin_base = (sin_far * cos_one + cos_far * sin_one) * jnp.where(base < 0, -1.0, 1.0)
        inside = line + base >= 0
        cos_all = jnp.where(inside, cos_base * near_cos - sin_base * near_sin, cos_all)
        sin_all = jnp.where(inside, sin_base * near_cos + cos_base * near_sin, sin_all)
        edge = edge + lengths[d]
    sin_all = jnp.where(low, -sin_all, sin_all)

    def turn(values, cos_part, sin_part):
        swapped = jnp.where(low, pltpu.roll(values, 96, 1), pltpu.roll(values, 32, 1))
        return values * cos_part + swapped * sin_part

    cos_kv, sin_kv = jnp.where(lane < 64, cos_all, 1.0), jnp.where(lane < 64, sin_all, 0.0)
    for head in range(kv_heads):
        columns = slice(head * 128, (head + 1) * 128)
        turned = turn(key_value_rows[:, columns], cos_kv, sin_kv).astype(jnp.bfloat16)
        for stream in range(2):
            keyval[0, stream, :, columns] = turned[stream * lines : (stream + 1) * lines]
    greet(at)

    sent, shared = [], []
    weights = ((w_gate, gate_w), (w_up, up_w), (w_down, down_w))
    local_copies, twin_copies = [], []
    for i, (source, held) in enumerate(weights):
        local_copies.append(pltpu.make_async_copy(source.at[0], held.at[0], w_local.at[i]))
        twin_copies.append(
            remote(source.at[0], held.at[1], w_send.at[i], w_recv.at[i], at.twin())
        )

    token = at.seq * block + lax.broadcasted_iota(jnp.int32, (1, block), 1)
    begin = jnp.zeros((1, block), jnp.int32)
    edge = lengths[0]
    for d in range(1, lengths.shape[0]):
        begin = jnp.where(token >= edge, edge, begin)
        edge = edge + lengths[d]
    group = w_query.shape[1] // 64 // kv_heads
    count_keys = KV_GROUP * lines
    key_row = lax.broadcasted_iota(jnp.int32, (count_keys, 1), 0)

    def attend(first, other):
        core = 1 - at.core if other else at.core
        key = jnp.zeros((count_keys, 1), jnp.int32)
        for i in range(KV_GROUP):
            stream, dx, dz = KEYVAL_TREE[first + i][:3]
            start = ((at.xs(dx) * CHIPS_Z + at.zs(dz)) * 2 + core) * block + stream * lines
            key = jnp.where(key_row >= i * lines, start + key_row - i * lines, key)
        bundle = keyval[other, first : first + KV_GROUP].reshape(count_keys, 128 * kv_heads)
        turned = bundle.T
        bias = jnp.where((key <= token) & (key >= begin), 0.0, -1e30)
        bias = jnp.concatenate([bias] * group, axis=1)
        for head in range(kv_heads):
            scores = lax.dot_general(
                bundle[:, head * 128 : (head + 1) * 128],
                queries[head],
                (((1,), (1,)), ((), ())),
                preferred_element_type=jnp.float32,
            )
            scores = scores + bias
            old = best[head]
            new = jnp.maximum(old, jnp.max(scores, axis=0, keepdims=True))
            expd = jnp.exp2(scores - new)
            fade = jnp.exp2(old - new)
            best[head] = new
            weight_sum[head] = weight_sum[head] * fade + jnp.sum(expd, axis=0, keepdims=True)
            fresh = jnp.dot(
                turned[head * 128 + 64 : (head + 1) * 128],
                expd.astype(jnp.bfloat16),
                preferred_element_type=jnp.float32,
            )
            weighted[head] = weighted[head] * fade + fresh

    progress = {"done": 0, "started": False}
    waiting = []

    def start_up():
        for copy in local_copies + twin_copies:
            copy.start()
        query_copy.wait()
        scale = 64**-0.5 * 1.4426950408889634
        query_rows = jnp.dot(normed, query_w[...], preferred_element_type=jnp.float32)
        for pair in range(query_rows.shape[1] // 128):
            turned = turn(query_rows[:, pair * 128 : (pair + 1) * 128], cos_all, sin_all) * scale
            for odd in range(2):
                head = 2 * pair + odd
                placed = pltpu.roll(turned, 64, 1) if odd else turned
                placed = jnp.where(lane < 64, placed, 0.0).astype(jnp.bfloat16)
                lower = (head % group) * block
                queries[head // group, lower : lower + block, :] = placed
        best[...] = jnp.full_like(best, -1e30)
        weight_sum[...] = jnp.zeros_like(weight_sum)
        weighted[...] = jnp.zeros_like(weighted)

    def meet_twin():
        for number in waiting:
            lower, upper = waiting_range(number)
            place = keyval.at[1, lower:upper]
            remote(place, place, tw_send.at[number], tw_recv.at[number], at.twin()).wait_recv()
            for first in range(lower, upper, KV_GROUP):
                attend(first, 1)
        waiting.clear()

    def waiting_range(number):
        return (KV_SHARES[number - 1] if number else 0), KV_SHARES[number]

    def keys_here(count):
        if not progress["started"]:
            progress["started"] = True
            start_up()
        number = progress["done"]
        if number < len(KV_SHARES) and count >= KV_SHARES[number]:
            lower, upper = waiting_range(number)
            copy = remote(
                keyval.at[0, lower:upper],
                keyval.at[1, lower:upper],
                tw_send.at[number],
                tw_recv.at[number],
                at.twin(),
            )
            copy.start()
            shared.append(copy)
            for first in range(lower, upper, KV_GROUP):
                attend(first, 0)
            meet_twin()
            waiting.append(number)
            progress["done"] = number + 1

    spread(
        at,
        KEYVAL_TREE,
        KEYVAL_ACTS,
        lambda r: keyval.at[0, r],
        kv_send,
        kv_recv,
        sent,
        keys_here,
    )
    meet_twin()

    columns = []
    for head in range(kv_heads):
        mean = weighted[head] / weight_sum[head]
        for g in range(group):
            columns.append(mean[:, g * block : (g + 1) * block])
    attended = jnp.concatenate(columns, axis=0).T.astype(jnp.bfloat16)

    out_copy.wait()
    projected[...] = jnp.dot(attended, out_w[...], preferred_element_type=jnp.float32)
    proj_send[...] = projected[...].astype(jnp.bfloat16)
    y_copies = []
    for step in (2, 1, 3):
        theirs = at.row(step)[1]
        y_copies.append(
            remote(
                proj_send.at[pl.ds(pl.multiple_of(theirs * share, share), share)],
                proj_recv.at[step - 1],
                y_send.at[step - 1],
                y_recv.at[step - 1],
                at.row(step),
            )
        )
        y_copies[-1].start()
    first = pl.multiple_of(at.tp * share, share)
    own = projected[pl.ds(first, share), :] + tokens[pl.ds(first, share), :].astype(jnp.float32)
    expert = lax.broadcasted_iota(jnp.int32, (128, share), 0)
    table = jnp.zeros((128, share), jnp.float32)
    for k in range(routes.shape[0]):
        chosen = expert % 32 == routes[k : k + 1, :]
        table = table + jnp.where(chosen, route_gates[k : k + 1, :], 0.0)
    rounded = table.astype(jnp.bfloat16).astype(jnp.float32)
    table = jnp.where(expert < 32, rounded, table - rounded).T.astype(jnp.bfloat16)
    for stream in range(2):
        rows[stream, :, width:] = table[stream * half : (stream + 1) * half]
    for slot in range(pages.shape[0]):
        wanted = at.seq * pages.shape[0] + slot

        def look(n, found):
            return jnp.where(page_slots[n] == wanted, n, found)

        page = lax.fori_loop(0, page_slots.shape[0], look, jnp.int32(-1), unroll=8)
        taken = jnp.maximum(page, 0)
        dx = (taken // (2 * CHIPS_Z) + CHIPS_X - at.x) % CHIPS_X
        dz = ((taken // 2) % CHIPS_Z + CHIPS_Z - at.z) % CHIPS_Z
        other = (taken + at.core) % 2
        for stream in range(2):
            held = keyval[other, numbers[(stream * CHIPS_X + dx) * CHIPS_Z + dz]]
            shown = jnp.broadcast_to(page, held.shape) >= 0
            held = jnp.where(shown, held.astype(jnp.float32), 0.0).astype(jnp.bfloat16)
            pages[slot, stream * lines : (stream + 1) * lines] = held.reshape(
                lines, kv_heads, 128
            )
    for copy in y_copies:
        copy.wait_recv()
    for step in range(3):
        own = own + proj_recv[step].astype(jnp.float32)
    resid[...] = own
    mean_sq = jnp.mean(own * own, axis=-1, keepdims=True)
    ffn_in = (own * lax.rsqrt(mean_sq + epsilon) * row_of(ffn_gain)).astype(jnp.bfloat16)
    for stream in range(2):
        rows[stream, :, :width] = ffn_in[stream * half : (stream + 1) * half]

    def experts(lower, upper):
        size = (upper - lower) * half
        gathered = rows[lower:upper].reshape(size, rows.shape[-1])
        wide = lax.broadcasted_iota(jnp.int32, (size, 128), 1)
        named = (wide % 32 == at.seq // 2) & (wide < 64)
        gate_col = jnp.where(named, gathered[:, width:].astype(jnp.float32), 0.0)
        gate_col = jnp.sum(gate_col, axis=1, keepdims=True)
        gathered = gathered[:, :width]
        total = None
        for part in range(2):
            gate_part = jnp.dot(gathered, gate_w[part], preferred_element_type=jnp.float32)
            up_part = jnp.dot(gathered, up_w[part], preferred_element_type=jnp.float32)
            hidden = gate_part / (1.0 + jnp.exp(-gate_part)) * up_part * gate_col
            term = jnp.dot(
                hidden.astype(jnp.bfloat16), down_w[part], preferred_element_type=jnp.float32
            )
            total = term if total is None else total + term
        parts[lower:upper] = total.astype(jnp.bfloat16).reshape(upper - lower, half, width)

    stage = {"done": 0, "weights": False}

    def rows_here(count):
        number = stage["done"]
        if number < len(ROW_GROUPS) and count >= ROW_GROUPS[number]:
            if not stage["weights"]:
                stage["weights"] = True
                for copy in local_copies:
                    copy.wait()
                for copy in twin_copies:
                    copy.wait_recv()
            experts(ROW_GROUPS[number - 1] if number else 0, ROW_GROUPS[number])
            stage["done"] = number + 1

    spread(at, ROWS_TREE, ROWS_ACTS, lambda r: rows.at[r], ag_send, ag_recv, sent, rows_here)

    def add_up(r):
        total = parts[r].astype(jnp.float32)
        for child in CHILDREN[ROWS_TREE][r]:
            total = total + sums[child].astype(jnp.float32)
        return total

    for act in reversed(ROWS_ACTS):
        if act < 0:
            place = sums.at[-act]
            remote(place, place, rs_send.at[-act], rs_recv.at[-act], at.twin()).wait_recv()
            continue
        if CHILDREN[ROWS_TREE][act]:
            parts[act] = add_up(act).astype(jnp.bfloat16)
        copy = remote(
            parts.at[act],
            sums.at[act],
            rs_send.at[act],
            rs_recv.at[act],
            at.chip(*ROWS_TREE[act][3:5]),
        )
        copy.start()
        sent.append(copy)
    for stream in range(2):
        mine = slice(stream * half, (stream + 1) * half)
        out[mine, :] = (resid[mine, :] + add_up(stream)).astype(jnp.bfloat16)
    for copy in y_copies + twin_copies + shared + sent:
        copy.wait_send()


def layer_call(lengths, page_slots, numbers, tokens, *others):
    block, width = tokens.shape
    w_keyval, w_query, w_out, w_gate, w_up, w_down = others[-6:]
    share, half, lines = block // 4, block // 8, block // 2
    piece = w_gate.shape[2]
    kv_heads = w_keyval.shape[1]
    kv_width = kv_heads * 128
    group = w_query.shape[1] // 64 // kv_heads
    smem = pl.BlockSpec(memory_space=pltpu.SMEM)
    vmem = pl.BlockSpec(memory_space=pltpu.VMEM)
    hbm = pl.BlockSpec(memory_space=pl.ANY)
    count = len(ROWS_TREE)
    dma = pltpu.SemaphoreType.DMA
    bf16, f32 = jnp.bfloat16, jnp.float32
    scratch = [
        (w_query.shape, bf16),
        (w_out.shape, bf16),
        ((2, width, piece), bf16),
        ((2, width, piece), bf16),
        ((2, piece, width), bf16),
        ((kv_heads, group * block, 128), bf16),
        ((2, count, lines, kv_width), bf16),
        ((kv_heads, 1, group * block), f32),
        ((kv_heads, 1, group * block), f32),
        ((kv_heads, 64, group * block), f32),
        ((block, width), f32),
        ((block, width), bf16),
        ((3, share, width), bf16),
        ((count, half, width + 128), bf16),
        ((count, half, width), bf16),
        ((count, half, width), bf16),
        ((share, width), f32),
    ]
    sems = [5, 3, 3, count, count, len(KV_SHARES), len(KV_SHARES), 3, 3]
    sems += [count, count, count, count]
    return pl.pallas_call(
        layer_kernel,
        out_shape=(
            jax.ShapeDtypeStruct((share, width), bf16),
            jax.ShapeDtypeStruct((2, block, kv_heads, 128), bf16),
        ),
        in_specs=[smem] * 3 + [vmem] * 8 + [hbm] * 5,
        out_specs=(vmem, vmem),
        scratch_shapes=[pltpu.VMEM(*s) for s in scratch] + [dma((n,)) for n in sems],
        compiler_params=pltpu.CompilerParams(
            collective_id=1, has_side_effects=True, vmem_limit_bytes=56 << 20
        ),
        name="layer",
    )(lengths, page_slots, numbers, tokens, *others)


def turn_tables(steps, stride):
    inv_freq = rope_base ** (-(np.arange(128) % 32) / 32.0)
    angle = (np.arange(steps) * stride)[:, None] * inv_freq[None, :]
    return np.stack([np.cos(angle), np.sin(angle)]).astype(np.float32)


def body(
    tokens,
    attn_gain,
    w_query,
    w_keyval,
    w_out,
    ffn_gain,
    lengths,
    routes,
    route_gates,
    w_gate,
    w_up,
    w_down,
    page_slot_index,
):
    block = tokens.shape[0]
    numbers = np.zeros(len(KEYVAL_TREE), np.int32)
    for r, (stream, dx, dz) in enumerate(row[:3] for row in KEYVAL_TREE):
        numbers[(stream * CHIPS_X + dx) * CHIPS_Z + dz] = r
    return layer_call(
        lengths,
        page_slot_index,
        jnp.asarray(numbers),
        tokens,
        attn_gain.reshape(-1, 128),
        ffn_gain.reshape(-1, 128),
        jnp.asarray(turn_tables(block, 1)),
        jnp.asarray(turn_tables(2 * CHIPS_X * CHIPS_Z, block)),
        routes.T,
        route_gates.T,
        w_keyval,
        w_query,
        w_out,
        w_gate,
        w_up,
        w_down,
    )


def solution(mesh):
    placed = (
        P("seq", None),
        P(),
        P(None, "tp"),
        P(None, "tp", None),
        P("tp", None),
        P(),
        P(),
        P(("seq", "tp"), None),
        P(("seq", "tp"), None),
        P("seq", None, None),
        P("seq", None, None),
        P("seq", None, None),
        P(),
    )
    return jax.shard_map(
        body,
        mesh=mesh,
        in_specs=placed,
        out_specs=(P(("seq", "tp"), None), P("seq", None, "tp", None)),
        check_vma=False,
    )
```

```python
import jax
import jax.numpy as jnp
import numpy as np
from jax import lax
from jax.experimental import pallas as pl
from jax.experimental.pallas import tpu as pltpu
from jax.sharding import PartitionSpec as P

PAGE_TOKENS = 128


epsilon = 1e-05
rope_base = 10000.0

MESH = pl.DeviceIdType.MESH
CHIPS_X = 4
CHIPS_Z = 8

KEYVAL_TREE = (
    (0, 0, 0, 0, 0, -1), (1, 0, 0, 0, 0, -1), (0, 3, 0, 0, -1, 0), (1, 1, 0, 0, 1, 1),
    (1, 0, 2, 1, 2, 1), (0, 1, 0, 0, 1, 0), (1, 3, 0, 0, -1, 1), (1, 0, 5, 1, -3, 1),
    (1, 0, 1, 1, 1, 1), (0, 0, 7, 1, -1, 0), (1, 0, 7, 1, -1, 1), (0, 2, 0, 0, -1, 2),
    (1, 2, 0, 0, 1, 3), (0, 0, 3, 1, 3, 0), (1, 1, 2, 0, 1, 4), (1, 3, 2, 0, -1, 4),
    (1, 1, 1, 0, 1, 8), (1, 3, 5, 0, -1, 7), (0, 0, 5, 1, -3, 0), (0, 3, 2, 1, 2, 2),
    (0, 3, 7, 0, -1, 9), (1, 1, 5, 0, 1, 7), (0, 0, 6, 1, -1, 9), (1, 3, 1, 1, 1, 6),
    (1, 1, 7, 0, 1, 10), (1, 3, 7, 0, -1, 10), (0, 1, 7, 1, -1, 5), (1, 0, 6, 1, 1, 7),
    (0, 1, 3, 0, 1, 13), (0, 3, 3, 0, -1, 13), (1, 1, 3, 1, 1, 14), (1, 2, 2, 0, 1, 14),
    (0, 0, 1, 1, -2, 13), (1, 2, 5, 0, -1, 17), (0, 2, 1, 1, 1, 11), (0, 1, 5, 0, 1, 18),
    (0, 3, 5, 0, -1, 18), (0, 1, 1, 1, 1, 5), (1, 1, 4, 1, -1, 21), (0, 0, 2, 0, 1, 19),
    (0, 3, 6, 0, -1, 22), (1, 2, 1, 1, 1, 12), (1, 1, 6, 0, 1, 27), (1, 3, 3, 1, -2, 17),
    (0, 2, 3, 0, -1, 29), (0, 3, 4, 1, 1, 29), (1, 2, 3, 0, 1, 30), (1, 2, 7, 0, -1, 25),
    (0, 3, 1, 1, -1, 19), (0, 2, 7, 0, 1, 26), (1, 3, 4, 1, 2, 15), (1, 3, 6, 0, -1, 27),
    (0, 1, 4, 1, -1, 35), (0, 2, 5, 0, 1, 35), (1, 0, 4, 0, -1, 38), (0, 1, 2, 1, -1, 28),
    (0, 1, 6, 1, 1, 35), (0, 2, 6, 0, -1, 40), (1, 2, 4, 1, -1, 33), (1, 2, 6, 1, 1, 33),
    (1, 0, 3, 0, 1, 43), (0, 2, 4, 0, -1, 45), (0, 2, 2, 1, 1, 34), (0, 0, 4, 0, 1, 45),
)
KEYVAL_ACTS = (
    -2, -4, -7, -3, -5, -6, -8, -13, -9, -10, -18, 2, 3, -11, -12, 4, -14, -15, -19, 5,
    6, 7, -17, 8, -16, -21, -23, 9, -22, -20, -26, -27, 10, -24, -25, 11, 12, 13, -28, -29,
    -32, 14, 15, -30, -31, -34, 16, 17, -33, 18, -35, 19, -36, -37, -39, 20, 21, -38, -41, -43,
    22, 23, -40, 24, 25, 26, 27, -42, 28, 29, -44, -45, -47, -48, -50, 30, -46, -49, 31, 32,
    -51, 33, 34, 35, -52, -53, 36, -55, -56, 37, 38, -54, 39, 40, -57, -58, -59, 41, 42, 43,
    -60, 44, -62, 45, -61, -63, 46, 47, 48, 49, 50, 51, 52, 53, 54, 55, 56, 57, 58, 59,
    60, 61, 62, 63,
)

ROWS_TREE = (
    (0, 0, 0, 0, 0, -1), (1, 0, 0, 0, 0, -1), (0, 1, 0, 0, 1, 0), (0, 3, 0, 0, -1, 0),
    (1, 0, 1, 1, 1, 1), (1, 0, 6, 1, -2, 1), (1, 1, 0, 0, 1, 1), (1, 3, 0, 0, -1, 1),
    (0, 0, 2, 1, 2, 0), (0, 0, 7, 1, -1, 0), (1, 0, 7, 1, -1, 1), (0, 2, 0, 0, -1, 3),
    (1, 0, 2, 1, 1, 4), (1, 1, 6, 0, 1, 5), (0, 3, 1, 1, 1, 3), (1, 3, 6, 0, -1, 5),
    (0, 1, 6, 1, -2, 2), (1, 2, 0, 0, 1, 6), (0, 1, 1, 1, 1, 2), (0, 3, 7, 0, -1, 9),
    (0, 1, 7, 0, 1, 9), (0, 0, 3, 1, 1, 8), (1, 3, 2, 0, -1, 12), (1, 1, 7, 0, 1, 10),
    (1, 1, 5, 1, -3, 6), (1, 0, 3, 1, 1, 12), (1, 2, 6, 0, -1, 15), (1, 1, 2, 0, 1, 12),
    (0, 3, 2, 1, 1, 14), (0, 0, 1, 0, -1, 18), (0, 2, 1, 0, 1, 18), (0, 1, 5, 1, -1, 16),
    (1, 3, 7, 1, 1, 15), (0, 2, 7, 0, -1, 19), (0, 1, 3, 0, 1, 21), (1, 3, 1, 1, -1, 22),
    (0, 3, 3, 0, -1, 21), (1, 0, 4, 1, 1, 25), (1, 2, 5, 0, 1, 24), (1, 1, 1, 1, -1, 27),
    (1, 1, 3, 1, 1, 27), (1, 3, 3, 0, -1, 25), (0, 2, 5, 0, 1, 31), (0, 0, 5, 0, -1, 31),
    (0, 2, 2, 1, 1, 30), (0, 3, 6, 1, -2, 3), (0, 2, 3, 0, 1, 34), (0, 1, 4, 1, 1, 34),
    (1, 2, 1, 0, -1, 35), (1, 2, 4, 1, -1, 38), (1, 3, 5, 0, 1, 38), (0, 3, 4, 1, 1, 36),
    (1, 0, 5, 0, -1, 24), (1, 2, 3, 0, 1, 40), (0, 2, 4, 1, -1, 42), (1, 1, 4, 1, 1, 40),
    (1, 3, 4, 0, -1, 37), (0, 0, 6, 0, 1, 45), (0, 0, 4, 1, -1, 43), (0, 2, 6, 0, -1, 45),
    (1, 2, 7, 1, 1, 26), (0, 3, 5, 0, 1, 42), (0, 1, 2, 0, -1, 44), (1, 2, 2, 1, 1, 48),
)
ROWS_ACTS = (
    -2, -3, -4, -5, -8, -6, -7, -9, -10, 2, 3, 4, -11, -12, 5, -13, -16, -14, -15, 6,
    7, -17, 8, -18, 9, -19, -20, -24, -21, 10, 11, 12, -22, -23, 13, -25, 14, 15, -26, -27,
    16, 17, -28, 18, 19, -29, -30, -31, 20, -32, -33, 21, -34, 22, -35, 23, -36, 24, 25, -37,
    -38, 26, 27, -39, -40, -41, 28, 29, -45, 30, -44, 31, -43, -42, 32, 33, 34, -46, -47, 35,
    -48, 36, 37, 38, -49, -50, -51, -52, 39, 40, 41, -53, -55, -56, 42, -54, 43, 44, 45, -57,
    -58, -59, -60, 46, 47, 48, -61, -62, -63, 49, 50, 51, 52, 53, 54, 55, 56, 57, 58, 59,
    60, 61, 62, 63,
)

CHILDREN = {
    tree: [[c for c in range(len(tree)) if tree[c][5] == r] for r in range(len(tree))]
    for tree in (KEYVAL_TREE, ROWS_TREE)
}


class Place:
    def __init__(self):
        self.seq = lax.axis_index("seq")
        self.tp = lax.axis_index("tp")
        self.x = self.seq // (2 * CHIPS_Z)
        self.z = (self.seq // 2) % CHIPS_Z
        self.core = self.seq % 2

    def xs(self, dx):
        return lax.rem(self.x + dx + CHIPS_X, CHIPS_X)

    def zs(self, dz):
        return lax.rem(self.z + dz + CHIPS_Z, CHIPS_Z)

    def chip(self, axis, step):
        if axis == 0:
            return ((self.xs(step) * CHIPS_Z + self.z) * 2 + self.core, self.tp)
        return ((self.x * CHIPS_Z + self.zs(step)) * 2 + self.core, self.tp)

    def twin(self):
        return ((self.x * CHIPS_Z + self.z) * 2 + 1 - self.core, self.tp)

    def row(self, step):
        return (self.seq, lax.rem(self.tp + step + 4, 4))


def remote(src, dst, send_sem, recv_sem, device):
    return pltpu.make_async_remote_copy(
        src_ref=src,
        dst_ref=dst,
        send_sem=send_sem,
        recv_sem=recv_sem,
        device_id=device,
        device_id_type=MESH,
    )


def greet(at):
    steps = set()
    for tree in (KEYVAL_TREE, ROWS_TREE):
        for row in tree:
            if row[5] >= 0:
                size = CHIPS_Z if row[3] else CHIPS_X
                steps |= {(row[3], row[4] % size), (row[3], -row[4] % size)}
    partners = [at.chip(*s) for s in sorted(steps)]
    partners += [at.twin()] + [at.row(d) for d in (1, 2, 3)]
    barrier = pltpu.get_barrier_semaphore()
    for partner in partners:
        pl.semaphore_signal(barrier, inc=1, device_id=partner, device_id_type=MESH)
    return lambda: pl.semaphore_wait(barrier, len(partners))


def spread(at, tree, acts, spot, send_sem, recv_sem, sent, arrived):
    count = 2
    for i, act in enumerate(acts):
        if act < 0:
            axis, step, parent = tree[-act][3:]
            copy = remote(
                spot(parent), spot(-act), send_sem.at[-act], recv_sem.at[-act], at.chip(axis, -step)
            )
            copy.start()
            sent.append(copy)
        else:
            remote(
                spot(act), spot(act), send_sem.at[act], recv_sem.at[act], at.chip(*tree[act][3:5])
            ).wait_recv()
            count = act + 1
        if i + 1 == len(acts) or acts[i + 1] > 0:
            arrived(count)


KV_SHARES = (8, 16, 24, 32, 40, 48, 56, 60, 64)
ROW_GROUPS = (8, 16, 24, 32, 40, 48, 56, 64)


def layer_kernel(
    lengths,
    page_slots,
    numbers,
    attn_gain,
    ffn_gain,
    far_turn,
    routes,
    route_gates,
    tokens_in,
    near_turn_in,
    w_keyval_in,
    w_query,
    w_out,
    w_gate,
    w_up,
    w_down,
    out,
    pages,
    tokens,
    near_turn,
    w_keyval,
    query_w,
    out_w,
    gate_w,
    up_w,
    down_w,
    queries,
    keyval,
    best,
    weighted,
    projected,
    proj_send,
    proj_recv,
    rows,
    parts,
    sums,
    resid,
    w_local,
    w_send,
    w_recv,
    kv_send,
    kv_recv,
    tw_send,
    tw_recv,
    y_send,
    y_recv,
    ag_send,
    ag_recv,
    rs_send,
    rs_recv,
):
    at = Place()
    all_here = greet(at)
    early = [
        pltpu.make_async_copy(source, held, w_local.at[5 + i])
        for i, (source, held) in enumerate(
            ((tokens_in, tokens), (w_keyval_in, w_keyval), (near_turn_in, near_turn))
        )
    ]
    for copy in early:
        copy.start()
    width = tokens.shape[1]
    block = tokens.shape[0]
    share = block // 4
    half = share // 2
    lines = block // 2
    kv_heads = w_keyval.shape[1]
    query_copy = pltpu.make_async_copy(w_query, query_w, w_local.at[3])
    out_copy = pltpu.make_async_copy(w_out, out_w, w_local.at[4])
    query_copy.start()
    out_copy.start()

    def row_of(gain):
        return jnp.concatenate([gain[i : i + 1, :] for i in range(gain.shape[0])], axis=1)

    early[0].wait()
    inputs = tokens[...].astype(jnp.float32)
    mean_sq = jnp.mean(inputs * inputs, axis=-1, keepdims=True)
    normed = (inputs * lax.rsqrt(mean_sq + epsilon) * row_of(attn_gain)).astype(jnp.bfloat16)
    early[1].wait()
    keyval_w = w_keyval[...].reshape(width, kv_heads * 128)
    key_value_rows = jnp.dot(normed, keyval_w, preferred_element_type=jnp.float32)

    line = lax.broadcasted_iota(jnp.int32, (block, 128), 0)
    lane = lax.broadcasted_iota(jnp.int32, (block, 128), 1)
    low = lane % 64 < 32
    cos_all = jnp.zeros((block, 128), jnp.float32)
    sin_all = jnp.zeros((block, 128), jnp.float32)
    early[2].wait()
    near_cos, near_sin = near_turn[0], near_turn[1]
    edge = jnp.int32(0)
    for d in range(lengths.shape[0]):
        base = at.seq * block - edge
        away = jnp.maximum(base, -base)
        tens, ones = pl.ds(away // block, 1), pl.ds(away % block, 1)
        cos_far, sin_far = far_turn[0, tens, :], far_turn[1, tens, :]
        cos_one, sin_one = near_turn[0, ones, :], near_turn[1, ones, :]
        cos_base = cos_far * cos_one - sin_far * sin_one
        sin_base = (sin_far * cos_one + cos_far * sin_one) * jnp.where(base < 0, -1.0, 1.0)
        inside = line + base >= 0
        cos_all = jnp.where(inside, cos_base * near_cos - sin_base * near_sin, cos_all)
        sin_all = jnp.where(inside, sin_base * near_cos + cos_base * near_sin, sin_all)
        edge = edge + lengths[d]
    sin_all = jnp.where(low, -sin_all, sin_all)

    def turn(values, cos_part, sin_part):
        swapped = jnp.where(low, pltpu.roll(values, 96, 1), pltpu.roll(values, 32, 1))
        return values * cos_part + swapped * sin_part

    cos_kv, sin_kv = jnp.where(lane < 64, cos_all, 1.0), jnp.where(lane < 64, sin_all, 0.0)
    for head in range(kv_heads):
        columns = slice(head * 128, (head + 1) * 128)
        turned = turn(key_value_rows[:, columns], cos_kv, sin_kv).astype(jnp.bfloat16)
        for stream in range(2):
            keyval[0, stream, :, columns] = turned[stream * lines : (stream + 1) * lines]
    all_here()

    sent, shared = [], []
    weights = ((w_gate, gate_w), (w_up, up_w), (w_down, down_w))
    local_copies, twin_copies = [], []
    for i, (source, held) in enumerate(weights):
        local_copies.append(pltpu.make_async_copy(source.at[0], held.at[0], w_local.at[i]))
        twin_copies.append(
            remote(source.at[0], held.at[1], w_send.at[i], w_recv.at[i], at.twin())
        )

    token = at.seq * block + lax.broadcasted_iota(jnp.int32, (1, block), 1)
    begin = jnp.zeros((1, block), jnp.int32)
    edge = lengths[0]
    for d in range(1, lengths.shape[0]):
        begin = jnp.where(token >= edge, edge, begin)
        edge = edge + lengths[d]
    group = w_query.shape[1] // 64 // kv_heads

    def attend(number, other):
        lower, upper = share_range(number)
        if other:
            place = keyval.at[1, lower:upper]
            remote(place, place, tw_send.at[number], tw_recv.at[number], at.twin()).wait_recv()
        core = 1 - at.core if other else at.core
        count_keys = (upper - lower) * lines
        key_row = lax.broadcasted_iota(jnp.int32, (count_keys, 1), 0)
        key = jnp.zeros((count_keys, 1), jnp.int32)
        for i in range(upper - lower):
            stream, dx, dz = KEYVAL_TREE[lower + i][:3]
            start = ((at.xs(dx) * CHIPS_Z + at.zs(dz)) * 2 + core) * block + stream * lines
            key = jnp.where(key_row >= i * lines, start + key_row - i * lines, key)
        bundle = keyval[other, lower:upper].reshape(count_keys, 128 * kv_heads)
        turned = bundle.T
        bias = jnp.where((key <= token) & (key >= begin), 0.0, -1e30)
        bias = jnp.concatenate([bias] * group, axis=1)
        for head in range(kv_heads):
            scores = lax.dot_general(
                bundle[:, head * 128 : (head + 1) * 128],
                queries[head],
                (((1,), (1,)), ((), ())),
                preferred_element_type=jnp.float32,
            )
            scores = scores + bias
            old = best[head]
            new = jnp.maximum(old, jnp.max(scores, axis=0, keepdims=True))
            expd = jnp.exp2(scores - new)
            fade = jnp.exp2(old - new)
            best[head] = new
            values = turned[head * 128 + 64 : (head + 1) * 128]
            values = jnp.concatenate([values, jnp.ones((16, count_keys), jnp.bfloat16)], axis=0)
            fresh = jnp.dot(values, expd.astype(jnp.bfloat16), preferred_element_type=jnp.float32)
            weighted[head] = weighted[head] * fade + fresh

    progress = {"done": 0, "started": False}
    waiting = []

    def share_range(number):
        return (KV_SHARES[number - 1] if number else 0), KV_SHARES[number]

    def start_up():
        for copy in local_copies + twin_copies:
            copy.start()
        query_copy.wait()
        scale = 64**-0.5 * 1.4426950408889634
        query_rows = jnp.dot(normed, query_w[...], preferred_element_type=jnp.float32)
        for pair in range(query_rows.shape[1] // 128):
            turned = turn(query_rows[:, pair * 128 : (pair + 1) * 128], cos_all, sin_all) * scale
            for odd in range(2):
                head = 2 * pair + odd
                placed = pltpu.roll(turned, 64, 1) if odd else turned
                placed = jnp.where(lane < 64, placed, 0.0).astype(jnp.bfloat16)
                lower = (head % group) * block
                queries[head // group, lower : lower + block, :] = placed
        best[...] = jnp.full_like(best, -1e30)
        weighted[...] = jnp.zeros_like(weighted)

    def keys_here(count):
        if not progress["started"]:
            progress["started"] = True
            start_up()
        number = progress["done"]
        if number < len(KV_SHARES) and count >= KV_SHARES[number]:
            lower, upper = share_range(number)
            copy = remote(
                keyval.at[0, lower:upper],
                keyval.at[1, lower:upper],
                tw_send.at[number],
                tw_recv.at[number],
                at.twin(),
            )
            copy.start()
            shared.append(copy)
            if number:
                waiting.append((number - 1, 1))
            waiting.append((number, 0))
            progress["done"] = number + 1
        if waiting:
            attend(*waiting.pop(0))

    spread(
        at,
        KEYVAL_TREE,
        KEYVAL_ACTS,
        lambda r: keyval.at[0, r],
        kv_send,
        kv_recv,
        sent,
        keys_here,
    )
    for unit in waiting + [(len(KV_SHARES) - 1, 1)]:
        attend(*unit)

    columns = []
    for head in range(kv_heads):
        mean = weighted[head, :64] / weighted[head, 64:65]
        for g in range(group):
            columns.append(mean[:, g * block : (g + 1) * block])
    attended = jnp.concatenate(columns, axis=0).T.astype(jnp.bfloat16)

    out_copy.wait()
    projected[...] = jnp.dot(attended, out_w[...], preferred_element_type=jnp.float32)
    proj_send[...] = projected[...].astype(jnp.bfloat16)
    y_copies = []
    for step in (2, 1, 3):
        theirs = at.row(step)[1]
        y_copies.append(
            remote(
                proj_send.at[pl.ds(pl.multiple_of(theirs * share, share), share)],
                proj_recv.at[step - 1],
                y_send.at[step - 1],
                y_recv.at[step - 1],
                at.row(step),
            )
        )
        y_copies[-1].start()
    first = pl.multiple_of(at.tp * share, share)
    own = projected[pl.ds(first, share), :] + tokens[pl.ds(first, share), :].astype(jnp.float32)
    expert = lax.broadcasted_iota(jnp.int32, (128, share), 0)
    table = jnp.zeros((128, share), jnp.float32)
    for k in range(routes.shape[0]):
        chosen = expert % 32 == routes[k : k + 1, :]
        table = table + jnp.where(chosen, route_gates[k : k + 1, :], 0.0)
    rounded = table.astype(jnp.bfloat16).astype(jnp.float32)
    table = jnp.where(expert < 32, rounded, table - rounded).T.astype(jnp.bfloat16)
    for stream in range(2):
        rows[stream, :, width:] = table[stream * half : (stream + 1) * half]
    for slot in range(pages.shape[0]):
        wanted = at.seq * pages.shape[0] + slot

        def look(n, found):
            return jnp.where(page_slots[n] == wanted, n, found)

        page = lax.fori_loop(0, page_slots.shape[0], look, jnp.int32(-1), unroll=8)
        taken = jnp.maximum(page, 0)
        dx = (taken // (2 * CHIPS_Z) + CHIPS_X - at.x) % CHIPS_X
        dz = ((taken // 2) % CHIPS_Z + CHIPS_Z - at.z) % CHIPS_Z
        other = (taken + at.core) % 2
        for stream in range(2):
            held = keyval[other, numbers[(stream * CHIPS_X + dx) * CHIPS_Z + dz]]
            shown = jnp.broadcast_to(page, held.shape) >= 0
            held = jnp.where(shown, held.astype(jnp.float32), 0.0).astype(jnp.bfloat16)
            pages[slot, stream * lines : (stream + 1) * lines] = held.reshape(
                lines, kv_heads, 128
            )
    for copy in y_copies:
        copy.wait_recv()
    for step in range(3):
        own = own + proj_recv[step].astype(jnp.float32)
    resid[...] = own
    mean_sq = jnp.mean(own * own, axis=-1, keepdims=True)
    ffn_in = (own * lax.rsqrt(mean_sq + epsilon) * row_of(ffn_gain)).astype(jnp.bfloat16)
    for stream in range(2):
        rows[stream, :, :width] = ffn_in[stream * half : (stream + 1) * half]

    def experts(lower, upper):
        size = (upper - lower) * half
        gathered = rows[lower:upper].reshape(size, rows.shape[-1])
        wide = lax.broadcasted_iota(jnp.int32, (size, 128), 1)
        named = (wide % 32 == at.seq // 2) & (wide < 64)
        gate_col = jnp.where(named, gathered[:, width:].astype(jnp.float32), 0.0)
        gate_col = jnp.sum(gate_col, axis=1, keepdims=True)
        gathered = gathered[:, :width]
        total = None
        for part in range(2):
            gate_part = jnp.dot(gathered, gate_w[part], preferred_element_type=jnp.float32)
            up_part = jnp.dot(gathered, up_w[part], preferred_element_type=jnp.float32)
            hidden = gate_part / (1.0 + jnp.exp(-gate_part)) * up_part * gate_col
            term = jnp.dot(
                hidden.astype(jnp.bfloat16), down_w[part], preferred_element_type=jnp.float32
            )
            total = term if total is None else total + term
        parts[lower:upper] = total.astype(jnp.bfloat16).reshape(upper - lower, half, width)

    stage = {"done": 0, "weights": False}

    def rows_here(count):
        number = stage["done"]
        if number < len(ROW_GROUPS) and count >= ROW_GROUPS[number]:
            if not stage["weights"]:
                stage["weights"] = True
                for copy in local_copies:
                    copy.wait()
                for copy in twin_copies:
                    copy.wait_recv()
            experts(ROW_GROUPS[number - 1] if number else 0, ROW_GROUPS[number])
            stage["done"] = number + 1

    spread(at, ROWS_TREE, ROWS_ACTS, lambda r: rows.at[r], ag_send, ag_recv, sent, rows_here)

    def add_up(r):
        total = parts[r].astype(jnp.float32)
        for child in CHILDREN[ROWS_TREE][r]:
            total = total + sums[child].astype(jnp.float32)
        return total

    for act in reversed(ROWS_ACTS):
        if act < 0:
            place = sums.at[-act]
            remote(place, place, rs_send.at[-act], rs_recv.at[-act], at.twin()).wait_recv()
            continue
        if CHILDREN[ROWS_TREE][act]:
            parts[act] = add_up(act).astype(jnp.bfloat16)
        copy = remote(
            parts.at[act],
            sums.at[act],
            rs_send.at[act],
            rs_recv.at[act],
            at.chip(*ROWS_TREE[act][3:5]),
        )
        copy.start()
        sent.append(copy)
    for stream in range(2):
        mine = slice(stream * half, (stream + 1) * half)
        out[mine, :] = (resid[mine, :] + add_up(stream)).astype(jnp.bfloat16)
    for copy in y_copies + twin_copies + shared + sent:
        copy.wait_send()


def layer_call(*operands):
    tokens, near_turn, w_keyval, w_query, w_out, w_gate, w_up, w_down = operands[-8:]
    block, width = tokens.shape
    share, half, lines = block // 4, block // 8, block // 2
    piece = w_gate.shape[2]
    kv_heads = w_keyval.shape[1]
    kv_width = kv_heads * 128
    group = w_query.shape[1] // 64 // kv_heads
    smem = pl.BlockSpec(memory_space=pltpu.SMEM)
    vmem = pl.BlockSpec(memory_space=pltpu.VMEM)
    hbm = pl.BlockSpec(memory_space=pl.ANY)
    count = len(ROWS_TREE)
    dma = pltpu.SemaphoreType.DMA
    bf16, f32 = jnp.bfloat16, jnp.float32
    scratch = [
        (tokens.shape, bf16),
        (near_turn.shape, f32),
        (w_keyval.shape, bf16),
        (w_query.shape, bf16),
        (w_out.shape, bf16),
        ((2, width, piece), bf16),
        ((2, width, piece), bf16),
        ((2, piece, width), bf16),
        ((kv_heads, group * block, 128), bf16),
        ((2, count, lines, kv_width), bf16),
        ((kv_heads, 1, group * block), f32),
        ((kv_heads, 80, group * block), f32),
        ((block, width), f32),
        ((block, width), bf16),
        ((3, share, width), bf16),
        ((count, half, width + 128), bf16),
        ((count, half, width), bf16),
        ((count, half, width), bf16),
        ((share, width), f32),
    ]
    sems = [8, 3, 3, count, count, len(KV_SHARES), len(KV_SHARES), 3, 3]
    sems += [count, count, count, count]
    return pl.pallas_call(
        layer_kernel,
        out_shape=(
            jax.ShapeDtypeStruct((share, width), bf16),
            jax.ShapeDtypeStruct((2, block, kv_heads, 128), bf16),
        ),
        in_specs=[smem] * 3 + [vmem] * 5 + [hbm] * 8,
        out_specs=(vmem, vmem),
        scratch_shapes=[pltpu.VMEM(*s) for s in scratch] + [dma((n,)) for n in sems],
        compiler_params=pltpu.CompilerParams(
            collective_id=1, has_side_effects=True, vmem_limit_bytes=56 << 20
        ),
        name="layer",
    )(*operands)


def hand_over(layer_out, pages):
    def kernel(first, second, first_out, second_out, sems):
        copies = [
            pltpu.make_async_copy(first, first_out, sems.at[0]),
            pltpu.make_async_copy(second, second_out, sems.at[1]),
        ]
        for copy in copies:
            copy.start()
        for copy in copies:
            copy.wait()

    hbm = pl.BlockSpec(memory_space=pl.ANY)
    return pl.pallas_call(
        kernel,
        out_shape=tuple(jax.ShapeDtypeStruct(a.shape, a.dtype) for a in (layer_out, pages)),
        in_specs=[hbm] * 2,
        out_specs=(hbm, hbm),
        scratch_shapes=[pltpu.SemaphoreType.DMA((2,))],
        name="hand_over",
    )(layer_out, pages)


def turn_tables(steps, stride):
    inv_freq = rope_base ** (-(np.arange(128) % 32) / 32.0)
    angle = (np.arange(steps) * stride)[:, None] * inv_freq[None, :]
    return np.stack([np.cos(angle), np.sin(angle)]).astype(np.float32)


def body(
    tokens,
    attn_gain,
    w_query,
    w_keyval,
    w_out,
    ffn_gain,
    lengths,
    routes,
    route_gates,
    w_gate,
    w_up,
    w_down,
    page_slot_index,
):
    block = tokens.shape[0]
    numbers = np.zeros(len(KEYVAL_TREE), np.int32)
    for r, (stream, dx, dz) in enumerate(row[:3] for row in KEYVAL_TREE):
        numbers[(stream * CHIPS_X + dx) * CHIPS_Z + dz] = r
    layer_out, pages = layer_call(
        lengths,
        page_slot_index,
        jnp.asarray(numbers),
        attn_gain.reshape(-1, 128),
        ffn_gain.reshape(-1, 128),
        jnp.asarray(turn_tables(2 * CHIPS_X * CHIPS_Z, block)),
        routes.T,
        route_gates.T,
        tokens,
        jnp.asarray(turn_tables(block, 1)),
        w_keyval,
        w_query,
        w_out,
        w_gate,
        w_up,
        w_down,
    )
    return hand_over(layer_out, pages)


def solution(mesh):
    placed = (
        P("seq", None),
        P(),
        P(None, "tp"),
        P(None, "tp", None),
        P("tp", None),
        P(),
        P(),
        P(("seq", "tp"), None),
        P(("seq", "tp"), None),
        P("seq", None, None),
        P("seq", None, None),
        P("seq", None, None),
        P(),
    )
    return jax.shard_map(
        body,
        mesh=mesh,
        in_specs=placed,
        out_specs=(P(("seq", "tp"), None), P("seq", None, "tp", None)),
        check_vma=False,
    )
```

```python
import jax
import jax.numpy as jnp
import numpy as np
from jax import lax
from jax.experimental import pallas as pl
from jax.experimental.pallas import tpu as pltpu
from jax.sharding import PartitionSpec as P

PAGE_TOKENS = 128


epsilon = 1e-05
rope_base = 10000.0

MESH = pl.DeviceIdType.MESH
CHIPS_X = 4
CHIPS_Z = 8

KEYVAL_TREE = (
    (0, 0, 0, 0, 0, -1), (1, 0, 0, 0, 0, -1), (0, 3, 0, 0, -1, 0), (1, 1, 0, 0, 1, 1),
    (1, 0, 2, 1, 2, 1), (0, 1, 0, 0, 1, 0), (1, 3, 0, 0, -1, 1), (1, 0, 5, 1, -3, 1),
    (1, 0, 1, 1, 1, 1), (0, 0, 7, 1, -1, 0), (1, 0, 7, 1, -1, 1), (0, 2, 0, 0, -1, 2),
    (1, 2, 0, 0, 1, 3), (0, 0, 3, 1, 3, 0), (1, 1, 2, 0, 1, 4), (1, 3, 2, 0, -1, 4),
    (1, 1, 1, 0, 1, 8), (1, 3, 5, 0, -1, 7), (0, 0, 5, 1, -3, 0), (0, 3, 2, 1, 2, 2),
    (0, 3, 7, 0, -1, 9), (1, 1, 5, 0, 1, 7), (0, 0, 6, 1, -1, 9), (1, 3, 1, 1, 1, 6),
    (1, 1, 7, 0, 1, 10), (1, 3, 7, 0, -1, 10), (0, 1, 7, 1, -1, 5), (1, 0, 6, 1, 1, 7),
    (0, 1, 3, 0, 1, 13), (0, 3, 3, 0, -1, 13), (1, 1, 3, 1, 1, 14), (1, 2, 2, 0, 1, 14),
    (0, 0, 1, 1, -2, 13), (1, 2, 5, 0, -1, 17), (0, 2, 1, 1, 1, 11), (0, 1, 5, 0, 1, 18),
    (0, 3, 5, 0, -1, 18), (0, 1, 1, 1, 1, 5), (1, 1, 4, 1, -1, 21), (0, 0, 2, 0, 1, 19),
    (0, 3, 6, 0, -1, 22), (1, 2, 1, 1, 1, 12), (1, 1, 6, 0, 1, 27), (1, 3, 3, 1, -2, 17),
    (0, 2, 3, 0, -1, 29), (0, 3, 4, 1, 1, 29), (1, 2, 3, 0, 1, 30), (1, 2, 7, 0, -1, 25),
    (0, 3, 1, 1, -1, 19), (0, 2, 7, 0, 1, 26), (1, 3, 4, 1, 2, 15), (1, 3, 6, 0, -1, 27),
    (0, 1, 4, 1, -1, 35), (0, 2, 5, 0, 1, 35), (1, 0, 4, 0, -1, 38), (0, 1, 2, 1, -1, 28),
    (0, 1, 6, 1, 1, 35), (0, 2, 6, 0, -1, 40), (1, 2, 4, 1, -1, 33), (1, 2, 6, 1, 1, 33),
    (1, 0, 3, 0, 1, 43), (0, 2, 4, 0, -1, 45), (0, 2, 2, 1, 1, 34), (0, 0, 4, 0, 1, 45),
)
KEYVAL_ACTS = (
    -2, -4, -7, -3, -5, -6, -8, -13, -9, -10, -18, 2, 3, -11, -12, 4, -14, -15, -19, 5,
    6, 7, -17, 8, -16, -21, -23, 9, -22, -20, -26, -27, 10, -24, -25, 11, 12, 13, -28, -29,
    -32, 14, 15, -30, -31, -34, 16, 17, -33, 18, -35, 19, -36, -37, -39, 20, 21, -38, -41, -43,
    22, 23, -40, 24, 25, 26, 27, -42, 28, 29, -44, -45, -47, -48, -50, 30, -46, -49, 31, 32,
    -51, 33, 34, 35, -52, -53, 36, -55, -56, 37, 38, -54, 39, 40, -57, -58, -59, 41, 42, 43,
    -60, 44, -62, 45, -61, -63, 46, 47, 48, 49, 50, 51, 52, 53, 54, 55, 56, 57, 58, 59,
    60, 61, 62, 63,
)

ROWS_TREE = (
    (0, 0, 0, 0, 0, -1), (1, 0, 0, 0, 0, -1), (0, 1, 0, 0, 1, 0), (0, 3, 0, 0, -1, 0),
    (1, 0, 1, 1, 1, 1), (1, 0, 6, 1, -2, 1), (1, 1, 0, 0, 1, 1), (1, 3, 0, 0, -1, 1),
    (0, 0, 2, 1, 2, 0), (0, 0, 7, 1, -1, 0), (1, 0, 7, 1, -1, 1), (0, 2, 0, 0, -1, 3),
    (1, 0, 2, 1, 1, 4), (1, 1, 6, 0, 1, 5), (0, 3, 1, 1, 1, 3), (1, 3, 6, 0, -1, 5),
    (0, 1, 6, 1, -2, 2), (1, 2, 0, 0, 1, 6), (0, 1, 1, 1, 1, 2), (0, 3, 7, 0, -1, 9),
    (0, 1, 7, 0, 1, 9), (0, 0, 3, 1, 1, 8), (1, 3, 2, 0, -1, 12), (1, 1, 7, 0, 1, 10),
    (1, 1, 5, 1, -3, 6), (1, 0, 3, 1, 1, 12), (1, 2, 6, 0, -1, 15), (1, 1, 2, 0, 1, 12),
    (0, 3, 2, 1, 1, 14), (0, 0, 1, 0, -1, 18), (0, 2, 1, 0, 1, 18), (0, 1, 5, 1, -1, 16),
    (1, 3, 7, 1, 1, 15), (0, 2, 7, 0, -1, 19), (0, 1, 3, 0, 1, 21), (1, 3, 1, 1, -1, 22),
    (0, 3, 3, 0, -1, 21), (1, 0, 4, 1, 1, 25), (1, 2, 5, 0, 1, 24), (1, 1, 1, 1, -1, 27),
    (1, 1, 3, 1, 1, 27), (1, 3, 3, 0, -1, 25), (0, 2, 5, 0, 1, 31), (0, 0, 5, 0, -1, 31),
    (0, 2, 2, 1, 1, 30), (0, 3, 6, 1, -2, 3), (0, 2, 3, 0, 1, 34), (0, 1, 4, 1, 1, 34),
    (1, 2, 1, 0, -1, 35), (1, 2, 4, 1, -1, 38), (1, 3, 5, 0, 1, 38), (0, 3, 4, 1, 1, 36),
    (1, 0, 5, 0, -1, 24), (1, 2, 3, 0, 1, 40), (0, 2, 4, 1, -1, 42), (1, 1, 4, 1, 1, 40),
    (1, 3, 4, 0, -1, 37), (0, 0, 6, 0, 1, 45), (0, 0, 4, 1, -1, 43), (0, 2, 6, 0, -1, 45),
    (1, 2, 7, 1, 1, 26), (0, 3, 5, 0, 1, 42), (0, 1, 2, 0, -1, 44), (1, 2, 2, 1, 1, 48),
)
ROWS_ACTS = (
    -2, -3, -4, -5, -8, -6, -7, -9, -10, 2, 3, 4, -11, -12, 5, -13, -16, -14, -15, 6,
    7, -17, 8, -18, 9, -19, -20, -24, -21, 10, 11, 12, -22, -23, 13, -25, 14, 15, -26, -27,
    16, 17, -28, 18, 19, -29, -30, -31, 20, -32, -33, 21, -34, 22, -35, 23, -36, 24, 25, -37,
    -38, 26, 27, -39, -40, -41, 28, 29, -45, 30, -44, 31, -43, -42, 32, 33, 34, -46, -47, 35,
    -48, 36, 37, 38, -49, -50, -51, -52, 39, 40, 41, -53, -55, -56, 42, -54, 43, 44, 45, -57,
    -58, -59, -60, 46, 47, 48, -61, -62, -63, 49, 50, 51, 52, 53, 54, 55, 56, 57, 58, 59,
    60, 61, 62, 63,
)

CHILDREN = {
    tree: [[c for c in range(len(tree)) if tree[c][5] == r] for r in range(len(tree))]
    for tree in (KEYVAL_TREE, ROWS_TREE)
}


class Place:
    def __init__(self):
        self.seq = lax.axis_index("seq")
        self.tp = lax.axis_index("tp")
        self.x = self.seq // (2 * CHIPS_Z)
        self.z = (self.seq // 2) % CHIPS_Z
        self.core = self.seq % 2

    def xs(self, dx):
        return lax.rem(self.x + dx + CHIPS_X, CHIPS_X)

    def zs(self, dz):
        return lax.rem(self.z + dz + CHIPS_Z, CHIPS_Z)

    def chip(self, axis, step):
        if axis == 0:
            return ((self.xs(step) * CHIPS_Z + self.z) * 2 + self.core, self.tp)
        return ((self.x * CHIPS_Z + self.zs(step)) * 2 + self.core, self.tp)

    def twin(self):
        return ((self.x * CHIPS_Z + self.z) * 2 + 1 - self.core, self.tp)

    def row(self, step):
        return (self.seq, lax.rem(self.tp + step + 4, 4))


def remote(src, dst, send_sem, recv_sem, device):
    return pltpu.make_async_remote_copy(
        src_ref=src,
        dst_ref=dst,
        send_sem=send_sem,
        recv_sem=recv_sem,
        device_id=device,
        device_id_type=MESH,
    )


def greet(at):
    steps = set()
    for tree in (KEYVAL_TREE, ROWS_TREE):
        for row in tree:
            if row[5] >= 0:
                size = CHIPS_Z if row[3] else CHIPS_X
                steps |= {(row[3], row[4] % size), (row[3], -row[4] % size)}
    partners = [at.chip(*s) for s in sorted(steps)]
    partners += [at.twin()] + [at.row(d) for d in (1, 2, 3)]
    barrier = pltpu.get_barrier_semaphore()
    for partner in partners:
        pl.semaphore_signal(barrier, inc=1, device_id=partner, device_id_type=MESH)
    return lambda: pl.semaphore_wait(barrier, len(partners))


def spread(at, tree, acts, spot, send_sem, recv_sem, own_piece, arrived):
    filled, count = 0, 2
    for i, act in enumerate(first_stream_first(tree, acts)):
        if act < 0:
            axis, step, parent = tree[-act][3:]
            if filled <= parent < 2:
                own_piece(parent)
                filled = parent + 1
            remote(
                spot(parent), spot(-act), send_sem, recv_sem.at[-act], at.chip(axis, -step)
            ).start()
        else:
            remote(
                spot(act), spot(act), send_sem, recv_sem.at[act], at.chip(*tree[act][3:5])
            ).wait_recv()
            count = act + 1
        if i + 1 == len(acts) or acts[i + 1] > 0:
            arrived(count)


def first_stream_first(tree, acts):
    opening = next(i for i, act in enumerate(acts) if act > 0)
    assert {tree[-act][5] for act in acts[:opening]} == {0, 1}
    return sorted(acts[:opening], key=lambda act: tree[-act][5]) + list(acts[opening:])


KV_SHARES = (8, 16, 24, 32, 40, 48, 56, 60, 64)
ROW_GROUPS = (8, 16, 24, 32, 40, 48, 56, 64)


def layer_kernel(
    lengths,
    page_slots,
    numbers,
    attn_gain,
    ffn_gain,
    far_turn,
    routes,
    route_gates,
    tokens_in,
    near_turn_in,
    w_keyval_in,
    w_query,
    w_out,
    w_gate,
    w_up,
    w_down,
    out,
    pages,
    tokens,
    near_turn,
    w_keyval,
    query_w,
    out_w,
    gate_w,
    up_w,
    down_w,
    queries,
    keyval,
    best,
    weighted,
    projected,
    proj_send,
    proj_recv,
    rows,
    parts,
    sums,
    resid,
    w_local,
    w_send,
    w_recv,
    kv_send,
    kv_recv,
    tw_send,
    tw_recv,
    y_send,
    y_recv,
    ag_send,
    ag_recv,
    rs_send,
    rs_recv,
):
    at = Place()
    all_here = greet(at)
    early = [
        pltpu.make_async_copy(source, held, w_local.at[5 + i])
        for i, (source, held) in enumerate(
            ((tokens_in, tokens), (w_keyval_in, w_keyval), (near_turn_in, near_turn))
        )
    ]
    for copy in early:
        copy.start()
    width = tokens.shape[1]
    block = tokens.shape[0]
    share = block // 4
    half = share // 2
    lines = block // 2
    kv_heads = w_keyval.shape[1]
    query_copy = pltpu.make_async_copy(w_query, query_w, w_local.at[3])
    out_copy = pltpu.make_async_copy(w_out, out_w, w_local.at[4])
    query_copy.start()
    out_copy.start()

    def row_of(gain):
        return jnp.concatenate([gain[i : i + 1, :] for i in range(gain.shape[0])], axis=1)

    early[0].wait()
    inputs = tokens[...].astype(jnp.float32)
    mean_sq = jnp.mean(inputs * inputs, axis=-1, keepdims=True)
    normed = (inputs * lax.rsqrt(mean_sq + epsilon) * row_of(attn_gain)).astype(jnp.bfloat16)
    early[1].wait()
    keyval_w = w_keyval[...].reshape(width, kv_heads * 128)
    key_value_rows = jnp.dot(normed, keyval_w, preferred_element_type=jnp.float32)

    line = lax.broadcasted_iota(jnp.int32, (block, 128), 0)
    lane = lax.broadcasted_iota(jnp.int32, (block, 128), 1)
    low = lane % 64 < 32
    cos_all = jnp.zeros((block, 128), jnp.float32)
    sin_all = jnp.zeros((block, 128), jnp.float32)
    early[2].wait()
    near_cos, near_sin = near_turn[0], near_turn[1]
    edge = jnp.int32(0)
    for d in range(lengths.shape[0]):
        base = at.seq * block - edge
        away = jnp.maximum(base, -base)
        tens, ones = pl.ds(away // block, 1), pl.ds(away % block, 1)
        cos_far, sin_far = far_turn[0, tens, :], far_turn[1, tens, :]
        cos_one, sin_one = near_turn[0, ones, :], near_turn[1, ones, :]
        cos_base = cos_far * cos_one - sin_far * sin_one
        sin_base = (sin_far * cos_one + cos_far * sin_one) * jnp.where(base < 0, -1.0, 1.0)
        inside = line + base >= 0
        cos_all = jnp.where(inside, cos_base * near_cos - sin_base * near_sin, cos_all)
        sin_all = jnp.where(inside, sin_base * near_cos + cos_base * near_sin, sin_all)
        edge = edge + lengths[d]
    sin_all = jnp.where(low, -sin_all, sin_all)

    def turn(values, cos_part, sin_part):
        swapped = jnp.where(low, pltpu.roll(values, 96, 1), pltpu.roll(values, 32, 1))
        return values * cos_part + swapped * sin_part

    cos_kv, sin_kv = jnp.where(lane < 64, cos_all, 1.0), jnp.where(lane < 64, sin_all, 0.0)
    for head in range(kv_heads):
        columns = slice(head * 128, (head + 1) * 128)
        turned = turn(key_value_rows[:, columns], cos_kv, sin_kv).astype(jnp.bfloat16)
        for stream in range(2):
            keyval[0, stream, :, columns] = turned[stream * lines : (stream + 1) * lines]
    all_here()

    shared = []
    weights = ((w_gate, gate_w), (w_up, up_w), (w_down, down_w))
    local_copies, twin_copies = [], []
    for i, (source, held) in enumerate(weights):
        local_copies.append(pltpu.make_async_copy(source.at[0], held.at[0], w_local.at[i]))
        twin_copies.append(
            remote(source.at[0], held.at[1], w_send.at[i], w_recv.at[i], at.twin())
        )

    token = at.seq * block + lax.broadcasted_iota(jnp.int32, (1, block), 1)
    begin = jnp.zeros((1, block), jnp.int32)
    edge = lengths[0]
    for d in range(1, lengths.shape[0]):
        begin = jnp.where(token >= edge, edge, begin)
        edge = edge + lengths[d]
    group = w_query.shape[1] // 64 // kv_heads

    def attend(number, other):
        lower, upper = share_range(number)
        if other:
            place = keyval.at[1, lower:upper]
            remote(place, place, tw_send.at[number], tw_recv.at[number], at.twin()).wait_recv()
        core = 1 - at.core if other else at.core
        count_keys = (upper - lower) * lines
        key_row = lax.broadcasted_iota(jnp.int32, (count_keys, 1), 0)
        key = jnp.zeros((count_keys, 1), jnp.int32)
        for i in range(upper - lower):
            stream, dx, dz = KEYVAL_TREE[lower + i][:3]
            start = ((at.xs(dx) * CHIPS_Z + at.zs(dz)) * 2 + core) * block + stream * lines
            key = jnp.where(key_row >= i * lines, start + key_row - i * lines, key)
        bundle = keyval[other, lower:upper].reshape(count_keys, 128 * kv_heads)
        turned = bundle.T
        bias = jnp.where((key <= token) & (key >= begin), 0.0, -1e30)
        bias = jnp.concatenate([bias] * group, axis=1)
        for head in range(kv_heads):
            scores = lax.dot_general(
                bundle[:, head * 128 : (head + 1) * 128],
                queries[head],
                (((1,), (1,)), ((), ())),
                preferred_element_type=jnp.float32,
            )
            scores = scores + bias
            old = best[head]
            new = jnp.maximum(old, jnp.max(scores, axis=0, keepdims=True))
            expd = jnp.exp2(scores - new)
            fade = jnp.exp2(old - new)
            best[head] = new
            values = turned[head * 128 + 64 : (head + 1) * 128]
            values = jnp.concatenate([values, jnp.ones((16, count_keys), jnp.bfloat16)], axis=0)
            fresh = jnp.dot(values, expd.astype(jnp.bfloat16), preferred_element_type=jnp.float32)
            weighted[head] = weighted[head] * fade + fresh

    progress = {"done": 0, "started": False}
    waiting = []

    def share_range(number):
        return (KV_SHARES[number - 1] if number else 0), KV_SHARES[number]

    def start_up():
        for copy in local_copies + twin_copies:
            copy.start()
        query_copy.wait()
        scale = 64**-0.5 * 1.4426950408889634
        query_rows = jnp.dot(normed, query_w[...], preferred_element_type=jnp.float32)
        for pair in range(query_rows.shape[1] // 128):
            turned = turn(query_rows[:, pair * 128 : (pair + 1) * 128], cos_all, sin_all) * scale
            for odd in range(2):
                head = 2 * pair + odd
                placed = pltpu.roll(turned, 64, 1) if odd else turned
                placed = jnp.where(lane < 64, placed, 0.0).astype(jnp.bfloat16)
                lower = (head % group) * block
                queries[head // group, lower : lower + block, :] = placed
        best[...] = jnp.full_like(best, -1e30)
        weighted[...] = jnp.zeros_like(weighted)

    def keys_here(count):
        if not progress["started"]:
            progress["started"] = True
            start_up()
        number = progress["done"]
        if number < len(KV_SHARES) and count >= KV_SHARES[number]:
            lower, upper = share_range(number)
            copy = remote(
                keyval.at[0, lower:upper],
                keyval.at[1, lower:upper],
                tw_send.at[number],
                tw_recv.at[number],
                at.twin(),
            )
            copy.start()
            shared.append(copy)
            if number:
                waiting.append((number - 1, 1))
            waiting.append((number, 0))
            progress["done"] = number + 1
        if waiting:
            attend(*waiting.pop(0))

    spread(
        at,
        KEYVAL_TREE,
        KEYVAL_ACTS,
        lambda r: keyval.at[0, r],
        kv_send.at[0],
        kv_recv,
        lambda r: None,
        keys_here,
    )
    for unit in waiting + [(len(KV_SHARES) - 1, 1)]:
        attend(*unit)

    columns = []
    for head in range(kv_heads):
        mean = weighted[head, :64] / weighted[head, 64:65]
        for g in range(group):
            columns.append(mean[:, g * block : (g + 1) * block])
    attended = jnp.concatenate(columns, axis=0).T.astype(jnp.bfloat16)

    out_copy.wait()
    projected[...] = jnp.dot(attended, out_w[...], preferred_element_type=jnp.float32)
    proj_send[...] = projected[...].astype(jnp.bfloat16)
    y_copies = [[], []]
    for stream in range(2):
        for step in (2, 1, 3):
            start = at.row(step)[1] * share + stream * half
            copy = remote(
                proj_send.at[pl.ds(pl.multiple_of(start, half), half)],
                proj_recv.at[stream, step - 1],
                y_send.at[stream, step - 1],
                y_recv.at[stream, step - 1],
                at.row(step),
            )
            copy.start()
            y_copies[stream].append(copy)
    expert = lax.broadcasted_iota(jnp.int32, (128, share), 0)
    table = jnp.zeros((128, share), jnp.float32)
    for k in range(routes.shape[0]):
        chosen = expert % 32 == routes[k : k + 1, :]
        table = table + jnp.where(chosen, route_gates[k : k + 1, :], 0.0)
    rounded = table.astype(jnp.bfloat16).astype(jnp.float32)
    table = jnp.where(expert < 32, rounded, table - rounded).T.astype(jnp.bfloat16)
    for stream in range(2):
        rows[stream, :, width:] = table[stream * half : (stream + 1) * half]
    for slot in range(pages.shape[0]):
        wanted = at.seq * pages.shape[0] + slot

        def look(n, found):
            return jnp.where(page_slots[n] == wanted, n, found)

        page = lax.fori_loop(0, page_slots.shape[0], look, jnp.int32(-1), unroll=8)
        taken = jnp.maximum(page, 0)
        dx = (taken // (2 * CHIPS_Z) + CHIPS_X - at.x) % CHIPS_X
        dz = ((taken // 2) % CHIPS_Z + CHIPS_Z - at.z) % CHIPS_Z
        other = (taken + at.core) % 2
        for stream in range(2):
            held = keyval[other, numbers[(stream * CHIPS_X + dx) * CHIPS_Z + dz]]
            shown = jnp.broadcast_to(page, held.shape) >= 0
            held = jnp.where(shown, held.astype(jnp.float32), 0.0).astype(jnp.bfloat16)
            pages[slot, stream * lines : (stream + 1) * lines] = held.reshape(
                lines, kv_heads, 128
            )
    def own_rows(stream):
        start = pl.multiple_of(at.tp * share + stream * half, half)
        own = projected[pl.ds(start, half), :] + tokens[pl.ds(start, half), :].astype(jnp.float32)
        for copy in y_copies[stream]:
            copy.wait_recv()
        for step in range(3):
            own = own + proj_recv[stream, step].astype(jnp.float32)
        resid[stream] = own
        mean_sq = jnp.mean(own * own, axis=-1, keepdims=True)
        ffn_in = own * lax.rsqrt(mean_sq + epsilon) * row_of(ffn_gain)
        rows[stream, :, :width] = ffn_in.astype(jnp.bfloat16)

    def experts(lower, upper):
        size = (upper - lower) * half
        gathered = rows[lower:upper].reshape(size, rows.shape[-1])
        wide = lax.broadcasted_iota(jnp.int32, (size, 128), 1)
        named = (wide % 32 == at.seq // 2) & (wide < 64)
        gate_col = jnp.where(named, gathered[:, width:].astype(jnp.float32), 0.0)
        gate_col = jnp.sum(gate_col, axis=1, keepdims=True)
        gathered = gathered[:, :width]
        total = None
        for part in range(2):
            gate_part = jnp.dot(gathered, gate_w[part], preferred_element_type=jnp.float32)
            up_part = jnp.dot(gathered, up_w[part], preferred_element_type=jnp.float32)
            hidden = gate_part / (1.0 + jnp.exp(-gate_part)) * up_part * gate_col
            term = jnp.dot(
                hidden.astype(jnp.bfloat16), down_w[part], preferred_element_type=jnp.float32
            )
            total = term if total is None else total + term
        parts[lower:upper] = total.astype(jnp.bfloat16).reshape(upper - lower, half, width)

    stage = {"done": 0, "weights": False}

    def rows_here(count):
        number = stage["done"]
        if number < len(ROW_GROUPS) and count >= ROW_GROUPS[number]:
            if not stage["weights"]:
                stage["weights"] = True
                for copy in local_copies:
                    copy.wait()
                for copy in twin_copies:
                    copy.wait_recv()
            experts(ROW_GROUPS[number - 1] if number else 0, ROW_GROUPS[number])
            stage["done"] = number + 1

    spread(
        at,
        ROWS_TREE,
        ROWS_ACTS,
        lambda r: rows.at[r],
        ag_send.at[0],
        ag_recv,
        own_rows,
        rows_here,
    )

    def add_up(r):
        total = parts[r].astype(jnp.float32)
        for child in CHILDREN[ROWS_TREE][r]:
            total = total + sums[child].astype(jnp.float32)
        return total

    for act in reversed(first_stream_first(ROWS_TREE, ROWS_ACTS)):
        if act < 0:
            place = sums.at[-act]
            remote(place, place, rs_send.at[0], rs_recv.at[-act], at.twin()).wait_recv()
            continue
        if CHILDREN[ROWS_TREE][act]:
            parts[act] = add_up(act).astype(jnp.bfloat16)
        remote(
            parts.at[act],
            sums.at[act],
            rs_send.at[0],
            rs_recv.at[act],
            at.chip(*ROWS_TREE[act][3:5]),
        ).start()
    for stream in range(2):
        mine = slice(stream * half, (stream + 1) * half)
        out[mine, :] = (resid[stream] + add_up(stream)).astype(jnp.bfloat16)
    for copy in y_copies[0] + y_copies[1] + twin_copies + shared:
        copy.wait_send()
    for held, send_sem in (
        (keyval.at[0, 2:], kv_send),
        (rows.at[2:], ag_send),
        (parts.at[2:], rs_send),
    ):
        remote(held, held, send_sem.at[0], send_sem.at[0], at.twin()).wait_send()


def layer_call(*operands):
    tokens, near_turn, w_keyval, w_query, w_out, w_gate, w_up, w_down = operands[-8:]
    block, width = tokens.shape
    share, half, lines = block // 4, block // 8, block // 2
    piece = w_gate.shape[2]
    kv_heads = w_keyval.shape[1]
    kv_width = kv_heads * 128
    group = w_query.shape[1] // 64 // kv_heads
    smem = pl.BlockSpec(memory_space=pltpu.SMEM)
    vmem = pl.BlockSpec(memory_space=pltpu.VMEM)
    hbm = pl.BlockSpec(memory_space=pl.ANY)
    count = len(ROWS_TREE)
    dma = pltpu.SemaphoreType.DMA
    bf16, f32 = jnp.bfloat16, jnp.float32
    scratch = [
        (tokens.shape, bf16),
        (near_turn.shape, f32),
        (w_keyval.shape, bf16),
        (w_query.shape, bf16),
        (w_out.shape, bf16),
        ((2, width, piece), bf16),
        ((2, width, piece), bf16),
        ((2, piece, width), bf16),
        ((kv_heads, group * block, 128), bf16),
        ((2, count, lines, kv_width), bf16),
        ((kv_heads, 1, group * block), f32),
        ((kv_heads, 80, group * block), f32),
        ((block, width), f32),
        ((block, width), bf16),
        ((2, 3, half, width), bf16),
        ((count, half, width + 128), bf16),
        ((count, half, width), bf16),
        ((count, half, width), bf16),
        ((2, half, width), f32),
    ]
    sems = [(8,), (3,), (3,), (1,), (count,), (len(KV_SHARES),), (len(KV_SHARES),), (2, 3), (2, 3)]
    sems += [(1,), (count,), (1,), (count,)]
    return pl.pallas_call(
        layer_kernel,
        out_shape=(
            jax.ShapeDtypeStruct((share, width), bf16),
            jax.ShapeDtypeStruct((2, block, kv_heads, 128), bf16),
        ),
        in_specs=[smem] * 3 + [vmem] * 5 + [hbm] * 8,
        out_specs=(vmem, vmem),
        scratch_shapes=[pltpu.VMEM(*s) for s in scratch] + [dma(shape) for shape in sems],
        compiler_params=pltpu.CompilerParams(
            collective_id=1, has_side_effects=True, vmem_limit_bytes=56 << 20
        ),
        name="layer",
    )(*operands)


def hand_over(layer_out, pages):
    def kernel(first, second, first_out, second_out, first_held, second_held, sems):
        ins = [
            pltpu.make_async_copy(first, first_held, sems.at[0]),
            pltpu.make_async_copy(second, second_held, sems.at[1]),
        ]
        outs = [
            pltpu.make_async_copy(first_held, first_out, sems.at[2]),
            pltpu.make_async_copy(second_held, second_out, sems.at[3]),
        ]
        for copy in ins:
            copy.start()
        for came, copy in zip(ins, outs):
            came.wait()
            copy.start()
        for copy in outs:
            copy.wait()

    hbm = pl.BlockSpec(memory_space=pl.ANY)
    return pl.pallas_call(
        kernel,
        out_shape=tuple(jax.ShapeDtypeStruct(a.shape, a.dtype) for a in (layer_out, pages)),
        in_specs=[hbm] * 2,
        out_specs=(hbm, hbm),
        scratch_shapes=[pltpu.VMEM(a.shape, a.dtype) for a in (layer_out, pages)]
        + [pltpu.SemaphoreType.DMA((4,))],
        name="hand_over",
    )(layer_out, pages)


def turn_tables(steps, stride):
    inv_freq = rope_base ** (-(np.arange(128) % 32) / 32.0)
    angle = (np.arange(steps) * stride)[:, None] * inv_freq[None, :]
    return np.stack([np.cos(angle), np.sin(angle)]).astype(np.float32)


def body(
    tokens,
    attn_gain,
    w_query,
    w_keyval,
    w_out,
    ffn_gain,
    lengths,
    routes,
    route_gates,
    w_gate,
    w_up,
    w_down,
    page_slot_index,
):
    block = tokens.shape[0]
    numbers = np.zeros(len(KEYVAL_TREE), np.int32)
    for r, (stream, dx, dz) in enumerate(row[:3] for row in KEYVAL_TREE):
        numbers[(stream * CHIPS_X + dx) * CHIPS_Z + dz] = r
    layer_out, pages = layer_call(
        lengths,
        page_slot_index,
        jnp.asarray(numbers),
        attn_gain.reshape(-1, 128),
        ffn_gain.reshape(-1, 128),
        jnp.asarray(turn_tables(2 * CHIPS_X * CHIPS_Z, block)),
        routes.T,
        route_gates.T,
        tokens,
        jnp.asarray(turn_tables(block, 1)),
        w_keyval,
        w_query,
        w_out,
        w_gate,
        w_up,
        w_down,
    )
    return hand_over(layer_out, pages)


def solution(mesh):
    placed = (
        P("seq", None),
        P(),
        P(None, "tp"),
        P(None, "tp", None),
        P("tp", None),
        P(),
        P(),
        P(("seq", "tp"), None),
        P(("seq", "tp"), None),
        P("seq", None, None),
        P("seq", None, None),
        P("seq", None, None),
        P(),
    )
    return jax.shard_map(
        body,
        mesh=mesh,
        in_specs=placed,
        out_specs=(P(("seq", "tp"), None), P("seq", None, "tp", None)),
        check_vma=False,
    )
```

```python
import jax
import jax.numpy as jnp
import numpy as np
from jax import lax
from jax.experimental import pallas as pl
from jax.experimental.pallas import tpu as pltpu
from jax.sharding import PartitionSpec as P

PAGE_TOKENS = 128


epsilon = 1e-05
rope_base = 10000.0

MESH = pl.DeviceIdType.MESH
CHIPS_X = 4
CHIPS_Z = 8

KEYVAL_TREE = (
    (0, 0, 0, 0, 0, -1), (1, 0, 0, 0, 0, -1), (0, 3, 0, 0, -1, 0), (1, 1, 0, 0, 1, 1),
    (1, 0, 2, 1, 2, 1), (0, 1, 0, 0, 1, 0), (1, 3, 0, 0, -1, 1), (1, 0, 5, 1, -3, 1),
    (1, 0, 1, 1, 1, 1), (0, 0, 7, 1, -1, 0), (1, 0, 7, 1, -1, 1), (0, 2, 0, 0, -1, 2),
    (1, 2, 0, 0, 1, 3), (0, 0, 3, 1, 3, 0), (1, 1, 2, 0, 1, 4), (1, 3, 2, 0, -1, 4),
    (1, 1, 1, 0, 1, 8), (1, 3, 5, 0, -1, 7), (0, 0, 5, 1, -3, 0), (0, 3, 2, 1, 2, 2),
    (0, 3, 7, 0, -1, 9), (1, 1, 5, 0, 1, 7), (0, 0, 6, 1, -1, 9), (1, 3, 1, 1, 1, 6),
    (1, 1, 7, 0, 1, 10), (1, 3, 7, 0, -1, 10), (0, 1, 7, 1, -1, 5), (1, 0, 6, 1, 1, 7),
    (0, 1, 3, 0, 1, 13), (0, 3, 3, 0, -1, 13), (1, 1, 3, 1, 1, 14), (1, 2, 2, 0, 1, 14),
    (0, 0, 1, 1, -2, 13), (1, 2, 5, 0, -1, 17), (0, 2, 1, 1, 1, 11), (0, 1, 5, 0, 1, 18),
    (0, 3, 5, 0, -1, 18), (0, 1, 1, 1, 1, 5), (1, 1, 4, 1, -1, 21), (0, 0, 2, 0, 1, 19),
    (0, 3, 6, 0, -1, 22), (1, 2, 1, 1, 1, 12), (1, 1, 6, 0, 1, 27), (1, 3, 3, 1, -2, 17),
    (0, 2, 3, 0, -1, 29), (0, 3, 4, 1, 1, 29), (1, 2, 3, 0, 1, 30), (1, 2, 7, 0, -1, 25),
    (0, 3, 1, 1, -1, 19), (0, 2, 7, 0, 1, 26), (1, 3, 4, 1, 2, 15), (1, 3, 6, 0, -1, 27),
    (0, 1, 4, 1, -1, 35), (0, 2, 5, 0, 1, 35), (1, 0, 4, 0, -1, 38), (0, 1, 2, 1, -1, 28),
    (0, 1, 6, 1, 1, 35), (0, 2, 6, 0, -1, 40), (1, 2, 4, 1, -1, 33), (1, 2, 6, 1, 1, 33),
    (1, 0, 3, 0, 1, 43), (0, 2, 4, 0, -1, 45), (0, 2, 2, 1, 1, 34), (0, 0, 4, 0, 1, 45),
)
KEYVAL_ACTS = (
    -2, -4, -7, -3, -5, -6, -8, -13, -9, -10, -18, 2, 3, -11, -12, 4, -14, -15, -19, 5,
    6, 7, -17, 8, -16, -21, -23, 9, -22, -20, -26, -27, 10, -24, -25, 11, 12, 13, -28, -29,
    -32, 14, 15, -30, -31, -34, 16, 17, -33, 18, -35, 19, -36, -37, -39, 20, 21, -38, -41, -43,
    22, 23, -40, 24, 25, 26, 27, -42, 28, 29, -44, -45, -47, -48, -50, 30, -46, -49, 31, 32,
    -51, 33, 34, 35, -52, -53, 36, -55, -56, 37, 38, -54, 39, 40, -57, -58, -59, 41, 42, 43,
    -60, 44, -62, 45, -61, -63, 46, 47, 48, 49, 50, 51, 52, 53, 54, 55, 56, 57, 58, 59,
    60, 61, 62, 63,
)

ROWS_TREE = (
    (0, 0, 0, 0, 0, -1), (1, 0, 0, 0, 0, -1), (0, 1, 0, 0, 1, 0), (1, 3, 0, 0, -1, 1),
    (0, 0, 2, 1, 2, 0), (1, 0, 6, 1, -2, 1), (1, 1, 0, 0, 1, 1), (0, 3, 0, 0, -1, 0),
    (1, 0, 1, 1, 1, 1), (0, 0, 7, 1, -1, 0), (0, 1, 1, 1, 1, 2), (1, 2, 0, 0, -1, 3),
    (0, 1, 2, 0, 1, 4), (0, 1, 5, 1, -3, 2), (1, 0, 7, 1, 1, 5), (1, 3, 6, 0, -1, 5),
    (1, 1, 6, 0, 1, 5), (1, 3, 1, 0, -1, 8), (1, 0, 3, 1, 2, 8), (1, 1, 1, 0, 1, 8),
    (1, 1, 7, 1, -1, 6), (0, 3, 7, 0, -1, 9), (0, 1, 7, 0, 1, 9), (1, 0, 2, 1, 1, 8),
    (0, 0, 1, 1, -1, 4), (0, 3, 2, 0, -1, 4), (0, 2, 5, 0, 1, 13), (0, 0, 3, 1, 1, 4),
    (1, 3, 7, 0, -1, 14), (0, 1, 4, 1, -1, 13), (1, 2, 6, 0, 1, 16), (0, 3, 1, 1, 1, 7),
    (1, 2, 1, 0, -1, 17), (1, 1, 5, 1, -1, 16), (1, 1, 3, 0, 1, 18), (0, 0, 5, 0, -1, 13),
    (0, 3, 6, 1, -1, 21), (0, 2, 7, 0, 1, 22), (1, 0, 5, 1, 2, 18), (0, 2, 2, 0, -1, 25),
    (1, 3, 5, 1, -1, 15), (0, 3, 5, 0, 1, 26), (0, 1, 6, 1, 1, 13), (1, 2, 7, 0, -1, 28),
    (1, 2, 5, 1, -1, 30), (0, 2, 4, 0, 1, 29), (0, 3, 3, 1, 1, 25), (0, 2, 1, 0, -1, 31),
    (1, 1, 4, 1, -1, 33), (1, 1, 2, 0, 1, 23), (0, 0, 6, 1, 1, 35), (0, 2, 6, 0, -1, 36),
    (0, 0, 4, 1, -1, 35), (1, 2, 3, 0, 1, 34), (0, 2, 3, 1, 1, 39), (1, 3, 2, 0, -1, 23),
    (1, 3, 4, 1, -1, 40), (1, 0, 4, 1, 1, 18), (1, 3, 3, 0, -1, 18), (0, 1, 3, 1, -1, 29),
    (1, 2, 4, 0, 1, 48), (0, 3, 4, 1, 1, 46), (0, 2, 0, 1, -1, 47), (1, 2, 2, 0, 1, 49),
)
ROWS_STEPS = (
    4, 2, 7, 9, 5, 3, 6, 8, 66, 67, 10, 13, 11, 68, 69, 12, 14, 15, 70, 71,
    128, 16, 72, 73, 18, 17, 19, 20, 21, 22, 74, 75, 23, 24, 25, 76, 77, 26, 78, 79,
    129, 27, 28, 29, 80, 30, 81, 31, 32, 33, 82, 83, 34, 84, 85, 38, 35, 36, 86, 37,
    87, 88, 89, 130, 39, 40, 90, 41, 91, 92, 93, 42, 43, 94, 44, 45, 95, 96, 97, 131,
    46, 47, 48, 98, 49, 99, 100, 50, 51, 52, 101, 102, 53, 103, 104, 132, 54, 55, 56, 105,
    224, 106, 107, 108, 57, 58, 59, 109, 110, 111, 112, 133, 60, 61, 211, 62, 113, 63, 114, 115,
    116, 237, 236, 234, 117, 203, 118, 119, 120, 134, 233, 216, 219, 288, 209, 121, 122, 123, 245, 244,
    242, 124, 247, 275, 125, 126, 229, 212, 246, 127, 135, 235, 301, 300, 298, 252, 248, 253, 267, 250,
    297, 280, 283, 222, 254, 249, 273, 243, 309, 308, 306, 226, 251, 202, 311, 227, 293, 276, 310, 255,
    230, 299, 231, 316, 240, 312, 317, 214, 314, 232, 220, 286, 318, 313, 198, 238, 307, 228, 239, 290,
    315, 266, 218, 291, 221, 195, 319, 241, 304, 295, 225, 294, 210, 278, 204, 296, 207, 284, 262, 302,
    217, 292, 303, 223, 282, 213, 206, 285, 205, 259, 305, 215, 289, 208, 274, 271, 268, 281, 196, 287,
    199, 277, 201, 270, 272, 197, 269, 194, 279, 200, 263, 260, 265, 258, 264, 261,
)

SEND, WAIT, EXPERTS, SEND_SUM, WAIT_SUM = range(5)
CHILDREN = [[c for c in range(64) if ROWS_TREE[c][5] == r] for r in range(64)]


class Place:
    def __init__(self):
        self.seq = lax.axis_index("seq")
        self.tp = lax.axis_index("tp")
        self.x = self.seq // (2 * CHIPS_Z)
        self.z = (self.seq // 2) % CHIPS_Z
        self.core = self.seq % 2

    def xs(self, dx):
        return lax.rem(self.x + dx + CHIPS_X, CHIPS_X)

    def zs(self, dz):
        return lax.rem(self.z + dz + CHIPS_Z, CHIPS_Z)

    def chip(self, axis, step):
        if axis == 0:
            return ((self.xs(step) * CHIPS_Z + self.z) * 2 + self.core, self.tp)
        return ((self.x * CHIPS_Z + self.zs(step)) * 2 + self.core, self.tp)

    def twin(self):
        return ((self.x * CHIPS_Z + self.z) * 2 + 1 - self.core, self.tp)

    def row(self, step):
        return (self.seq, lax.rem(self.tp + step + 4, 4))


def remote(src, dst, send_sem, recv_sem, device):
    return pltpu.make_async_remote_copy(
        src_ref=src,
        dst_ref=dst,
        send_sem=send_sem,
        recv_sem=recv_sem,
        device_id=device,
        device_id_type=MESH,
    )


def greet(at):
    steps = set()
    for tree in (KEYVAL_TREE, ROWS_TREE):
        for row in tree:
            if row[5] >= 0:
                size = CHIPS_Z if row[3] else CHIPS_X
                steps |= {(row[3], row[4] % size), (row[3], -row[4] % size)}
    partners = [at.chip(*s) for s in sorted(steps)]
    partners += [at.twin()] + [at.row(d) for d in (1, 2, 3)]
    barrier = pltpu.get_barrier_semaphore()
    for partner in partners:
        pl.semaphore_signal(barrier, inc=1, device_id=partner, device_id_type=MESH)
    return lambda: pl.semaphore_wait(barrier, len(partners))


def spread(at, tree, acts, spot, send_sem, recv_sem, own_piece, arrived):
    filled, count = 0, 2
    for i, act in enumerate(first_stream_first(tree, acts)):
        if act < 0:
            axis, step, parent = tree[-act][3:]
            if filled <= parent < 2:
                own_piece(parent)
                filled = parent + 1
            remote(
                spot(parent), spot(-act), send_sem, recv_sem.at[-act], at.chip(axis, -step)
            ).start()
        else:
            remote(
                spot(act), spot(act), send_sem, recv_sem.at[act], at.chip(*tree[act][3:5])
            ).wait_recv()
            count = act + 1
        if i + 1 == len(acts) or acts[i + 1] > 0:
            arrived(count)


def first_stream_first(tree, acts):
    opening = next(i for i, act in enumerate(acts) if act > 0)
    assert {tree[-act][5] for act in acts[:opening]} == {0, 1}
    return sorted(acts[:opening], key=lambda act: tree[-act][5]) + list(acts[opening:])


KV_SHARES = (8, 24, 40, 56, 64)
ROW_GROUP = 8


def layer_kernel(
    lengths,
    page_slots,
    numbers,
    attn_gain,
    ffn_gain,
    far_turn,
    routes,
    route_gates,
    tokens_in,
    near_turn_in,
    w_keyval_in,
    w_query,
    w_out,
    w_gate,
    w_up,
    w_down,
    out,
    pages,
    tokens,
    near_turn,
    w_keyval,
    query_w,
    out_w,
    gate_w,
    up_w,
    down_w,
    queries,
    keyval,
    best,
    weighted,
    projected,
    proj_send,
    proj_recv,
    rows,
    parts,
    sums,
    resid,
    w_local,
    w_send,
    w_recv,
    kv_send,
    kv_recv,
    tw_send,
    tw_recv,
    y_send,
    y_recv,
    ag_send,
    ag_recv,
    rs_send,
    rs_recv,
):
    at = Place()
    all_here = greet(at)
    early = [
        pltpu.make_async_copy(source, held, w_local.at[5 + i])
        for i, (source, held) in enumerate(
            ((tokens_in, tokens), (w_keyval_in, w_keyval), (near_turn_in, near_turn))
        )
    ]
    for copy in early:
        copy.start()
    width = tokens.shape[1]
    block = tokens.shape[0]
    share = block // 4
    half = share // 2
    lines = block // 2
    kv_heads = w_keyval.shape[1]
    query_copy = pltpu.make_async_copy(w_query, query_w, w_local.at[3])
    out_copy = pltpu.make_async_copy(w_out, out_w, w_local.at[4])
    query_copy.start()
    out_copy.start()

    def row_of(gain):
        return jnp.concatenate([gain[i : i + 1, :] for i in range(gain.shape[0])], axis=1)

    early[0].wait()
    inputs = tokens[...].astype(jnp.float32)
    mean_sq = jnp.mean(inputs * inputs, axis=-1, keepdims=True)
    normed = (inputs * lax.rsqrt(mean_sq + epsilon) * row_of(attn_gain)).astype(jnp.bfloat16)
    early[1].wait()
    keyval_w = w_keyval[...].reshape(width, kv_heads * 128)
    key_value_rows = jnp.dot(normed, keyval_w, preferred_element_type=jnp.float32)

    line = lax.broadcasted_iota(jnp.int32, (block, 128), 0)
    lane = lax.broadcasted_iota(jnp.int32, (block, 128), 1)
    low = lane % 64 < 32
    cos_all = jnp.zeros((block, 128), jnp.float32)
    sin_all = jnp.zeros((block, 128), jnp.float32)
    early[2].wait()
    near_cos, near_sin = near_turn[0], near_turn[1]
    edge = jnp.int32(0)
    for d in range(lengths.shape[0]):
        base = at.seq * block - edge
        away = jnp.maximum(base, -base)
        tens, ones = pl.ds(away // block, 1), pl.ds(away % block, 1)
        cos_far, sin_far = far_turn[0, tens, :], far_turn[1, tens, :]
        cos_one, sin_one = near_turn[0, ones, :], near_turn[1, ones, :]
        cos_base = cos_far * cos_one - sin_far * sin_one
        sin_base = (sin_far * cos_one + cos_far * sin_one) * jnp.where(base < 0, -1.0, 1.0)
        inside = line + base >= 0
        cos_all = jnp.where(inside, cos_base * near_cos - sin_base * near_sin, cos_all)
        sin_all = jnp.where(inside, sin_base * near_cos + cos_base * near_sin, sin_all)
        edge = edge + lengths[d]
    sin_all = jnp.where(low, -sin_all, sin_all)

    def turn(values, cos_part, sin_part):
        swapped = jnp.where(low, pltpu.roll(values, 96, 1), pltpu.roll(values, 32, 1))
        return values * cos_part + swapped * sin_part

    cos_kv, sin_kv = jnp.where(lane < 64, cos_all, 1.0), jnp.where(lane < 64, sin_all, 0.0)
    for head in range(kv_heads):
        columns = slice(head * 128, (head + 1) * 128)
        turned = turn(key_value_rows[:, columns], cos_kv, sin_kv).astype(jnp.bfloat16)
        for stream in range(2):
            keyval[0, stream, :, columns] = turned[stream * lines : (stream + 1) * lines]
    all_here()

    shared = []
    weights = ((w_gate, gate_w), (w_up, up_w), (w_down, down_w))
    local_copies, twin_copies = [], []
    for i, (source, held) in enumerate(weights):
        local_copies.append(pltpu.make_async_copy(source.at[0], held.at[0], w_local.at[i]))
        twin_copies.append(
            remote(source.at[0], held.at[1], w_send.at[i], w_recv.at[i], at.twin())
        )

    token = at.seq * block + lax.broadcasted_iota(jnp.int32, (1, block), 1)
    begin = jnp.zeros((1, block), jnp.int32)
    edge = lengths[0]
    for d in range(1, lengths.shape[0]):
        begin = jnp.where(token >= edge, edge, begin)
        edge = edge + lengths[d]
    group = w_query.shape[1] // 64 // kv_heads

    def attend(number, other):
        lower, upper = share_range(number)
        if other:
            place = keyval.at[1, lower:upper]
            remote(place, place, tw_send.at[number], tw_recv.at[number], at.twin()).wait_recv()
        core = 1 - at.core if other else at.core
        count_keys = (upper - lower) * lines
        key_row = lax.broadcasted_iota(jnp.int32, (count_keys, 1), 0)
        key = jnp.zeros((count_keys, 1), jnp.int32)
        for i in range(upper - lower):
            stream, dx, dz = KEYVAL_TREE[lower + i][:3]
            start = ((at.xs(dx) * CHIPS_Z + at.zs(dz)) * 2 + core) * block + stream * lines
            key = jnp.where(key_row >= i * lines, start + key_row - i * lines, key)
        bundle = keyval[other, lower:upper].reshape(count_keys, 128 * kv_heads)
        turned = bundle.T
        bias = jnp.where((key <= token) & (key >= begin), 0.0, -1e30)
        bias = jnp.concatenate([bias] * group, axis=1)
        for head in range(kv_heads):
            scores = lax.dot_general(
                bundle[:, head * 128 : (head + 1) * 128],
                queries[head],
                (((1,), (1,)), ((), ())),
                preferred_element_type=jnp.float32,
            )
            scores = scores + bias
            old = best[head]
            new = jnp.maximum(old, jnp.max(scores, axis=0, keepdims=True))
            expd = jnp.exp2(scores - new)
            fade = jnp.exp2(old - new)
            best[head] = new
            values = turned[head * 128 + 64 : (head + 1) * 128]
            values = jnp.concatenate([values, jnp.ones((16, count_keys), jnp.bfloat16)], axis=0)
            fresh = jnp.dot(values, expd.astype(jnp.bfloat16), preferred_element_type=jnp.float32)
            weighted[head] = weighted[head] * fade + fresh

    progress = {"done": 0, "started": False}
    waiting = []

    def share_range(number):
        return (KV_SHARES[number - 1] if number else 0), KV_SHARES[number]

    def start_up():
        for copy in local_copies + twin_copies:
            copy.start()
        query_copy.wait()
        scale = 64**-0.5 * 1.4426950408889634
        query_rows = jnp.dot(normed, query_w[...], preferred_element_type=jnp.float32)
        for pair in range(query_rows.shape[1] // 128):
            turned = turn(query_rows[:, pair * 128 : (pair + 1) * 128], cos_all, sin_all) * scale
            for odd in range(2):
                head = 2 * pair + odd
                placed = pltpu.roll(turned, 64, 1) if odd else turned
                placed = jnp.where(lane < 64, placed, 0.0).astype(jnp.bfloat16)
                lower = (head % group) * block
                queries[head // group, lower : lower + block, :] = placed
        best[...] = jnp.full_like(best, -1e30)
        weighted[...] = jnp.zeros_like(weighted)

    def keys_here(count):
        if not progress["started"]:
            progress["started"] = True
            start_up()
        number = progress["done"]
        if number < len(KV_SHARES) and count >= KV_SHARES[number]:
            lower, upper = share_range(number)
            copy = remote(
                keyval.at[0, lower:upper],
                keyval.at[1, lower:upper],
                tw_send.at[number],
                tw_recv.at[number],
                at.twin(),
            )
            copy.start()
            shared.append(copy)
            if number:
                waiting.append((number - 1, 1))
            waiting.append((number, 0))
            progress["done"] = number + 1
        if waiting:
            attend(*waiting.pop(0))

    spread(
        at,
        KEYVAL_TREE,
        KEYVAL_ACTS,
        lambda r: keyval.at[0, r],
        kv_send.at[0],
        kv_recv,
        lambda r: None,
        keys_here,
    )
    for unit in waiting + [(len(KV_SHARES) - 1, 1)]:
        attend(*unit)

    columns = []
    for head in range(kv_heads):
        mean = weighted[head, :64] / weighted[head, 64:65]
        for g in range(group):
            columns.append(mean[:, g * block : (g + 1) * block])
    attended = jnp.concatenate(columns, axis=0).T.astype(jnp.bfloat16)

    out_copy.wait()
    projected[...] = jnp.dot(attended, out_w[...], preferred_element_type=jnp.float32)
    proj_send[...] = projected[...].astype(jnp.bfloat16)
    y_copies = [[], []]
    for stream in range(2):
        for step in (2, 1, 3):
            start = at.row(step)[1] * share + stream * half
            copy = remote(
                proj_send.at[pl.ds(pl.multiple_of(start, half), half)],
                proj_recv.at[stream, step - 1],
                y_send.at[stream, step - 1],
                y_recv.at[stream, step - 1],
                at.row(step),
            )
            copy.start()
            y_copies[stream].append(copy)
    expert = lax.broadcasted_iota(jnp.int32, (128, share), 0)
    table = jnp.zeros((128, share), jnp.float32)
    for k in range(routes.shape[0]):
        chosen = expert % 32 == routes[k : k + 1, :]
        table = table + jnp.where(chosen, route_gates[k : k + 1, :], 0.0)
    rounded = table.astype(jnp.bfloat16).astype(jnp.float32)
    table = jnp.where(expert < 32, rounded, table - rounded).T.astype(jnp.bfloat16)
    for stream in range(2):
        rows[stream, :, width:] = table[stream * half : (stream + 1) * half]
    for slot in range(pages.shape[0]):
        wanted = at.seq * pages.shape[0] + slot

        def look(n, found):
            return jnp.where(page_slots[n] == wanted, n, found)

        page = lax.fori_loop(0, page_slots.shape[0], look, jnp.int32(-1), unroll=8)
        taken = jnp.maximum(page, 0)
        dx = (taken // (2 * CHIPS_Z) + CHIPS_X - at.x) % CHIPS_X
        dz = ((taken // 2) % CHIPS_Z + CHIPS_Z - at.z) % CHIPS_Z
        other = (taken + at.core) % 2
        for stream in range(2):
            held = keyval[other, numbers[(stream * CHIPS_X + dx) * CHIPS_Z + dz]]
            shown = jnp.broadcast_to(page, held.shape) >= 0
            held = jnp.where(shown, held.astype(jnp.float32), 0.0).astype(jnp.bfloat16)
            pages[slot, stream * lines : (stream + 1) * lines] = held.reshape(
                lines, kv_heads, 128
            )
    def own_rows(stream):
        start = pl.multiple_of(at.tp * share + stream * half, half)
        own = projected[pl.ds(start, half), :] + tokens[pl.ds(start, half), :].astype(jnp.float32)
        for copy in y_copies[stream]:
            copy.wait_recv()
        for step in range(3):
            own = own + proj_recv[stream, step].astype(jnp.float32)
        resid[stream] = own
        mean_sq = jnp.mean(own * own, axis=-1, keepdims=True)
        ffn_in = own * lax.rsqrt(mean_sq + epsilon) * row_of(ffn_gain)
        rows[stream, :, :width] = ffn_in.astype(jnp.bfloat16)

    def experts(lower, upper):
        size = (upper - lower) * half
        gathered = rows[lower:upper].reshape(size, rows.shape[-1])
        wide = lax.broadcasted_iota(jnp.int32, (size, 128), 1)
        named = (wide % 32 == at.seq // 2) & (wide < 64)
        gate_col = jnp.where(named, gathered[:, width:].astype(jnp.float32), 0.0)
        gate_col = jnp.sum(gate_col, axis=1, keepdims=True)
        gathered = gathered[:, :width]
        total = None
        for part in range(2):
            gate_part = jnp.dot(gathered, gate_w[part], preferred_element_type=jnp.float32)
            up_part = jnp.dot(gathered, up_w[part], preferred_element_type=jnp.float32)
            hidden = gate_part / (1.0 + jnp.exp(-gate_part)) * up_part * gate_col
            term = jnp.dot(
                hidden.astype(jnp.bfloat16), down_w[part], preferred_element_type=jnp.float32
            )
            total = term if total is None else total + term
        parts[lower:upper] = total.astype(jnp.bfloat16).reshape(upper - lower, half, width)

    def add_up(r):
        total = parts[r].astype(jnp.float32)
        for child in CHILDREN[r]:
            total = total + sums[child].astype(jnp.float32)
        return total

    filled = 0
    for code in ROWS_STEPS:
        kind, r = divmod(code, 64)
        axis, step, parent = ROWS_TREE[r][3:]
        if kind == SEND:
            if filled <= parent < 2:
                own_rows(parent)
                filled = parent + 1
            remote(
                rows.at[parent], rows.at[r], ag_send.at[0], ag_recv.at[r], at.chip(axis, -step)
            ).start()
        elif kind == WAIT:
            remote(
                rows.at[r], rows.at[r], ag_send.at[0], ag_recv.at[r], at.chip(axis, step)
            ).wait_recv()
        elif kind == EXPERTS:
            if r == 0:
                for copy in local_copies:
                    copy.wait()
                for copy in twin_copies:
                    copy.wait_recv()
            experts(r * ROW_GROUP, (r + 1) * ROW_GROUP)
        elif kind == SEND_SUM:
            if CHILDREN[r]:
                parts[r] = add_up(r).astype(jnp.bfloat16)
            remote(
                parts.at[r], sums.at[r], rs_send.at[0], rs_recv.at[r], at.chip(axis, step)
            ).start()
        else:
            remote(
                sums.at[r], sums.at[r], rs_send.at[0], rs_recv.at[r], at.chip(axis, step)
            ).wait_recv()
    for stream in range(2):
        mine = slice(stream * half, (stream + 1) * half)
        out[mine, :] = (resid[stream] + add_up(stream)).astype(jnp.bfloat16)
    for copy in y_copies[0] + y_copies[1] + twin_copies + shared:
        copy.wait_send()
    for held, send_sem in (
        (keyval.at[0, 2:], kv_send),
        (rows.at[2:], ag_send),
        (parts.at[2:], rs_send),
    ):
        remote(held, held, send_sem.at[0], send_sem.at[0], at.twin()).wait_send()


def layer_call(*operands):
    tokens, near_turn, w_keyval, w_query, w_out, w_gate, w_up, w_down = operands[-8:]
    block, width = tokens.shape
    share, half, lines = block // 4, block // 8, block // 2
    piece = w_gate.shape[2]
    kv_heads = w_keyval.shape[1]
    kv_width = kv_heads * 128
    group = w_query.shape[1] // 64 // kv_heads
    smem = pl.BlockSpec(memory_space=pltpu.SMEM)
    vmem = pl.BlockSpec(memory_space=pltpu.VMEM)
    hbm = pl.BlockSpec(memory_space=pl.ANY)
    count = len(ROWS_TREE)
    dma = pltpu.SemaphoreType.DMA
    bf16, f32 = jnp.bfloat16, jnp.float32
    scratch = [
        (tokens.shape, bf16),
        (near_turn.shape, f32),
        (w_keyval.shape, bf16),
        (w_query.shape, bf16),
        (w_out.shape, bf16),
        ((2, width, piece), bf16),
        ((2, width, piece), bf16),
        ((2, piece, width), bf16),
        ((kv_heads, group * block, 128), bf16),
        ((2, count, lines, kv_width), bf16),
        ((kv_heads, 1, group * block), f32),
        ((kv_heads, 80, group * block), f32),
        ((block, width), f32),
        ((block, width), bf16),
        ((2, 3, half, width), bf16),
        ((count, half, width + 128), bf16),
        ((count, half, width), bf16),
        ((count, half, width), bf16),
        ((2, half, width), f32),
    ]
    sems = [(8,), (3,), (3,), (1,), (count,), (len(KV_SHARES),), (len(KV_SHARES),), (2, 3), (2, 3)]
    sems += [(1,), (count,), (1,), (count,)]
    return pl.pallas_call(
        layer_kernel,
        out_shape=(
            jax.ShapeDtypeStruct((share, width), bf16),
            jax.ShapeDtypeStruct((2, block, kv_heads, 128), bf16),
        ),
        in_specs=[smem] * 3 + [vmem] * 5 + [hbm] * 8,
        out_specs=(vmem, vmem),
        scratch_shapes=[pltpu.VMEM(*s) for s in scratch] + [dma(shape) for shape in sems],
        compiler_params=pltpu.CompilerParams(
            collective_id=1, has_side_effects=True, vmem_limit_bytes=56 << 20
        ),
        name="layer",
    )(*operands)


def hand_over(layer_out, pages):
    def kernel(first, second, first_out, second_out, first_held, second_held, sems):
        ins = [
            pltpu.make_async_copy(first, first_held, sems.at[0]),
            pltpu.make_async_copy(second, second_held, sems.at[1]),
        ]
        outs = [
            pltpu.make_async_copy(first_held, first_out, sems.at[2]),
            pltpu.make_async_copy(second_held, second_out, sems.at[3]),
        ]
        for copy in ins:
            copy.start()
        for came, copy in zip(ins, outs):
            came.wait()
            copy.start()
        for copy in outs:
            copy.wait()

    hbm = pl.BlockSpec(memory_space=pl.ANY)
    return pl.pallas_call(
        kernel,
        out_shape=tuple(jax.ShapeDtypeStruct(a.shape, a.dtype) for a in (layer_out, pages)),
        in_specs=[hbm] * 2,
        out_specs=(hbm, hbm),
        scratch_shapes=[pltpu.VMEM(a.shape, a.dtype) for a in (layer_out, pages)]
        + [pltpu.SemaphoreType.DMA((4,))],
        name="hand_over",
    )(layer_out, pages)


def turn_tables(steps, stride):
    inv_freq = rope_base ** (-(np.arange(128) % 32) / 32.0)
    angle = (np.arange(steps) * stride)[:, None] * inv_freq[None, :]
    return np.stack([np.cos(angle), np.sin(angle)]).astype(np.float32)


def body(
    tokens,
    attn_gain,
    w_query,
    w_keyval,
    w_out,
    ffn_gain,
    lengths,
    routes,
    route_gates,
    w_gate,
    w_up,
    w_down,
    page_slot_index,
):
    block = tokens.shape[0]
    numbers = np.zeros(len(KEYVAL_TREE), np.int32)
    for r, (stream, dx, dz) in enumerate(row[:3] for row in KEYVAL_TREE):
        numbers[(stream * CHIPS_X + dx) * CHIPS_Z + dz] = r
    layer_out, pages = layer_call(
        lengths,
        page_slot_index,
        jnp.asarray(numbers),
        attn_gain.reshape(-1, 128),
        ffn_gain.reshape(-1, 128),
        jnp.asarray(turn_tables(2 * CHIPS_X * CHIPS_Z, block)),
        routes.T,
        route_gates.T,
        tokens,
        jnp.asarray(turn_tables(block, 1)),
        w_keyval,
        w_query,
        w_out,
        w_gate,
        w_up,
        w_down,
    )
    return hand_over(layer_out, pages)


def solution(mesh):
    placed = (
        P("seq", None),
        P(),
        P(None, "tp"),
        P(None, "tp", None),
        P("tp", None),
        P(),
        P(),
        P(("seq", "tp"), None),
        P(("seq", "tp"), None),
        P("seq", None, None),
        P("seq", None, None),
        P("seq", None, None),
        P(),
    )
    return jax.shard_map(
        body,
        mesh=mesh,
        in_specs=placed,
        out_specs=(P(("seq", "tp"), None), P("seq", None, "tp", None)),
        check_vma=False,
    )
```

```python
import jax
import jax.numpy as jnp
import numpy as np
from jax import lax
from jax.experimental import pallas as pl
from jax.experimental.pallas import tpu as pltpu
from jax.sharding import PartitionSpec as P

PAGE_TOKENS = 128


epsilon = 1e-05
rope_base = 10000.0

MESH = pl.DeviceIdType.MESH
CHIPS_X = 4
CHIPS_Z = 8

KEYVAL_TREE = (
    (0, 0, 0, 0, 0, -1), (1, 0, 0, 0, 0, -1), (0, 3, 0, 0, -1, 0), (1, 1, 0, 0, 1, 1),
    (1, 0, 2, 1, 2, 1), (0, 1, 0, 0, 1, 0), (1, 3, 0, 0, -1, 1), (1, 0, 5, 1, -3, 1),
    (1, 0, 1, 1, 1, 1), (0, 0, 7, 1, -1, 0), (1, 0, 7, 1, -1, 1), (0, 2, 0, 0, -1, 2),
    (1, 2, 0, 0, 1, 3), (0, 0, 3, 1, 3, 0), (1, 1, 2, 0, 1, 4), (1, 3, 2, 0, -1, 4),
    (1, 1, 1, 0, 1, 8), (1, 3, 5, 0, -1, 7), (0, 0, 5, 1, -3, 0), (0, 3, 2, 1, 2, 2),
    (0, 3, 7, 0, -1, 9), (1, 1, 5, 0, 1, 7), (0, 0, 6, 1, -1, 9), (1, 3, 1, 1, 1, 6),
    (1, 1, 7, 0, 1, 10), (1, 3, 7, 0, -1, 10), (0, 1, 7, 1, -1, 5), (1, 0, 6, 1, 1, 7),
    (0, 1, 3, 0, 1, 13), (0, 3, 3, 0, -1, 13), (1, 1, 3, 1, 1, 14), (1, 2, 2, 0, 1, 14),
    (0, 0, 1, 1, -2, 13), (1, 2, 5, 0, -1, 17), (0, 2, 1, 1, 1, 11), (0, 1, 5, 0, 1, 18),
    (0, 3, 5, 0, -1, 18), (0, 1, 1, 1, 1, 5), (1, 1, 4, 1, -1, 21), (0, 0, 2, 0, 1, 19),
    (0, 3, 6, 0, -1, 22), (1, 2, 1, 1, 1, 12), (1, 1, 6, 0, 1, 27), (1, 3, 3, 1, -2, 17),
    (0, 2, 3, 0, -1, 29), (0, 3, 4, 1, 1, 29), (1, 2, 3, 0, 1, 30), (1, 2, 7, 0, -1, 25),
    (0, 3, 1, 1, -1, 19), (0, 2, 7, 0, 1, 26), (1, 3, 4, 1, 2, 15), (1, 3, 6, 0, -1, 27),
    (0, 1, 4, 1, -1, 35), (0, 2, 5, 0, 1, 35), (1, 0, 4, 0, -1, 38), (0, 1, 2, 1, -1, 28),
    (0, 1, 6, 1, 1, 35), (0, 2, 6, 0, -1, 40), (1, 2, 4, 1, -1, 33), (1, 2, 6, 1, 1, 33),
    (1, 0, 3, 0, 1, 43), (0, 2, 4, 0, -1, 45), (0, 2, 2, 1, 1, 34), (0, 0, 4, 0, 1, 45),
)
KEYVAL_ACTS = (
    -2, -4, -7, -3, -5, -6, -8, -13, -9, -10, -18, 2, 3, -11, -12, 4, -14, -15, -19, 5,
    6, 7, -17, 8, -16, -21, -23, 9, -22, -20, -26, -27, 10, -24, -25, 11, 12, 13, -28, -29,
    -32, 14, 15, -30, -31, -34, 16, 17, -33, 18, -35, 19, -36, -37, -39, 20, 21, -38, -41, -43,
    22, 23, -40, 24, 25, 26, 27, -42, 28, 29, -44, -45, -47, -48, -50, 30, -46, -49, 31, 32,
    -51, 33, 34, 35, -52, -53, 36, -55, -56, 37, 38, -54, 39, 40, -57, -58, -59, 41, 42, 43,
    -60, 44, -62, 45, -61, -63, 46, 47, 48, 49, 50, 51, 52, 53, 54, 55, 56, 57, 58, 59,
    60, 61, 62, 63,
)

ROWS_TREE = (
    (0, 0, 0, 0, 0, -1), (1, 0, 0, 0, 0, -1), (1, 0, 1, 1, 1, 1), (0, 1, 0, 0, 1, 0),
    (0, 3, 0, 0, -1, 0), (1, 0, 6, 1, -2, 1), (1, 1, 0, 0, 1, 1), (1, 3, 0, 0, -1, 1),
    (0, 0, 2, 1, 2, 0), (0, 0, 7, 1, -1, 0), (1, 0, 2, 1, 1, 2), (1, 1, 1, 0, 1, 2),
    (1, 3, 1, 0, -1, 2), (0, 1, 5, 1, -3, 3), (1, 1, 6, 0, 1, 5), (1, 3, 6, 0, -1, 5),
    (1, 0, 3, 1, 2, 2), (1, 2, 0, 0, -1, 7), (0, 1, 2, 0, 1, 8), (0, 3, 1, 1, 1, 4),
    (0, 0, 1, 1, -1, 8), (0, 3, 2, 0, -1, 8), (0, 1, 7, 0, 1, 9), (1, 0, 7, 1, 1, 5),
    (1, 1, 7, 1, -1, 6), (0, 3, 7, 0, -1, 9), (1, 1, 2, 0, 1, 10), (0, 1, 1, 1, 1, 3),
    (0, 0, 5, 0, -1, 13), (1, 1, 5, 1, -1, 14), (0, 2, 5, 0, 1, 13), (0, 0, 3, 1, 1, 8),
    (1, 3, 3, 0, -1, 16), (1, 3, 5, 1, -1, 15), (1, 2, 6, 0, 1, 14), (0, 3, 3, 1, 1, 21),
    (0, 2, 2, 0, -1, 21), (0, 1, 4, 1, -1, 13), (1, 1, 3, 0, 1, 16), (0, 1, 6, 1, 1, 13),
    (1, 3, 7, 0, -1, 23), (1, 2, 2, 0, 1, 26), (0, 3, 6, 1, -1, 25), (0, 0, 6, 1, 1, 28),
    (0, 2, 1, 0, -1, 19), (0, 2, 7, 0, 1, 22), (1, 1, 4, 1, -1, 29), (1, 3, 2, 0, -1, 10),
    (0, 3, 5, 0, 1, 30), (1, 3, 4, 1, -1, 33), (1, 0, 5, 1, 2, 16), (1, 2, 1, 0, -1, 12),
    (1, 2, 3, 0, 1, 38), (1, 2, 4, 1, -2, 34), (0, 2, 3, 1, 1, 36), (1, 2, 7, 0, -1, 40),
    (0, 2, 4, 0, 1, 37), (1, 2, 5, 1, -1, 34), (0, 3, 4, 1, 1, 35), (0, 2, 6, 0, -1, 42),
    (0, 1, 3, 0, 1, 31), (0, 2, 0, 1, -1, 44), (1, 0, 4, 1, 1, 16), (0, 0, 4, 0, -1, 37),
)
ROWS_STEPS = (
    3, 4, 8, 9, 2, 5, 6, 7, 66, 67, 68, 10, 11, 12, 13, 69, 16, 14, 15, 70,
    71, 128, 72, 17, 18, 73, 19, 20, 21, 22, 74, 75, 76, 23, 24, 25, 26, 77, 78, 79,
    129, 27, 28, 29, 30, 80, 81, 82, 31, 32, 33, 34, 83, 84, 85, 86, 35, 36, 37, 38,
    87, 88, 89, 90, 130, 39, 40, 41, 42, 91, 92, 93, 94, 43, 44, 45, 46, 95, 96, 97,
    98, 131, 50, 47, 48, 49, 99, 100, 101, 102, 51, 52, 53, 103, 104, 105, 106, 132, 54, 55,
    56, 107, 108, 109, 110, 57, 58, 59, 60, 111, 112, 113, 133, 61, 62, 63, 224, 114, 115, 116,
    239, 235, 238, 233, 117, 118, 119, 120, 134, 209, 231, 212, 237, 121, 122, 123, 124, 247, 242, 245,
    240, 288, 125, 126, 127, 135, 243, 244, 303, 299, 302, 297, 251, 246, 241, 248, 273, 295, 276, 301,
    255, 254, 249, 252, 311, 304, 220, 250, 253, 222, 306, 309, 307, 308, 204, 219, 221, 218, 315, 310,
    305, 312, 228, 234, 230, 319, 318, 313, 316, 223, 232, 229, 226, 284, 314, 317, 286, 227, 236, 225,
    203, 268, 283, 285, 282, 202, 199, 216, 214, 292, 298, 294, 208, 217, 210, 287, 296, 293, 290, 205,
    206, 291, 213, 215, 300, 289, 267, 207, 266, 211, 263, 280, 278, 198, 281, 201, 272, 194, 274, 277,
    200, 270, 279, 269, 195, 271, 197, 275, 262, 196, 265, 258, 259, 264, 261, 260,
)

SEND, WAIT, EXPERTS, SEND_SUM, WAIT_SUM = range(5)
CHILDREN = [[c for c in range(64) if ROWS_TREE[c][5] == r] for r in range(64)]


class Place:
    def __init__(self):
        self.seq = lax.axis_index("seq")
        self.tp = lax.axis_index("tp")
        self.x = self.seq // (2 * CHIPS_Z)
        self.z = (self.seq // 2) % CHIPS_Z
        self.core = self.seq % 2

    def xs(self, dx):
        return lax.rem(self.x + dx + CHIPS_X, CHIPS_X)

    def zs(self, dz):
        return lax.rem(self.z + dz + CHIPS_Z, CHIPS_Z)

    def chip(self, axis, step):
        if axis == 0:
            return ((self.xs(step) * CHIPS_Z + self.z) * 2 + self.core, self.tp)
        return ((self.x * CHIPS_Z + self.zs(step)) * 2 + self.core, self.tp)

    def twin(self):
        return ((self.x * CHIPS_Z + self.z) * 2 + 1 - self.core, self.tp)

    def row(self, step):
        return (self.seq, lax.rem(self.tp + step + 4, 4))


def remote(src, dst, send_sem, recv_sem, device):
    return pltpu.make_async_remote_copy(
        src_ref=src,
        dst_ref=dst,
        send_sem=send_sem,
        recv_sem=recv_sem,
        device_id=device,
        device_id_type=MESH,
    )


def greet(at):
    steps = set()
    for tree in (KEYVAL_TREE, ROWS_TREE):
        for row in tree:
            if row[5] >= 0:
                size = CHIPS_Z if row[3] else CHIPS_X
                steps |= {(row[3], row[4] % size), (row[3], -row[4] % size)}
    partners = [at.chip(*s) for s in sorted(steps)]
    partners += [at.twin()] + [at.row(d) for d in (1, 2, 3)]
    barrier = pltpu.get_barrier_semaphore()
    for partner in partners:
        pl.semaphore_signal(barrier, inc=1, device_id=partner, device_id_type=MESH)
    return lambda: pl.semaphore_wait(barrier, len(partners))


def spread(at, tree, acts, spot, send_sem, recv_sem, own_piece, arrived):
    filled, count = 0, 2
    for i, act in enumerate(first_stream_first(tree, acts)):
        if act < 0:
            axis, step, parent = tree[-act][3:]
            if filled <= parent < 2:
                own_piece(parent)
                filled = parent + 1
            remote(
                spot(parent), spot(-act), send_sem, recv_sem.at[-act], at.chip(axis, -step)
            ).start()
        else:
            remote(
                spot(act), spot(act), send_sem, recv_sem.at[act], at.chip(*tree[act][3:5])
            ).wait_recv()
            count = act + 1
        if i + 1 == len(acts) or acts[i + 1] > 0:
            arrived(count)


def first_stream_first(tree, acts):
    opening = next(i for i, act in enumerate(acts) if act > 0)
    assert {tree[-act][5] for act in acts[:opening]} == {0, 1}
    return sorted(acts[:opening], key=lambda act: tree[-act][5]) + list(acts[opening:])


KV_SHARES = (8, 16, 24, 32, 40, 48, 56, 64)
ROW_GROUP = 8


def layer_kernel(
    lengths,
    page_slots,
    numbers,
    attn_gain,
    ffn_gain,
    far_turn,
    routes,
    route_gates,
    tokens_in,
    near_turn_in,
    w_keyval_in,
    w_query,
    w_out,
    w_gate,
    w_up,
    w_down,
    out,
    pages,
    tokens,
    near_turn,
    w_keyval,
    query_w,
    out_w,
    gate_w,
    up_w,
    down_w,
    queries,
    keyval,
    best,
    weighted,
    projected,
    proj_send,
    proj_recv,
    rows,
    parts,
    sums,
    resid,
    w_local,
    w_send,
    w_recv,
    kv_send,
    kv_recv,
    tw_send,
    tw_recv,
    y_send,
    y_recv,
    ag_send,
    ag_recv,
    rs_send,
    rs_recv,
):
    at = Place()
    early = [
        pltpu.make_async_copy(source, held, w_local.at[5 + i])
        for i, (source, held) in enumerate(
            ((tokens_in, tokens), (w_keyval_in, w_keyval), (near_turn_in, near_turn))
        )
    ]
    for copy in early:
        copy.start()
    all_here = greet(at)
    width = tokens.shape[1]
    block = tokens.shape[0]
    share = block // 4
    half = share // 2
    lines = block // 2
    kv_heads = w_keyval.shape[1]
    query_copy = pltpu.make_async_copy(w_query, query_w, w_local.at[3])
    out_copy = pltpu.make_async_copy(w_out, out_w, w_local.at[4])
    query_copy.start()
    out_copy.start()

    def row_of(gain):
        return jnp.concatenate([gain[i : i + 1, :] for i in range(gain.shape[0])], axis=1)

    early[0].wait()
    inputs = tokens[...].astype(jnp.float32)
    mean_sq = jnp.mean(inputs * inputs, axis=-1, keepdims=True)
    normed = (inputs * lax.rsqrt(mean_sq + epsilon) * row_of(attn_gain)).astype(jnp.bfloat16)
    early[1].wait()
    keyval_w = w_keyval[...].reshape(width, kv_heads * 128)
    key_value_rows = jnp.dot(normed, keyval_w, preferred_element_type=jnp.float32)

    line = lax.broadcasted_iota(jnp.int32, (block, 128), 0)
    lane = lax.broadcasted_iota(jnp.int32, (block, 128), 1)
    low = lane % 64 < 32
    cos_all = jnp.zeros((block, 128), jnp.float32)
    sin_all = jnp.zeros((block, 128), jnp.float32)
    early[2].wait()
    near_cos, near_sin = near_turn[0], near_turn[1]
    edge = jnp.int32(0)
    for d in range(lengths.shape[0]):
        base = at.seq * block - edge
        away = jnp.maximum(base, -base)
        tens, ones = pl.ds(away // block, 1), pl.ds(away % block, 1)
        cos_far, sin_far = far_turn[0, tens, :], far_turn[1, tens, :]
        cos_one, sin_one = near_turn[0, ones, :], near_turn[1, ones, :]
        cos_base = cos_far * cos_one - sin_far * sin_one
        sin_base = (sin_far * cos_one + cos_far * sin_one) * jnp.where(base < 0, -1.0, 1.0)
        inside = line + base >= 0
        cos_all = jnp.where(inside, cos_base * near_cos - sin_base * near_sin, cos_all)
        sin_all = jnp.where(inside, sin_base * near_cos + cos_base * near_sin, sin_all)
        edge = edge + lengths[d]
    sin_all = jnp.where(low, -sin_all, sin_all)

    def turn(values, cos_part, sin_part):
        swapped = jnp.where(low, pltpu.roll(values, 96, 1), pltpu.roll(values, 32, 1))
        return values * cos_part + swapped * sin_part

    cos_kv, sin_kv = jnp.where(lane < 64, cos_all, 1.0), jnp.where(lane < 64, sin_all, 0.0)
    for head in range(kv_heads):
        columns = slice(head * 128, (head + 1) * 128)
        turned = turn(key_value_rows[:, columns], cos_kv, sin_kv).astype(jnp.bfloat16)
        for stream in range(2):
            keyval[0, stream, :, columns] = turned[stream * lines : (stream + 1) * lines]
    all_here()

    shared = []
    weights = ((w_gate, gate_w), (w_up, up_w), (w_down, down_w))
    local_copies, twin_copies = [], []
    for i, (source, held) in enumerate(weights):
        local_copies.append(pltpu.make_async_copy(source.at[0], held.at[0], w_local.at[i]))
        twin_copies.append(
            remote(source.at[0], held.at[1], w_send.at[i], w_recv.at[i], at.twin())
        )

    token = at.seq * block + lax.broadcasted_iota(jnp.int32, (1, block), 1)
    begin = jnp.zeros((1, block), jnp.int32)
    edge = lengths[0]
    for d in range(1, lengths.shape[0]):
        begin = jnp.where(token >= edge, edge, begin)
        edge = edge + lengths[d]
    group = w_query.shape[1] // 64 // kv_heads

    def attend(units):
        keys, bundles = [], []
        for number, other in units:
            lower, upper = share_range(number)
            if other:
                place = keyval.at[1, lower:upper]
                remote(
                    place, place, tw_send.at[number], tw_recv.at[number], at.twin()
                ).wait_recv()
            core = 1 - at.core if other else at.core
            key_row = lax.broadcasted_iota(jnp.int32, ((upper - lower) * lines, 1), 0)
            key = jnp.zeros_like(key_row)
            for i in range(upper - lower):
                stream, dx, dz = KEYVAL_TREE[lower + i][:3]
                start = ((at.xs(dx) * CHIPS_Z + at.zs(dz)) * 2 + core) * block + stream * lines
                key = jnp.where(key_row >= i * lines, start + key_row - i * lines, key)
            keys.append(key)
            bundles.append(keyval[other, lower:upper].reshape(-1, 128 * kv_heads))
        key = jnp.concatenate(keys, axis=0)
        bundle = jnp.concatenate(bundles, axis=0)
        count_keys = key.shape[0]
        turned = bundle.T
        bias = jnp.where((key <= token) & (key >= begin), 0.0, -1e30)
        bias = jnp.concatenate([bias] * group, axis=1)
        for head in range(kv_heads):
            scores = lax.dot_general(
                bundle[:, head * 128 : (head + 1) * 128],
                queries[head],
                (((1,), (1,)), ((), ())),
                preferred_element_type=jnp.float32,
            )
            scores = scores + bias
            old = best[head]
            new = jnp.maximum(old, jnp.max(scores, axis=0, keepdims=True))
            expd = jnp.exp2(scores - new)
            fade = jnp.exp2(old - new)
            best[head] = new
            values = turned[head * 128 + 64 : (head + 1) * 128]
            values = jnp.concatenate([values, jnp.ones((16, count_keys), jnp.bfloat16)], axis=0)
            fresh = jnp.dot(values, expd.astype(jnp.bfloat16), preferred_element_type=jnp.float32)
            weighted[head] = weighted[head] * fade + fresh

    progress = {"done": 0, "started": False}
    waiting = []

    def share_range(number):
        return (KV_SHARES[number - 1] if number else 0), KV_SHARES[number]

    def start_up():
        for copy in local_copies + twin_copies:
            copy.start()
        query_copy.wait()
        scale = 64**-0.5 * 1.4426950408889634
        query_rows = jnp.dot(normed, query_w[...], preferred_element_type=jnp.float32)
        for pair in range(query_rows.shape[1] // 128):
            turned = turn(query_rows[:, pair * 128 : (pair + 1) * 128], cos_all, sin_all) * scale
            for odd in range(2):
                head = 2 * pair + odd
                placed = pltpu.roll(turned, 64, 1) if odd else turned
                placed = jnp.where(lane < 64, placed, 0.0).astype(jnp.bfloat16)
                lower = (head % group) * block
                queries[head // group, lower : lower + block, :] = placed
        best[...] = jnp.full_like(best, -1e30)
        weighted[...] = jnp.zeros_like(weighted)

    def keys_here(count):
        if not progress["started"]:
            progress["started"] = True
            start_up()
        number = progress["done"]
        if number < len(KV_SHARES) and count >= KV_SHARES[number]:
            lower, upper = share_range(number)
            copy = remote(
                keyval.at[0, lower:upper],
                keyval.at[1, lower:upper],
                tw_send.at[number],
                tw_recv.at[number],
                at.twin(),
            )
            copy.start()
            shared.append(copy)
            waiting.append([(number, 0)] + ([(number - 1, 1)] if number else []))
            progress["done"] = number + 1
        if waiting:
            attend(waiting.pop(0))

    spread(
        at,
        KEYVAL_TREE,
        KEYVAL_ACTS,
        lambda r: keyval.at[0, r],
        kv_send.at[0],
        kv_recv,
        lambda r: None,
        keys_here,
    )
    for units in waiting + [[(len(KV_SHARES) - 1, 1)]]:
        attend(units)

    columns = []
    for head in range(kv_heads):
        mean = weighted[head, :64] / weighted[head, 64:65]
        for g in range(group):
            columns.append(mean[:, g * block : (g + 1) * block])
    attended = jnp.concatenate(columns, axis=0).T.astype(jnp.bfloat16)

    out_copy.wait()
    projected[...] = jnp.dot(attended, out_w[...], preferred_element_type=jnp.float32)
    proj_send[...] = projected[...].astype(jnp.bfloat16)
    y_copies = [[], []]
    for stream in range(2):
        for step in (2, 1, 3):
            start = at.row(step)[1] * share + stream * half
            copy = remote(
                proj_send.at[pl.ds(pl.multiple_of(start, half), half)],
                proj_recv.at[stream, step - 1],
                y_send.at[stream, step - 1],
                y_recv.at[stream, step - 1],
                at.row(step),
            )
            copy.start()
            y_copies[stream].append(copy)
    expert = lax.broadcasted_iota(jnp.int32, (128, share), 0)
    table = jnp.zeros((128, share), jnp.float32)
    for k in range(routes.shape[0]):
        chosen = expert % 32 == routes[k : k + 1, :]
        table = table + jnp.where(chosen, route_gates[k : k + 1, :], 0.0)
    rounded = table.astype(jnp.bfloat16).astype(jnp.float32)
    table = jnp.where(expert < 32, rounded, table - rounded).T.astype(jnp.bfloat16)
    for stream in range(2):
        rows[stream, :, width:] = table[stream * half : (stream + 1) * half]
    for slot in range(pages.shape[0]):
        wanted = at.seq * pages.shape[0] + slot

        def look(n, found):
            return jnp.where(page_slots[n] == wanted, n, found)

        page = lax.fori_loop(0, page_slots.shape[0], look, jnp.int32(-1), unroll=8)
        taken = jnp.maximum(page, 0)
        dx = (taken // (2 * CHIPS_Z) + CHIPS_X - at.x) % CHIPS_X
        dz = ((taken // 2) % CHIPS_Z + CHIPS_Z - at.z) % CHIPS_Z
        other = (taken + at.core) % 2
        for stream in range(2):
            held = keyval[other, numbers[(stream * CHIPS_X + dx) * CHIPS_Z + dz]]
            shown = jnp.broadcast_to(page, held.shape) >= 0
            held = jnp.where(shown, held.astype(jnp.float32), 0.0).astype(jnp.bfloat16)
            pages[slot, stream * lines : (stream + 1) * lines] = held.reshape(
                lines, kv_heads, 128
            )
    def own_rows(stream):
        start = pl.multiple_of(at.tp * share + stream * half, half)
        own = projected[pl.ds(start, half), :] + tokens[pl.ds(start, half), :].astype(jnp.float32)
        for copy in y_copies[stream]:
            copy.wait_recv()
        for step in range(3):
            own = own + proj_recv[stream, step].astype(jnp.float32)
        resid[stream] = own
        mean_sq = jnp.mean(own * own, axis=-1, keepdims=True)
        ffn_in = own * lax.rsqrt(mean_sq + epsilon) * row_of(ffn_gain)
        rows[stream, :, :width] = ffn_in.astype(jnp.bfloat16)

    def experts(lower, upper):
        size = (upper - lower) * half
        gathered = rows[lower:upper].reshape(size, rows.shape[-1])
        wide = lax.broadcasted_iota(jnp.int32, (size, 128), 1)
        named = (wide % 32 == at.seq // 2) & (wide < 64)
        gate_col = jnp.where(named, gathered[:, width:].astype(jnp.float32), 0.0)
        gate_col = jnp.sum(gate_col, axis=1, keepdims=True)
        gathered = gathered[:, :width]
        total = None
        for part in range(2):
            gate_part = jnp.dot(gathered, gate_w[part], preferred_element_type=jnp.float32)
            up_part = jnp.dot(gathered, up_w[part], preferred_element_type=jnp.float32)
            hidden = gate_part / (1.0 + jnp.exp(-gate_part)) * up_part * gate_col
            term = jnp.dot(
                hidden.astype(jnp.bfloat16), down_w[part], preferred_element_type=jnp.float32
            )
            total = term if total is None else total + term
        parts[lower:upper] = total.astype(jnp.bfloat16).reshape(upper - lower, half, width)

    def add_up(r):
        total = parts[r].astype(jnp.float32)
        for child in CHILDREN[r]:
            total = total + sums[child].astype(jnp.float32)
        return total

    filled = 0
    for code in ROWS_STEPS:
        kind, r = divmod(code, 64)
        axis, step, parent = ROWS_TREE[r][3:]
        if kind == SEND:
            if filled <= parent < 2:
                own_rows(parent)
                filled = parent + 1
            remote(
                rows.at[parent], rows.at[r], ag_send.at[0], ag_recv.at[r], at.chip(axis, -step)
            ).start()
        elif kind == WAIT:
            remote(
                rows.at[r], rows.at[r], ag_send.at[0], ag_recv.at[r], at.chip(axis, step)
            ).wait_recv()
        elif kind == EXPERTS:
            if r == 0:
                for copy in local_copies:
                    copy.wait()
                for copy in twin_copies:
                    copy.wait_recv()
            experts(r * ROW_GROUP, (r + 1) * ROW_GROUP)
        elif kind == SEND_SUM:
            if CHILDREN[r]:
                parts[r] = add_up(r).astype(jnp.bfloat16)
            remote(
                parts.at[r], sums.at[r], rs_send.at[0], rs_recv.at[r], at.chip(axis, step)
            ).start()
        else:
            remote(
                sums.at[r], sums.at[r], rs_send.at[0], rs_recv.at[r], at.chip(axis, step)
            ).wait_recv()
    for stream in range(2):
        mine = slice(stream * half, (stream + 1) * half)
        out[mine, :] = (resid[stream] + add_up(stream)).astype(jnp.bfloat16)
    for copy in y_copies[0] + y_copies[1] + twin_copies + shared:
        copy.wait_send()
    for held, send_sem in (
        (keyval.at[0, 2:], kv_send),
        (rows.at[2:], ag_send),
        (parts.at[2:], rs_send),
    ):
        remote(held, held, send_sem.at[0], send_sem.at[0], at.twin()).wait_send()


def layer_call(*operands):
    tokens, near_turn, w_keyval, w_query, w_out, w_gate, w_up, w_down = operands[-8:]
    block, width = tokens.shape
    share, half, lines = block // 4, block // 8, block // 2
    piece = w_gate.shape[2]
    kv_heads = w_keyval.shape[1]
    kv_width = kv_heads * 128
    group = w_query.shape[1] // 64 // kv_heads
    smem = pl.BlockSpec(memory_space=pltpu.SMEM)
    vmem = pl.BlockSpec(memory_space=pltpu.VMEM)
    hbm = pl.BlockSpec(memory_space=pl.ANY)
    count = len(ROWS_TREE)
    dma = pltpu.SemaphoreType.DMA
    bf16, f32 = jnp.bfloat16, jnp.float32
    scratch = [
        (tokens.shape, bf16),
        (near_turn.shape, f32),
        (w_keyval.shape, bf16),
        (w_query.shape, bf16),
        (w_out.shape, bf16),
        ((2, width, piece), bf16),
        ((2, width, piece), bf16),
        ((2, piece, width), bf16),
        ((kv_heads, group * block, 128), bf16),
        ((2, count, lines, kv_width), bf16),
        ((kv_heads, 1, group * block), f32),
        ((kv_heads, 80, group * block), f32),
        ((block, width), f32),
        ((block, width), bf16),
        ((2, 3, half, width), bf16),
        ((count, half, width + 128), bf16),
        ((count, half, width), bf16),
        ((count, half, width), bf16),
        ((2, half, width), f32),
    ]
    sems = [(8,), (3,), (3,), (1,), (count,), (len(KV_SHARES),), (len(KV_SHARES),), (2, 3), (2, 3)]
    sems += [(1,), (count,), (1,), (count,)]
    return pl.pallas_call(
        layer_kernel,
        out_shape=(
            jax.ShapeDtypeStruct((share, width), bf16),
            jax.ShapeDtypeStruct((2, block, kv_heads, 128), bf16),
        ),
        in_specs=[smem] * 3 + [vmem] * 5 + [hbm] * 8,
        out_specs=(vmem, vmem),
        scratch_shapes=[pltpu.VMEM(*s) for s in scratch] + [dma(shape) for shape in sems],
        compiler_params=pltpu.CompilerParams(
            collective_id=1, has_side_effects=True, vmem_limit_bytes=56 << 20
        ),
        name="layer",
    )(*operands)


def hand_over(layer_out, pages):
    def kernel(first, second, first_out, second_out, first_held, second_held, sems):
        ins = [
            pltpu.make_async_copy(first, first_held, sems.at[0]),
            pltpu.make_async_copy(second, second_held, sems.at[1]),
        ]
        outs = [
            pltpu.make_async_copy(first_held, first_out, sems.at[2]),
            pltpu.make_async_copy(second_held, second_out, sems.at[3]),
        ]
        for copy in ins:
            copy.start()
        for came, copy in zip(ins, outs):
            came.wait()
            copy.start()
        for copy in outs:
            copy.wait()

    hbm = pl.BlockSpec(memory_space=pl.ANY)
    return pl.pallas_call(
        kernel,
        out_shape=tuple(jax.ShapeDtypeStruct(a.shape, a.dtype) for a in (layer_out, pages)),
        in_specs=[hbm] * 2,
        out_specs=(hbm, hbm),
        scratch_shapes=[pltpu.VMEM(a.shape, a.dtype) for a in (layer_out, pages)]
        + [pltpu.SemaphoreType.DMA((4,))],
        name="hand_over",
    )(layer_out, pages)


def turn_tables(steps, stride):
    inv_freq = rope_base ** (-(np.arange(128) % 32) / 32.0)
    angle = (np.arange(steps) * stride)[:, None] * inv_freq[None, :]
    return np.stack([np.cos(angle), np.sin(angle)]).astype(np.float32)


def body(
    tokens,
    attn_gain,
    w_query,
    w_keyval,
    w_out,
    ffn_gain,
    lengths,
    routes,
    route_gates,
    w_gate,
    w_up,
    w_down,
    page_slot_index,
):
    block = tokens.shape[0]
    numbers = np.zeros(len(KEYVAL_TREE), np.int32)
    for r, (stream, dx, dz) in enumerate(row[:3] for row in KEYVAL_TREE):
        numbers[(stream * CHIPS_X + dx) * CHIPS_Z + dz] = r
    layer_out, pages = layer_call(
        lengths,
        page_slot_index,
        jnp.asarray(numbers),
        attn_gain.reshape(-1, 128),
        ffn_gain.reshape(-1, 128),
        jnp.asarray(turn_tables(2 * CHIPS_X * CHIPS_Z, block)),
        routes.T,
        route_gates.T,
        tokens,
        jnp.asarray(turn_tables(block, 1)),
        w_keyval,
        w_query,
        w_out,
        w_gate,
        w_up,
        w_down,
    )
    return hand_over(layer_out, pages)


def solution(mesh):
    placed = (
        P("seq", None),
        P(),
        P(None, "tp"),
        P(None, "tp", None),
        P("tp", None),
        P(),
        P(),
        P(("seq", "tp"), None),
        P(("seq", "tp"), None),
        P("seq", None, None),
        P("seq", None, None),
        P("seq", None, None),
        P(),
    )
    return jax.shard_map(
        body,
        mesh=mesh,
        in_specs=placed,
        out_specs=(P(("seq", "tp"), None), P("seq", None, "tp", None)),
        check_vma=False,
    )
```

```python
import jax
import jax.numpy as jnp
import numpy as np
from jax import lax
from jax.experimental import pallas as pl
from jax.experimental.pallas import tpu as pltpu
from jax.sharding import PartitionSpec as P

PAGE_TOKENS = 128


epsilon = 1e-05
rope_base = 10000.0

MESH = pl.DeviceIdType.MESH
CHIPS_X = 4
CHIPS_Z = 8

KEYVAL_TREE = (
    (0, 0, 0, 0, 0, -1), (1, 0, 0, 0, 0, -1), (0, 3, 0, 0, -1, 0), (1, 1, 0, 0, 1, 1),
    (1, 0, 2, 1, 2, 1), (0, 1, 0, 0, 1, 0), (1, 3, 0, 0, -1, 1), (1, 0, 5, 1, -3, 1),
    (1, 0, 1, 1, 1, 1), (0, 0, 7, 1, -1, 0), (1, 0, 7, 1, -1, 1), (0, 2, 0, 0, -1, 2),
    (1, 2, 0, 0, 1, 3), (0, 0, 3, 1, 3, 0), (1, 1, 2, 0, 1, 4), (1, 3, 2, 0, -1, 4),
    (1, 1, 1, 0, 1, 8), (1, 3, 5, 0, -1, 7), (0, 0, 5, 1, -3, 0), (0, 3, 2, 1, 2, 2),
    (0, 3, 7, 0, -1, 9), (1, 1, 5, 0, 1, 7), (0, 0, 6, 1, -1, 9), (1, 3, 1, 1, 1, 6),
    (1, 1, 7, 0, 1, 10), (1, 3, 7, 0, -1, 10), (0, 1, 7, 1, -1, 5), (1, 0, 6, 1, 1, 7),
    (0, 1, 3, 0, 1, 13), (0, 3, 3, 0, -1, 13), (1, 1, 3, 1, 1, 14), (1, 2, 2, 0, 1, 14),
    (0, 0, 1, 1, -2, 13), (1, 2, 5, 0, -1, 17), (0, 2, 1, 1, 1, 11), (0, 1, 5, 0, 1, 18),
    (0, 3, 5, 0, -1, 18), (0, 1, 1, 1, 1, 5), (1, 1, 4, 1, -1, 21), (0, 0, 2, 0, 1, 19),
    (0, 3, 6, 0, -1, 22), (1, 2, 1, 1, 1, 12), (1, 1, 6, 0, 1, 27), (1, 3, 3, 1, -2, 17),
    (0, 2, 3, 0, -1, 29), (0, 3, 4, 1, 1, 29), (1, 2, 3, 0, 1, 30), (1, 2, 7, 0, -1, 25),
    (0, 3, 1, 1, -1, 19), (0, 2, 7, 0, 1, 26), (1, 3, 4, 1, 2, 15), (1, 3, 6, 0, -1, 27),
    (0, 1, 4, 1, -1, 35), (0, 2, 5, 0, 1, 35), (1, 0, 4, 0, -1, 38), (0, 1, 2, 1, -1, 28),
    (0, 1, 6, 1, 1, 35), (0, 2, 6, 0, -1, 40), (1, 2, 4, 1, -1, 33), (1, 2, 6, 1, 1, 33),
    (1, 0, 3, 0, 1, 43), (0, 2, 4, 0, -1, 45), (0, 2, 2, 1, 1, 34), (0, 0, 4, 0, 1, 45),
)
KEYVAL_ACTS = (
    -2, -4, -7, -3, -5, -6, -8, -13, -9, -10, -18, 2, 3, -11, -12, 4, -14, -15, -19, 5,
    6, 7, -17, 8, -16, -21, -23, 9, -22, -20, -26, -27, 10, -24, -25, 11, 12, 13, -28, -29,
    -32, 14, 15, -30, -31, -34, 16, 17, -33, 18, -35, 19, -36, -37, -39, 20, 21, -38, -41, -43,
    22, 23, -40, 24, 25, 26, 27, -42, 28, 29, -44, -45, -47, -48, -50, 30, -46, -49, 31, 32,
    -51, 33, 34, 35, -52, -53, 36, -55, -56, 37, 38, -54, 39, 40, -57, -58, -59, 41, 42, 43,
    -60, 44, -62, 45, -61, -63, 46, 47, 48, 49, 50, 51, 52, 53, 54, 55, 56, 57, 58, 59,
    60, 61, 62, 63,
)

ROWS_TREE = (
    (0, 0, 0, 0, 0, -1), (1, 0, 0, 0, 0, -1), (1, 0, 1, 1, 1, 1), (0, 1, 0, 0, 1, 0),
    (0, 3, 0, 0, -1, 0), (1, 0, 6, 1, -2, 1), (1, 1, 0, 0, 1, 1), (1, 3, 0, 0, -1, 1),
    (0, 0, 2, 1, 2, 0), (0, 0, 7, 1, -1, 0), (1, 0, 2, 1, 1, 2), (1, 1, 1, 0, 1, 2),
    (1, 3, 1, 0, -1, 2), (0, 1, 5, 1, -3, 3), (1, 1, 6, 0, 1, 5), (1, 3, 6, 0, -1, 5),
    (1, 0, 3, 1, 2, 2), (1, 2, 0, 0, -1, 7), (0, 1, 2, 0, 1, 8), (0, 3, 1, 1, 1, 4),
    (0, 0, 1, 1, -1, 8), (0, 3, 2, 0, -1, 8), (0, 1, 7, 0, 1, 9), (1, 0, 7, 1, 1, 5),
    (1, 1, 7, 1, -1, 6), (0, 3, 7, 0, -1, 9), (1, 1, 2, 0, 1, 10), (0, 1, 1, 1, 1, 3),
    (0, 0, 5, 0, -1, 13), (1, 1, 5, 1, -1, 14), (0, 2, 5, 0, 1, 13), (0, 0, 3, 1, 1, 8),
    (1, 3, 3, 0, -1, 16), (1, 3, 5, 1, -1, 15), (1, 2, 6, 0, 1, 14), (0, 3, 3, 1, 1, 21),
    (0, 2, 2, 0, -1, 21), (0, 1, 4, 1, -1, 13), (1, 1, 3, 0, 1, 16), (0, 1, 6, 1, 1, 13),
    (1, 3, 7, 0, -1, 23), (1, 2, 2, 0, 1, 26), (0, 3, 6, 1, -1, 25), (0, 0, 6, 1, 1, 28),
    (0, 2, 1, 0, -1, 19), (0, 2, 7, 0, 1, 22), (1, 1, 4, 1, -1, 29), (1, 3, 2, 0, -1, 10),
    (0, 3, 5, 0, 1, 30), (1, 3, 4, 1, -1, 33), (1, 0, 5, 1, 2, 16), (1, 2, 1, 0, -1, 12),
    (1, 2, 3, 0, 1, 38), (1, 2, 4, 1, -2, 34), (0, 2, 3, 1, 1, 36), (1, 2, 7, 0, -1, 40),
    (0, 2, 4, 0, 1, 37), (1, 2, 5, 1, -1, 34), (0, 3, 4, 1, 1, 35), (0, 2, 6, 0, -1, 42),
    (0, 1, 3, 0, 1, 31), (0, 2, 0, 1, -1, 44), (1, 0, 4, 1, 1, 16), (0, 0, 4, 0, -1, 37),
)
ROWS_STEPS = (
    3, 4, 8, 9, 2, 5, 6, 7, 66, 67, 68, 10, 11, 12, 13, 69, 16, 14, 15, 70,
    71, 128, 72, 17, 18, 73, 19, 20, 21, 22, 74, 75, 76, 23, 24, 25, 26, 77, 78, 79,
    129, 27, 28, 29, 30, 80, 81, 82, 31, 32, 33, 34, 83, 84, 85, 86, 35, 36, 37, 38,
    87, 88, 89, 90, 130, 39, 40, 41, 42, 91, 92, 93, 94, 43, 44, 45, 46, 95, 96, 97,
    98, 131, 50, 47, 48, 49, 99, 100, 101, 102, 51, 52, 53, 103, 104, 105, 106, 132, 54, 55,
    56, 107, 108, 109, 110, 57, 58, 59, 60, 111, 112, 113, 133, 61, 62, 63, 224, 114, 115, 116,
    239, 235, 238, 233, 117, 118, 119, 120, 134, 209, 231, 212, 237, 121, 122, 123, 124, 247, 242, 245,
    240, 288, 125, 126, 127, 135, 243, 244, 303, 299, 302, 297, 251, 246, 241, 248, 273, 295, 276, 301,
    255, 254, 249, 252, 311, 304, 220, 250, 253, 222, 306, 309, 307, 308, 204, 219, 221, 218, 315, 310,
    305, 312, 228, 234, 230, 319, 318, 313, 316, 223, 232, 229, 226, 284, 314, 317, 286, 227, 236, 225,
    203, 268, 283, 285, 282, 202, 199, 216, 214, 292, 298, 294, 208, 217, 210, 287, 296, 293, 290, 205,
    206, 291, 213, 215, 300, 289, 267, 207, 266, 211, 263, 280, 278, 198, 281, 201, 272, 194, 274, 277,
    200, 270, 279, 269, 195, 271, 197, 275, 262, 196, 265, 258, 259, 264, 261, 260,
)

SEND, WAIT, EXPERTS, SEND_SUM, WAIT_SUM = range(5)
CHILDREN = [[c for c in range(64) if ROWS_TREE[c][5] == r] for r in range(64)]


class Place:
    def __init__(self):
        self.seq = lax.axis_index("seq")
        self.tp = lax.axis_index("tp")
        self.x = self.seq // (2 * CHIPS_Z)
        self.z = (self.seq // 2) % CHIPS_Z
        self.core = self.seq % 2

    def xs(self, dx):
        return lax.rem(self.x + dx + CHIPS_X, CHIPS_X)

    def zs(self, dz):
        return lax.rem(self.z + dz + CHIPS_Z, CHIPS_Z)

    def chip(self, axis, step):
        if axis == 0:
            return ((self.xs(step) * CHIPS_Z + self.z) * 2 + self.core, self.tp)
        return ((self.x * CHIPS_Z + self.zs(step)) * 2 + self.core, self.tp)

    def twin(self):
        return ((self.x * CHIPS_Z + self.z) * 2 + 1 - self.core, self.tp)

    def row(self, step):
        return (self.seq, lax.rem(self.tp + step + 4, 4))


def remote(src, dst, send_sem, recv_sem, device):
    return pltpu.make_async_remote_copy(
        src_ref=src,
        dst_ref=dst,
        send_sem=send_sem,
        recv_sem=recv_sem,
        device_id=device,
        device_id_type=MESH,
    )


def greet(at):
    steps = set()
    for tree in (KEYVAL_TREE, ROWS_TREE):
        for row in tree:
            if row[5] >= 0:
                size = CHIPS_Z if row[3] else CHIPS_X
                steps |= {(row[3], row[4] % size), (row[3], -row[4] % size)}
    partners = [at.chip(*s) for s in sorted(steps)]
    partners += [at.twin()] + [at.row(d) for d in (1, 2, 3)]
    barrier = pltpu.get_barrier_semaphore()
    for partner in partners:
        pl.semaphore_signal(barrier, inc=1, device_id=partner, device_id_type=MESH)
    return lambda: pl.semaphore_wait(barrier, len(partners))


def spread(at, tree, acts, spot, send_sem, recv_sem, own_piece, arrived):
    filled, count = 0, 2
    for i, act in enumerate(first_stream_first(tree, acts)):
        if act < 0:
            axis, step, parent = tree[-act][3:]
            if filled <= parent < 2:
                own_piece(parent)
                filled = parent + 1
            remote(
                spot(parent), spot(-act), send_sem, recv_sem.at[-act], at.chip(axis, -step)
            ).start()
        else:
            remote(
                spot(act), spot(act), send_sem, recv_sem.at[act], at.chip(*tree[act][3:5])
            ).wait_recv()
            count = act + 1
        if i + 1 == len(acts) or acts[i + 1] > 0:
            arrived(count)


def first_stream_first(tree, acts):
    opening = next(i for i, act in enumerate(acts) if act > 0)
    assert {tree[-act][5] for act in acts[:opening]} == {0, 1}
    return sorted(acts[:opening], key=lambda act: tree[-act][5]) + list(acts[opening:])


KV_SHARES = (8, 16, 24, 32, 40, 48, 56, 60, 64)
ROW_GROUP = 8


def layer_kernel(
    lengths,
    page_slots,
    numbers,
    attn_gain,
    ffn_gain,
    far_turn,
    routes,
    route_gates,
    tokens_in,
    near_turn_in,
    w_keyval_in,
    w_query,
    w_out,
    w_gate,
    w_up,
    w_down,
    out,
    pages,
    tokens,
    near_turn,
    w_keyval,
    query_w,
    out_w,
    gate_w,
    up_w,
    down_w,
    queries,
    keyval,
    best,
    weighted,
    projected,
    proj_send,
    proj_recv,
    rows,
    parts,
    sums,
    resid,
    w_local,
    w_send,
    w_recv,
    kv_send,
    kv_recv,
    tw_send,
    tw_recv,
    y_send,
    y_recv,
    ag_send,
    ag_recv,
    rs_send,
    rs_recv,
):
    at = Place()
    early = [
        pltpu.make_async_copy(source, held, w_local.at[5 + i])
        for i, (source, held) in enumerate(
            ((tokens_in, tokens), (w_keyval_in, w_keyval), (near_turn_in, near_turn))
        )
    ]
    for copy in early:
        copy.start()
    all_here = greet(at)
    width = tokens.shape[1]
    block = tokens.shape[0]
    share = block // 4
    half = share // 2
    lines = block // 2
    kv_heads = w_keyval.shape[1]
    query_copy = pltpu.make_async_copy(w_query, query_w, w_local.at[3])
    out_copy = pltpu.make_async_copy(w_out, out_w, w_local.at[4])
    query_copy.start()
    out_copy.start()

    def row_of(gain):
        return jnp.concatenate([gain[i : i + 1, :] for i in range(gain.shape[0])], axis=1)

    early[0].wait()
    inputs = tokens[...].astype(jnp.float32)
    mean_sq = jnp.mean(inputs * inputs, axis=-1, keepdims=True)
    normed = (inputs * lax.rsqrt(mean_sq + epsilon) * row_of(attn_gain)).astype(jnp.bfloat16)
    early[1].wait()
    keyval_w = w_keyval[...].reshape(width, kv_heads * 128)
    key_value_rows = jnp.dot(normed, keyval_w, preferred_element_type=jnp.float32)

    line = lax.broadcasted_iota(jnp.int32, (block, 128), 0)
    lane = lax.broadcasted_iota(jnp.int32, (block, 128), 1)
    low = lane % 64 < 32
    cos_all = jnp.zeros((block, 128), jnp.float32)
    sin_all = jnp.zeros((block, 128), jnp.float32)
    early[2].wait()
    near_cos, near_sin = near_turn[0], near_turn[1]
    edge = jnp.int32(0)
    for d in range(lengths.shape[0]):
        base = at.seq * block - edge
        away = jnp.maximum(base, -base)
        tens, ones = pl.ds(away // block, 1), pl.ds(away % block, 1)
        cos_far, sin_far = far_turn[0, tens, :], far_turn[1, tens, :]
        cos_one, sin_one = near_turn[0, ones, :], near_turn[1, ones, :]
        cos_base = cos_far * cos_one - sin_far * sin_one
        sin_base = (sin_far * cos_one + cos_far * sin_one) * jnp.where(base < 0, -1.0, 1.0)
        inside = line + base >= 0
        cos_all = jnp.where(inside, cos_base * near_cos - sin_base * near_sin, cos_all)
        sin_all = jnp.where(inside, sin_base * near_cos + cos_base * near_sin, sin_all)
        edge = edge + lengths[d]
    sin_all = jnp.where(low, -sin_all, sin_all)

    def turn(values, cos_part, sin_part):
        swapped = jnp.where(low, pltpu.roll(values, 96, 1), pltpu.roll(values, 32, 1))
        return values * cos_part + swapped * sin_part

    cos_kv, sin_kv = jnp.where(lane < 64, cos_all, 1.0), jnp.where(lane < 64, sin_all, 0.0)
    for head in range(kv_heads):
        columns = slice(head * 128, (head + 1) * 128)
        turned = turn(key_value_rows[:, columns], cos_kv, sin_kv).astype(jnp.bfloat16)
        for stream in range(2):
            keyval[0, stream, :, columns] = turned[stream * lines : (stream + 1) * lines]
    all_here()

    shared = []
    weights = ((w_gate, gate_w), (w_up, up_w), (w_down, down_w))
    local_copies, twin_copies = [], []
    for i, (source, held) in enumerate(weights):
        local_copies.append(pltpu.make_async_copy(source.at[0], held.at[0], w_local.at[i]))
        twin_copies.append(
            remote(source.at[0], held.at[1], w_send.at[i], w_recv.at[i], at.twin())
        )

    token = at.seq * block + lax.broadcasted_iota(jnp.int32, (1, block), 1)
    begin = jnp.zeros((1, block), jnp.int32)
    edge = lengths[0]
    for d in range(1, lengths.shape[0]):
        begin = jnp.where(token >= edge, edge, begin)
        edge = edge + lengths[d]
    group = w_query.shape[1] // 64 // kv_heads

    def attend(units):
        keys, bundles = [], []
        for number, other in units:
            lower, upper = share_range(number)
            if other:
                place = keyval.at[1, lower:upper]
                remote(
                    place, place, tw_send.at[number], tw_recv.at[number], at.twin()
                ).wait_recv()
            core = 1 - at.core if other else at.core
            key_row = lax.broadcasted_iota(jnp.int32, ((upper - lower) * lines, 1), 0)
            key = jnp.zeros_like(key_row)
            for i in range(upper - lower):
                stream, dx, dz = KEYVAL_TREE[lower + i][:3]
                start = ((at.xs(dx) * CHIPS_Z + at.zs(dz)) * 2 + core) * block + stream * lines
                key = jnp.where(key_row >= i * lines, start + key_row - i * lines, key)
            keys.append(key)
            bundles.append(keyval[other, lower:upper].reshape(-1, 128 * kv_heads))
        key = jnp.concatenate(keys, axis=0)
        bundle = jnp.concatenate(bundles, axis=0)
        count_keys = key.shape[0]
        turned = bundle.T
        bias = jnp.where((key <= token) & (key >= begin), 0.0, -1e30)
        bias = jnp.concatenate([bias] * group, axis=1)
        for head in range(kv_heads):
            scores = lax.dot_general(
                bundle[:, head * 128 : (head + 1) * 128],
                queries[head],
                (((1,), (1,)), ((), ())),
                preferred_element_type=jnp.float32,
            )
            scores = scores + bias
            old = best[head]
            new = jnp.maximum(old, jnp.max(scores, axis=0, keepdims=True))
            expd = jnp.exp2(scores - new)
            fade = jnp.exp2(old - new)
            best[head] = new
            values = turned[head * 128 + 64 : (head + 1) * 128]
            values = jnp.concatenate([values, jnp.ones((16, count_keys), jnp.bfloat16)], axis=0)
            fresh = jnp.dot(values, expd.astype(jnp.bfloat16), preferred_element_type=jnp.float32)
            weighted[head] = weighted[head] * fade + fresh

    progress = {"done": 0, "started": False}
    waiting = []

    def share_range(number):
        return (KV_SHARES[number - 1] if number else 0), KV_SHARES[number]

    def start_up():
        for copy in local_copies + twin_copies:
            copy.start()
        query_copy.wait()
        scale = 64**-0.5 * 1.4426950408889634
        query_rows = jnp.dot(normed, query_w[...], preferred_element_type=jnp.float32)
        for pair in range(query_rows.shape[1] // 128):
            turned = turn(query_rows[:, pair * 128 : (pair + 1) * 128], cos_all, sin_all) * scale
            for odd in range(2):
                head = 2 * pair + odd
                placed = pltpu.roll(turned, 64, 1) if odd else turned
                placed = jnp.where(lane < 64, placed, 0.0).astype(jnp.bfloat16)
                lower = (head % group) * block
                queries[head // group, lower : lower + block, :] = placed
        best[...] = jnp.full_like(best, -1e30)
        weighted[...] = jnp.zeros_like(weighted)

    def keys_here(count):
        if not progress["started"]:
            progress["started"] = True
            start_up()
        number = progress["done"]
        if number < len(KV_SHARES) and count >= KV_SHARES[number]:
            lower, upper = share_range(number)
            copy = remote(
                keyval.at[0, lower:upper],
                keyval.at[1, lower:upper],
                tw_send.at[number],
                tw_recv.at[number],
                at.twin(),
            )
            copy.start()
            shared.append(copy)
            waiting.append([(number, 0)] + ([(number - 1, 1)] if number else []))
            progress["done"] = number + 1
        if waiting:
            attend(waiting.pop(0))

    spread(
        at,
        KEYVAL_TREE,
        KEYVAL_ACTS,
        lambda r: keyval.at[0, r],
        kv_send.at[0],
        kv_recv,
        lambda r: None,
        keys_here,
    )
    for units in waiting + [[(len(KV_SHARES) - 1, 1)]]:
        attend(units)

    columns = []
    for head in range(kv_heads):
        mean = weighted[head, :64] / weighted[head, 64:65]
        for g in range(group):
            columns.append(mean[:, g * block : (g + 1) * block])
    attended = jnp.concatenate(columns, axis=0).T.astype(jnp.bfloat16)

    out_copy.wait()
    projected[...] = jnp.dot(attended, out_w[...], preferred_element_type=jnp.float32)
    proj_send[...] = projected[...].astype(jnp.bfloat16)
    y_copies = [[], []]
    for stream in range(2):
        for step in (2, 1, 3):
            start = at.row(step)[1] * share + stream * half
            copy = remote(
                proj_send.at[pl.ds(pl.multiple_of(start, half), half)],
                proj_recv.at[stream, step - 1],
                y_send.at[stream, step - 1],
                y_recv.at[stream, step - 1],
                at.row(step),
            )
            copy.start()
            y_copies[stream].append(copy)
    expert = lax.broadcasted_iota(jnp.int32, (128, share), 0)
    table = jnp.zeros((128, share), jnp.float32)
    for k in range(routes.shape[0]):
        chosen = expert % 32 == routes[k : k + 1, :]
        table = table + jnp.where(chosen, route_gates[k : k + 1, :], 0.0)
    rounded = table.astype(jnp.bfloat16).astype(jnp.float32)
    table = jnp.where(expert < 32, rounded, table - rounded).T.astype(jnp.bfloat16)
    for stream in range(2):
        rows[stream, :, width:] = table[stream * half : (stream + 1) * half]
    for slot in range(pages.shape[0]):
        wanted = at.seq * pages.shape[0] + slot

        def look(n, found):
            return jnp.where(page_slots[n] == wanted, n, found)

        page = lax.fori_loop(0, page_slots.shape[0], look, jnp.int32(-1), unroll=8)
        taken = jnp.maximum(page, 0)
        dx = (taken // (2 * CHIPS_Z) + CHIPS_X - at.x) % CHIPS_X
        dz = ((taken // 2) % CHIPS_Z + CHIPS_Z - at.z) % CHIPS_Z
        other = (taken + at.core) % 2
        for stream in range(2):
            held = keyval[other, numbers[(stream * CHIPS_X + dx) * CHIPS_Z + dz]]
            shown = jnp.broadcast_to(page, held.shape) >= 0
            held = jnp.where(shown, held.astype(jnp.float32), 0.0).astype(jnp.bfloat16)
            pages[slot, stream * lines : (stream + 1) * lines] = held.reshape(
                lines, kv_heads, 128
            )
    def own_rows(stream):
        start = pl.multiple_of(at.tp * share + stream * half, half)
        own = projected[pl.ds(start, half), :] + tokens[pl.ds(start, half), :].astype(jnp.float32)
        for copy in y_copies[stream]:
            copy.wait_recv()
        for step in range(3):
            own = own + proj_recv[stream, step].astype(jnp.float32)
        resid[stream] = own
        mean_sq = jnp.mean(own * own, axis=-1, keepdims=True)
        ffn_in = own * lax.rsqrt(mean_sq + epsilon) * row_of(ffn_gain)
        rows[stream, :, :width] = ffn_in.astype(jnp.bfloat16)

    def experts(lower, upper):
        size = (upper - lower) * half
        gathered = rows[lower:upper].reshape(size, rows.shape[-1])
        wide = lax.broadcasted_iota(jnp.int32, (size, 128), 1)
        named = (wide % 32 == at.seq // 2) & (wide < 64)
        gate_col = jnp.where(named, gathered[:, width:].astype(jnp.float32), 0.0)
        gate_col = jnp.sum(gate_col, axis=1, keepdims=True)
        gathered = gathered[:, :width]
        total = None
        for part in range(2):
            gate_part = jnp.dot(gathered, gate_w[part], preferred_element_type=jnp.float32)
            up_part = jnp.dot(gathered, up_w[part], preferred_element_type=jnp.float32)
            hidden = gate_part / (1.0 + jnp.exp(-gate_part)) * up_part * gate_col
            term = jnp.dot(
                hidden.astype(jnp.bfloat16), down_w[part], preferred_element_type=jnp.float32
            )
            total = term if total is None else total + term
        parts[lower:upper] = total.astype(jnp.bfloat16).reshape(upper - lower, half, width)

    def add_up(r):
        total = parts[r].astype(jnp.float32)
        for child in CHILDREN[r]:
            total = total + sums[child].astype(jnp.float32)
        return total

    filled = 0
    for code in ROWS_STEPS:
        kind, r = divmod(code, 64)
        axis, step, parent = ROWS_TREE[r][3:]
        if kind == SEND:
            if filled <= parent < 2:
                own_rows(parent)
                filled = parent + 1
            remote(
                rows.at[parent], rows.at[r], ag_send.at[0], ag_recv.at[r], at.chip(axis, -step)
            ).start()
        elif kind == WAIT:
            remote(
                rows.at[r], rows.at[r], ag_send.at[0], ag_recv.at[r], at.chip(axis, step)
            ).wait_recv()
        elif kind == EXPERTS:
            if r == 0:
                for copy in local_copies:
                    copy.wait()
                for copy in twin_copies:
                    copy.wait_recv()
            experts(r * ROW_GROUP, (r + 1) * ROW_GROUP)
        elif kind == SEND_SUM:
            if CHILDREN[r]:
                parts[r] = add_up(r).astype(jnp.bfloat16)
            remote(
                parts.at[r], sums.at[r], rs_send.at[0], rs_recv.at[r], at.chip(axis, step)
            ).start()
        else:
            remote(
                sums.at[r], sums.at[r], rs_send.at[0], rs_recv.at[r], at.chip(axis, step)
            ).wait_recv()
    for stream in range(2):
        mine = slice(stream * half, (stream + 1) * half)
        out[mine, :] = (resid[stream] + add_up(stream)).astype(jnp.bfloat16)
    for copy in y_copies[0] + y_copies[1] + twin_copies + shared:
        copy.wait_send()
    for held, send_sem in (
        (keyval.at[0, 2:], kv_send),
        (rows.at[2:], ag_send),
        (parts.at[2:], rs_send),
    ):
        remote(held, held, send_sem.at[0], send_sem.at[0], at.twin()).wait_send()


def layer_call(*operands):
    tokens, near_turn, w_keyval, w_query, w_out, w_gate, w_up, w_down = operands[-8:]
    block, width = tokens.shape
    share, half, lines = block // 4, block // 8, block // 2
    piece = w_gate.shape[2]
    kv_heads = w_keyval.shape[1]
    kv_width = kv_heads * 128
    group = w_query.shape[1] // 64 // kv_heads
    smem = pl.BlockSpec(memory_space=pltpu.SMEM)
    vmem = pl.BlockSpec(memory_space=pltpu.VMEM)
    hbm = pl.BlockSpec(memory_space=pl.ANY)
    count = len(ROWS_TREE)
    dma = pltpu.SemaphoreType.DMA
    bf16, f32 = jnp.bfloat16, jnp.float32
    scratch = [
        (tokens.shape, bf16),
        (near_turn.shape, f32),
        (w_keyval.shape, bf16),
        (w_query.shape, bf16),
        (w_out.shape, bf16),
        ((2, width, piece), bf16),
        ((2, width, piece), bf16),
        ((2, piece, width), bf16),
        ((kv_heads, group * block, 128), bf16),
        ((2, count, lines, kv_width), bf16),
        ((kv_heads, 1, group * block), f32),
        ((kv_heads, 80, group * block), f32),
        ((block, width), f32),
        ((block, width), bf16),
        ((2, 3, half, width), bf16),
        ((count, half, width + 128), bf16),
        ((count, half, width), bf16),
        ((count, half, width), bf16),
        ((2, half, width), f32),
    ]
    sems = [(8,), (3,), (3,), (1,), (count,), (len(KV_SHARES),), (len(KV_SHARES),), (2, 3), (2, 3)]
    sems += [(1,), (count,), (1,), (count,)]
    return pl.pallas_call(
        layer_kernel,
        out_shape=(
            jax.ShapeDtypeStruct((share, width), bf16),
            jax.ShapeDtypeStruct((2, block, kv_heads, 128), bf16),
        ),
        in_specs=[smem] * 3 + [vmem] * 5 + [hbm] * 8,
        out_specs=(vmem, vmem),
        scratch_shapes=[pltpu.VMEM(*s) for s in scratch] + [dma(shape) for shape in sems],
        compiler_params=pltpu.CompilerParams(
            collective_id=1, has_side_effects=True, vmem_limit_bytes=56 << 20
        ),
        name="layer",
    )(*operands)


def hand_over(layer_out, pages):
    def kernel(first, second, first_out, second_out, first_held, second_held, sems):
        ins = [
            pltpu.make_async_copy(first, first_held, sems.at[0]),
            pltpu.make_async_copy(second, second_held, sems.at[1]),
        ]
        outs = [
            pltpu.make_async_copy(first_held, first_out, sems.at[2]),
            pltpu.make_async_copy(second_held, second_out, sems.at[3]),
        ]
        for copy in ins:
            copy.start()
        for came, copy in zip(ins, outs):
            came.wait()
            copy.start()
        for copy in outs:
            copy.wait()

    hbm = pl.BlockSpec(memory_space=pl.ANY)
    return pl.pallas_call(
        kernel,
        out_shape=tuple(jax.ShapeDtypeStruct(a.shape, a.dtype) for a in (layer_out, pages)),
        in_specs=[hbm] * 2,
        out_specs=(hbm, hbm),
        scratch_shapes=[pltpu.VMEM(a.shape, a.dtype) for a in (layer_out, pages)]
        + [pltpu.SemaphoreType.DMA((4,))],
        name="hand_over",
    )(layer_out, pages)


def turn_tables(steps, stride):
    inv_freq = rope_base ** (-(np.arange(128) % 32) / 32.0)
    angle = (np.arange(steps) * stride)[:, None] * inv_freq[None, :]
    return np.stack([np.cos(angle), np.sin(angle)]).astype(np.float32)


def body(
    tokens,
    attn_gain,
    w_query,
    w_keyval,
    w_out,
    ffn_gain,
    lengths,
    routes,
    route_gates,
    w_gate,
    w_up,
    w_down,
    page_slot_index,
):
    block = tokens.shape[0]
    numbers = np.zeros(len(KEYVAL_TREE), np.int32)
    for r, (stream, dx, dz) in enumerate(row[:3] for row in KEYVAL_TREE):
        numbers[(stream * CHIPS_X + dx) * CHIPS_Z + dz] = r
    layer_out, pages = layer_call(
        lengths,
        page_slot_index,
        jnp.asarray(numbers),
        attn_gain.reshape(-1, 128),
        ffn_gain.reshape(-1, 128),
        jnp.asarray(turn_tables(2 * CHIPS_X * CHIPS_Z, block)),
        routes.T,
        route_gates.T,
        tokens,
        jnp.asarray(turn_tables(block, 1)),
        w_keyval,
        w_query,
        w_out,
        w_gate,
        w_up,
        w_down,
    )
    return hand_over(layer_out, pages)


def solution(mesh):
    placed = (
        P("seq", None),
        P(),
        P(None, "tp"),
        P(None, "tp", None),
        P("tp", None),
        P(),
        P(),
        P(("seq", "tp"), None),
        P(("seq", "tp"), None),
        P("seq", None, None),
        P("seq", None, None),
        P("seq", None, None),
        P(),
    )
    return jax.shard_map(
        body,
        mesh=mesh,
        in_specs=placed,
        out_specs=(P(("seq", "tp"), None), P("seq", None, "tp", None)),
        check_vma=False,
    )
```
